256 devices in a mesh: dp: 8 (over z), seq: 32 (over x, y, core).
Axes of the slice: x: 4, y: 4, z: 8, core: 2. Of those that a mesh axis runs over, the one named last changes fastest.
Arguments:
- query: bfloat16 [8, 8192, 1024], P('dp', 'seq'), may hold values from -150 to 150
- key: bfloat16 [8, 8192, 128], P('dp', 'seq'), may hold values from -5 to 5
- value: bfloat16 [8, 8192, 128], P('dp', 'seq'), may hold values from -6 to 6
- ssm_input: bfloat16 [8, 8192, 1024], P('dp', 'seq'), may hold values from -9 to 9
- in_b: bfloat16 [8, 8192, 128], P('dp', 'seq'), may hold values from -0.5 to 0.5
- in_c: bfloat16 [8, 8192, 128], P('dp', 'seq'), may hold values from -0.5 to 0.5
- step: float32 [8, 8192, 8], P('dp', 'seq'), may hold values from 0.3 to 24576
- rate_log: float32 [8], replicated, may hold values from -20 to 0
- skip: float32 [8], replicated, may hold values from 0.5 to 1.5
- block_mask: int32 [8, 64, 64], P('dp'), may hold values from 0 to 1, as said below
- grad_out: bfloat16 [8, 8192, 1024], P('dp', 'seq'), may hold values from -10 to 10
Outputs:
- layer_out: bfloat16 [8, 8192, 1024], P('dp', 'seq')
- query_gradient: bfloat16 [8, 8192, 1024], P('dp', 'seq')
- key_gradient: bfloat16 [8, 8192, 128], P('dp', 'seq')
- value_gradient: bfloat16 [8, 8192, 128], P('dp', 'seq')
- grad_input: bfloat16 [8, 8192, 1024], P('dp', 'seq')
- grad_in_b: bfloat16 [8, 8192, 128], P('dp', 'seq')
- grad_in_c: bfloat16 [8, 8192, 128], P('dp', 'seq')
- grad_rate_log: float32 [8], replicated
- grad_skip: float32 [8], replicated
The draws below stay inside these ranges and needn't reach their ends.
Inputs may be any that keep to these rules, and one draw needn't show every extreme that they name: block_mask[b, i, i] = 1; every row holds at most 24 ones, and the last row of every sequence's mask holds exactly 24.
All inputs are finite; a program needn't handle non-finite values.
Results may differ from the reference program's by a relative error of at most 0.02.
Values may be sent and summed in bfloat16 or wider, within the bound.
A program may use at most 192 MiB of HBM per device.

```python
import math
import jax
import jax.numpy as jnp
from jax import lax

HEAD_WIDTH = 128
QUERY_HEADS = 8
KEY_VALUE_HEADS = 1
HS = 8
P_SIZE = 128
NS = 128
BLOCK_TOKENS = 128
TOK_DEV = 256
STREAM_TOTAL_NUM = 8
STREAM_SPAN = 8192
NB = 64
MOST_KEY_BLOCKS = 24


def query_key_pair(key):
    baseline_level = jax.random.fold_in(key, 11)
    key_q, random_key_keys = jax.random.split(baseline_level, 2)
    key_rows = jnp.clip(jax.random.normal(random_key_keys, (STREAM_TOTAL_NUM, STREAM_SPAN, KEY_VALUE_HEADS * HEAD_WIDTH), jnp.float32), -5.0, 5.0)
    query_rows = jnp.clip(jax.random.normal(key_q, (STREAM_TOTAL_NUM, STREAM_SPAN, QUERY_HEADS * HEAD_WIDTH), jnp.float32), -5.0, 5.0)
    return (query_rows, key_rows)


def draw_query(key, part):
    return query_key_pair(key)[0].astype(jnp.bfloat16)


def draw_key(key, part):
    return query_key_pair(key)[1].astype(jnp.bfloat16)


def input_pair(key):
    key_x, key_g = jax.random.split(jax.random.fold_in(key, 23))
    shape = (STREAM_TOTAL_NUM, STREAM_SPAN, HS * P_SIZE)
    place = (jnp.arange(STREAM_SPAN, dtype=jnp.float32) / STREAM_SPAN)[None, :, None]
    inputs = jax.random.normal(key_x, shape, jnp.float32) * (0.7 + 0.6 * place)
    gradient_list = jax.random.normal(key_g, shape, jnp.float32) * (0.6 + 0.8 * place) + 0.25 * inputs
    return (jnp.clip(inputs, -9.0, 9.0), jnp.clip(gradient_list, -10.0, 10.0))


def draw_ssm_input(key, part):
    return input_pair(key)[0].astype(jnp.bfloat16)


def draw_grad_out(key, part):
    return input_pair(key)[1].astype(jnp.bfloat16)


def decay_pair(key):
    key_p, key_s, key_f, entropy_seed_later, key_u, key_a, key_r = jax.random.split(jax.random.fold_in(key, 37), 7)
    ranking = jax.random.permutation(key_p, HS)
    slow_count = HS // 2
    slow = ranking < slow_count
    slow_rate = jnp.exp(jax.random.uniform(key_s, (HS,), jnp.float32, math.log(0.16), math.log(0.5))) / STREAM_SPAN
    fast_rate = jax.random.uniform(key_f, (HS,), jnp.float32, 2.5, 4.0) / BLOCK_TOKENS
    speed_factor = jnp.where(slow, slow_rate, fast_rate)
    regions = STREAM_SPAN // TOK_DEV
    district_multiplier = jnp.exp(jax.random.uniform(key_r, (STREAM_TOTAL_NUM, regions, HS), jnp.float32, math.log(0.7), math.log(1.4)))
    district_multiplier = jnp.repeat(district_multiplier, TOK_DEV, axis=1)
    baseline_level = jnp.exp(jax.random.uniform(key_a, (STREAM_TOTAL_NUM, STREAM_SPAN, HS), jnp.float32, math.log(0.5), math.log(2.0)))
    surge_location = jax.random.randint(entropy_seed_later, (STREAM_TOTAL_NUM, 3), 0, STREAM_SPAN)
    surge_switched_on = jnp.any(jnp.arange(STREAM_SPAN)[None, :, None] == surge_location[:, None, :], axis=-1)
    objective_trace = jax.random.uniform(key_u, (STREAM_TOTAL_NUM, STREAM_SPAN, HS), jnp.float32, 0.2, 0.45)
    iteration_number = jnp.where(surge_switched_on[:, :, None], objective_trace / speed_factor[None, None, :], baseline_level * district_multiplier)
    return (jnp.log(speed_factor), iteration_number)


def draw_rate_log(key, part):
    return decay_pair(key)[0]


def draw_step(key, part):
    return decay_pair(key)[1]


def draw_block_mask(key, part):
    key_c, key_s = jax.random.split(jax.random.fold_in(key, 51))
    block_rows = jnp.arange(NB, dtype=jnp.int32)
    ramp_count = 1 + (MOST_KEY_BLOCKS - 1) * block_rows * block_rows // ((NB - 1) * (NB - 1))
    lowest = jnp.maximum(ramp_count // 2, 1)
    counts = jax.random.randint(key_c, (STREAM_TOTAL_NUM, NB), 0, 1 << 20) % (ramp_count - lowest + 1)[None, :] + lowest[None, :]
    counts = counts.at[:, NB - 1].set(MOST_KEY_BLOCKS)
    ranking_scores = jax.random.randint(key_s, (STREAM_TOTAL_NUM, NB, NB), 0, 1 << 16) * NB + block_rows[None, None, :]
    ranking_scores = jnp.where((block_rows[:, None] == block_rows[None, :])[None, :, :], -1, ranking_scores)
    ordering = jnp.argsort(ranking_scores, axis=-1)
    ranks = jnp.argsort(ordering, axis=-1)
    return (ranks < counts[:, :, None]).astype(jnp.int32)


def steps_of(own_key, dims, cuts, smallest, largest):
    def one(dim, parts):
        steps = jax.random.uniform(jax.random.fold_in(jax.random.fold_in(own_key, 6), dim), (parts,), jnp.float32, smallest / len(cuts), largest / len(cuts))
        return jnp.repeat(jnp.exp(steps), dims[dim] // parts).reshape((-1,) + (1,) * (len(dims) - dim - 1))

    level = one(*cuts[0])
    for cut in cuts[1:]:
        level = level * one(*cut)
    return level


def bell_draw(rng, dims, deviation, reach, shards=(), kind=jnp.bfloat16):
    array = jax.random.normal(rng, dims, jnp.float32) * deviation
    if len(shards) > 0:
        array = steps_of(rng, dims, shards, -0.22, 0.18) * array
    return jnp.clip(array, min=-reach, max=reach).astype(kind)


def setup_inputs(seed: int = 0) -> dict:
    seeds = jax.random.split(jax.random.key(seed), 12)
    return {
        "query": draw_query(jax.random.fold_in(seeds[11], 71), 0),
        "key": draw_key(jax.random.fold_in(seeds[11], 71), 0),
        "value": bell_draw(seeds[2], (STREAM_TOTAL_NUM, STREAM_SPAN, KEY_VALUE_HEADS * HEAD_WIDTH), 1.0, 6.0, ((0, 8), (1, 32))),
        "ssm_input": draw_ssm_input(jax.random.fold_in(seeds[11], 71), 0),
        "in_b": bell_draw(seeds[4], (STREAM_TOTAL_NUM, STREAM_SPAN, NS), ((NS * STREAM_SPAN) ** -0.25), 0.5, ((0, 8), (1, 32))),
        "in_c": bell_draw(seeds[5], (STREAM_TOTAL_NUM, STREAM_SPAN, NS), ((NS * STREAM_SPAN) ** -0.25), 0.5, ((0, 8), (1, 32))),
        "step": draw_step(jax.random.fold_in(seeds[11], 71), 0),
        "rate_log": draw_rate_log(jax.random.fold_in(seeds[11], 71), 0),
        "skip": jnp.clip(1.0 + 0.1 * jax.random.normal(seeds[8], (HS,), jnp.float32), 0.5, 1.5),
        "block_mask": draw_block_mask(jax.random.fold_in(seeds[11], 71), 0),
        "grad_out": draw_grad_out(jax.random.fold_in(seeds[11], 71), 0),
    }


HIGH = lax.Precision.HIGHEST

def ssm_blocks(h_start, x_seq, b_seq, c_seq, rate_log, skip, step_sizes):
    heads = rate_log.shape[0]
    length = x_seq.shape[0]
    width = x_seq.shape[1] // heads
    count_of_blocks = length // BLOCK_TOKENS
    decay_log = -step_sizes * jnp.exp(rate_log)[None, :]
    lower = jnp.arange(BLOCK_TOKENS)[:, None] >= jnp.arange(BLOCK_TOKENS)[None, :]

    def one_block(state, pieces):
        x_block, b_block, c_block, log_block = pieces
        running = jnp.cumsum(log_block, axis=0)
        spread = running.T[:, :, None] - running.T[:, None, :]
        decay = jnp.exp(jnp.where(lower[None, :, :], spread, -jnp.inf))
        inner = jnp.dot(c_block, b_block.T, precision=HIGH)
        y_inner = jnp.einsum('hij,jhp->ihp', decay * inner[None, :, :], x_block, precision=HIGH)
        carried = jnp.einsum('in,hpn->ihp', c_block, state, precision=HIGH)
        y_block = y_inner + jnp.exp(running)[:, :, None] * carried + skip[None, :, None] * x_block
        tail = jnp.exp(running[-1][None, :] - running)
        fresh = jnp.einsum('jh,jhp,jn->hpn', tail, x_block, b_block, precision=HIGH)
        new_state = jnp.exp(running[-1])[:, None, None] * state + fresh
        return (new_state, y_block)
    pieces = (x_seq.reshape(count_of_blocks, BLOCK_TOKENS, heads, width), b_seq.reshape(count_of_blocks, BLOCK_TOKENS, -1), c_seq.reshape(count_of_blocks, BLOCK_TOKENS, -1), decay_log.reshape(count_of_blocks, BLOCK_TOKENS, heads))
    h_end, y_all = lax.scan(one_block, h_start, pieces)
    return (y_all.reshape(length, heads * width), h_end)

def attend_block(query_block, block_gradient, mask_row, key_rows, value_rows):
    count_of_blocks = mask_row.shape[0]
    head_groups = QUERY_HEADS // KEY_VALUE_HEADS
    factor = HEAD_WIDTH ** (-0.5)
    ranking = jnp.argsort((1 - mask_row) * count_of_blocks + jnp.arange(count_of_blocks, dtype=jnp.int32))
    picked_blocks = ranking[:MOST_KEY_BLOCKS].astype(jnp.int32)
    live = jnp.arange(MOST_KEY_BLOCKS, dtype=jnp.int32) < jnp.sum(mask_row)
    selected_keys = key_rows.reshape(count_of_blocks, BLOCK_TOKENS, KEY_VALUE_HEADS, HEAD_WIDTH)[picked_blocks].reshape(MOST_KEY_BLOCKS * BLOCK_TOKENS, KEY_VALUE_HEADS, HEAD_WIDTH).astype(jnp.float32)
    selected_values = value_rows.reshape(count_of_blocks, BLOCK_TOKENS, KEY_VALUE_HEADS, HEAD_WIDTH)[picked_blocks].reshape(MOST_KEY_BLOCKS * BLOCK_TOKENS, KEY_VALUE_HEADS, HEAD_WIDTH).astype(jnp.float32)
    query_rows = query_block.reshape(BLOCK_TOKENS, KEY_VALUE_HEADS, head_groups, HEAD_WIDTH).astype(jnp.float32)
    gradient_list = block_gradient.reshape(BLOCK_TOKENS, KEY_VALUE_HEADS, head_groups, HEAD_WIDTH).astype(jnp.float32)
    scores = jnp.einsum('qhgd,khd->hgqk', query_rows, selected_keys) * factor
    scores = jnp.where(jnp.repeat(live, BLOCK_TOKENS)[None, None, None, :], scores, -jnp.inf)
    best = lax.optimization_barrier(jnp.max(scores, axis=-1, keepdims=True))
    weights = jnp.exp(scores - best)
    total = lax.optimization_barrier(jnp.sum(weights, axis=-1, keepdims=True))
    rounded = lax.optimization_barrier(weights.astype(jnp.bfloat16)).astype(jnp.float32)
    output = jnp.einsum('hgqk,khd->hgqd', rounded, selected_values) / total
    delta = lax.optimization_barrier(jnp.sum(jnp.transpose(gradient_list, (1, 2, 0, 3)) * output, axis=-1, keepdims=True))
    probs = weights / total
    probs_low = lax.optimization_barrier(probs.astype(jnp.bfloat16)).astype(jnp.float32)
    dprobs = jnp.einsum('qhgd,khd->hgqk', gradient_list, selected_values)
    dscores = lax.optimization_barrier((probs * (dprobs - delta)).astype(jnp.bfloat16)).astype(jnp.float32)
    query_gradient_part = jnp.einsum('hgqk,khd->qhgd', dscores, selected_keys) * factor
    key_gradient_part = jnp.einsum('hgqk,qhgd->khd', dscores, query_rows) * factor
    value_gradient_part = jnp.einsum('hgqk,qhgd->khd', probs_low, gradient_list)
    output_row_block = jnp.transpose(output, (2, 0, 1, 3)).reshape(BLOCK_TOKENS, QUERY_HEADS * HEAD_WIDTH)
    return (output_row_block, query_gradient_part.reshape(BLOCK_TOKENS, QUERY_HEADS * HEAD_WIDTH), picked_blocks, key_gradient_part.reshape(MOST_KEY_BLOCKS, BLOCK_TOKENS, KEY_VALUE_HEADS * HEAD_WIDTH), value_gradient_part.reshape(MOST_KEY_BLOCKS, BLOCK_TOKENS, KEY_VALUE_HEADS * HEAD_WIDTH))

def one_sequence(items, rate_log, skip):
    query, key, value, ssm_input, in_b, in_c, step, block_mask, grad_out = items
    count_of_blocks = STREAM_SPAN // BLOCK_TOKENS

    def per_block(holding_array, pieces):
        query_block, block_gradient, mask_row = pieces
        output_row_block, grad_rows, picked_blocks, key_gradient_part, value_gradient_part = attend_block(query_block, block_gradient, mask_row, key, value)
        holding_array = holding_array.at[picked_blocks].add(jnp.concatenate([key_gradient_part, value_gradient_part], axis=-1))
        return (holding_array, (output_row_block, grad_rows))
    blank_rows = jnp.zeros((count_of_blocks, BLOCK_TOKENS, 2 * KEY_VALUE_HEADS * HEAD_WIDTH), jnp.float32)
    holding_array, (attention, query_gradient) = lax.scan(per_block, blank_rows, (query.reshape(count_of_blocks, BLOCK_TOKENS, QUERY_HEADS * HEAD_WIDTH), grad_out.reshape(count_of_blocks, BLOCK_TOKENS, QUERY_HEADS * HEAD_WIDTH), block_mask))
    attention = attention.reshape(STREAM_SPAN, QUERY_HEADS * HEAD_WIDTH)
    holding_array = holding_array.reshape(STREAM_SPAN, 2 * KEY_VALUE_HEADS * HEAD_WIDTH)

    def branch(x_float, b_float, c_float, rate_value, gain):
        outcome, final_state = ssm_blocks(jnp.zeros((HS, P_SIZE, NS), jnp.float32), x_float, b_float, c_float, rate_value, gain, step)
        return outcome
    ssm_out, pullback = jax.vjp(branch, ssm_input.astype(jnp.float32), in_b.astype(jnp.float32), in_c.astype(jnp.float32), rate_log, skip)
    input_gradient, gradient_input_weights, gradient_output_weights, rate_gradient, gain_gradient = pullback(grad_out.astype(jnp.float32))
    layer_function = (attention + ssm_out).astype(jnp.bfloat16)
    return (layer_function, query_gradient.reshape(STREAM_SPAN, QUERY_HEADS * HEAD_WIDTH).astype(jnp.bfloat16), holding_array[:, :KEY_VALUE_HEADS * HEAD_WIDTH].astype(jnp.bfloat16), holding_array[:, KEY_VALUE_HEADS * HEAD_WIDTH:].astype(jnp.bfloat16), input_gradient.astype(jnp.bfloat16), gradient_input_weights.astype(jnp.bfloat16), gradient_output_weights.astype(jnp.bfloat16), rate_gradient, gain_gradient)

def reference(query, key, value, ssm_input, in_b, in_c, step, rate_log, skip, block_mask, grad_out):
    results = lax.map(lambda items: one_sequence(items, rate_log, skip), (query, key, value, ssm_input, in_b, in_c, step, block_mask, grad_out))
    tokens_all = STREAM_TOTAL_NUM * STREAM_SPAN
    grad_rate_log = lax.optimization_barrier(jnp.sum(results[7], axis=0)) / tokens_all
    grad_skip = lax.optimization_barrier(jnp.sum(results[8], axis=0)) / (tokens_all * P_SIZE)
    return (results[0], results[1], results[2], results[3], results[4], results[5], results[6], grad_rate_log, grad_skip)
```

```python
import functools

import jax
import jax.numpy as jnp
from jax import lax
from jax.experimental import pallas as pl
from jax.experimental.pallas import tpu as pltpu
from jax.sharding import PartitionSpec as P

HW = 128
HEADS = 8
BT = 128
MOST = 24
MOST_PAIRS = MOST // 2
FACTOR = HW ** (-0.5)
LOG2E = 1.4426950408889634
BF = jnp.bfloat16
F32 = jnp.float32
MESH = pl.DeviceIdType.MESH
HIGH = lax.Precision.HIGHEST

VM = pl.BlockSpec(memory_space=pltpu.VMEM)
SM = pl.BlockSpec(memory_space=pltpu.SMEM)


def nn(a, b):
    return lax.dot_general(a, b, (((1,), (0,)), ((), ())), preferred_element_type=F32)


def nt(a, b):
    return lax.dot_general(a, b, (((1,), (1,)), ((), ())), preferred_element_type=F32)


def tn(a, b):
    return lax.dot_general(a, b, (((0,), (0,)), ((), ())), preferred_element_type=F32)


def cols(h):
    return pl.ds(h * HW, HW)


def attention_kernel(
    mask_ref, q_ref, g_ref, k_ref, v_ref,
    o_ref, dq_ref, tk_ref, tv_ref,
    s_buf, acc_k, acc_v, qs, gs, g_t, o_t, dq_t, picked,
):
    total_blocks = mask_ref.shape[1]
    seq_at = lax.axis_index("seq")
    per_device = q_ref.shape[0] // BT
    acc_k[...] = jnp.zeros_like(acc_k)
    acc_v[...] = jnp.zeros_like(acc_v)

    @pl.loop(0, per_device)
    def _(block):
        row = seq_at * per_device + block

        def note(j, n):
            picked[n] = j
            return n + mask_ref[row, j]

        count = lax.fori_loop(0, total_blocks, note, jnp.int32(0))
        picked[count] = picked[0]
        pairs = (count + 1) // 2
        rows = pl.ds(pl.multiple_of(block * BT, BT), BT)
        for h in range(HEADS):
            qs[cols(h), :] = q_ref[rows, cols(h)]
            g_head = g_ref[rows, cols(h)]
            gs[cols(h), :] = g_head
            g_t[:, cols(h)] = g_head.astype(F32).T

        def starts(p):
            return tuple(pl.multiple_of(picked[2 * p + i] * BT, BT) for i in range(2))

        def pair_of(ref, p):
            first, second = starts(p)
            return jnp.concatenate([ref[pl.ds(first, BT), :], ref[pl.ds(second, BT), :]], axis=0)

        def score_step(p, top):
            s = nt(pair_of(k_ref, p), qs[...])
            bias = jnp.where(2 * p + 1 < count, 0.0, -1e30).astype(F32)
            s = jnp.concatenate([s[:BT], s[BT:] + bias], axis=0)
            s_buf[p] = s
            return jnp.maximum(top, jnp.max(s.reshape(-1, 8, s.shape[1]), axis=0))

        top = lax.fori_loop(
            0, pairs, score_step, jnp.full((8, HEADS * BT), -3e38, F32)
        )
        top = jnp.max(top, axis=0, keepdims=True)
        o_t[...] = jnp.zeros_like(o_t)

        def weight_step(p, total):
            w = jnp.exp2((s_buf[p] - top) * (FACTOR * LOG2E))
            s_buf[p] = w
            o_t[...] += nn(pair_of(v_ref, p).T, w.astype(BF))
            return total + jnp.sum(w.reshape(-1, 8, w.shape[1]), axis=0)

        total = lax.fori_loop(0, pairs, weight_step, jnp.zeros((8, HEADS * BT), F32))
        inverse = 1.0 / jnp.sum(total, axis=0, keepdims=True)
        o_t[...] = o_t[...] * inverse
        delta = jnp.sum(o_t[...] * g_t[...], axis=0, keepdims=True)
        for h in range(HEADS):
            o_ref[rows, cols(h)] = o_t[:, cols(h)].T
        dq_t[...] = jnp.zeros_like(dq_t)

        def gradient_step(p, carry):
            probs = s_buf[p] * inverse
            dprobs = nt(pair_of(v_ref, p), gs[...])
            ds = (probs * (dprobs - delta)).astype(BF)
            dq_t[...] += nn(pair_of(k_ref, p).T, ds)
            dk = nn(ds, qs[...])
            dv = nn(probs.astype(BF), gs[...])
            for i, first in enumerate(starts(p)):
                here = pl.ds(first, BT)
                acc_k[here, :] += dk[i * BT : (i + 1) * BT]
                acc_v[here, :] += dv[i * BT : (i + 1) * BT]
            return carry

        lax.fori_loop(0, pairs, gradient_step, 0)
        for h in range(HEADS):
            dq_ref[rows, cols(h)] = (dq_t[:, cols(h)] * FACTOR).T.astype(BF)

    @pl.loop(0, total_blocks)
    def _(j):
        here = pl.ds(pl.multiple_of(j * BT, BT), BT)
        chip = j // 4
        at = (
            lax.rem(j // 2, 2), chip // SIDE, lax.rem(chip, SIDE),
            pl.ds(pl.multiple_of(lax.rem(j, 2) * BT, BT), BT),
        )
        tk_ref[at] = (acc_k[here, :] * FACTOR).astype(BF)
        tv_ref[at] = acc_v[here, :].astype(BF)


def attention(mask, q, g, keys, values):
    local, wide = q.shape
    total = keys.shape[0]
    width = HEADS * BT
    return pl.pallas_call(
        attention_kernel,
        out_shape=(
            jax.ShapeDtypeStruct((local, wide), F32),
            jax.ShapeDtypeStruct((local, wide), BF),
            jax.ShapeDtypeStruct((2, SIDE, SIDE, local, HW), BF),
            jax.ShapeDtypeStruct((2, SIDE, SIDE, local, HW), BF),
        ),
        in_specs=[SM, VM, VM, VM, VM],
        out_specs=(VM, VM, VM, VM),
        scratch_shapes=[
            pltpu.VMEM((MOST_PAIRS, 2 * BT, width), F32),
            pltpu.VMEM((total, HW), F32),
            pltpu.VMEM((total, HW), F32),
            pltpu.VMEM((width, HW), BF),
            pltpu.VMEM((width, HW), BF),
            pltpu.VMEM((HW, width), F32),
            pltpu.VMEM((HW, width), F32),
            pltpu.VMEM((HW, width), F32),
            pltpu.SMEM((total // BT + 8,), jnp.int32),
        ],
        compiler_params=pltpu.CompilerParams(vmem_limit_bytes=56 << 20),
        cost_estimate=pl.CostEstimate(
            flops=12 * 24 * 1024 * 128 * 128 * 2, bytes_accessed=12 << 20, transcendentals=1 << 22
        ),
        name="attention",
    )(mask, q, g, keys, values)


def ssm_local_kernel(
    x_ref, g_ref, b_ref, c_ref, step_ref, rate_ref, skip_ref,
    y_ref, dx_ref, xt_ref, eg_ref, send_ref, decay_ref, db_ref, dc_ref, cum_ref, rate_out, skip_out,
    dl, sum00, sum11, sum10,
):
    lanes = lax.broadcasted_iota(jnp.int32, (BT, BT), 1)
    subs = lax.broadcasted_iota(jnp.int32, (BT, BT), 0)
    lower = subs >= lanes
    tri = lower.astype(F32)
    dl[...] = jnp.zeros_like(dl)
    for h in range(HEADS):
        rate = jnp.exp(jnp.full((1, 1), rate_ref[h], F32))
        dl[:, h : h + 1] = -step_ref[:, h : h + 1] * rate
    run = []
    for i in range(2):
        run.append(
            lax.dot_general(
                tri, dl[i * BT : (i + 1) * BT, :], (((1,), (0,)), ((), ())),
                precision=HIGH, preferred_element_type=F32,
            )
        )
    run0, run1 = run
    end0, end1 = run0[BT - 1 : BT, :], run1[BT - 1 : BT, :]
    whole = end0 + end1
    run0_t, run1_t = run0.T, run1.T
    from_start = jnp.concatenate([run0, run1 + end0], axis=0)
    to_end = jnp.concatenate([end0 - run0 + end1, end1 - run1], axis=0)
    cum_ref[0] = from_start
    cum_ref[1] = to_end
    decay_ref[...] = jnp.broadcast_to(whole, decay_ref.shape)

    b0, b1 = b_ref[0:BT, :], b_ref[BT : 2 * BT, :]
    c0, c1 = c_ref[0:BT, :], c_ref[BT : 2 * BT, :]
    cb00, cb11, cb10 = nt(c0, b0), nt(c1, b1), nt(c1, b0)
    sum00[...] = jnp.zeros_like(sum00)
    sum11[...] = jnp.zeros_like(sum11)
    sum10[...] = jnp.zeros_like(sum10)
    b_t, c_t = b_ref[...].T, c_ref[...].T
    for h in range(HEADS):
        x0, x1 = x_ref[0:BT, cols(h)], x_ref[BT : 2 * BT, cols(h)]
        g0, g1 = g_ref[0:BT, cols(h)], g_ref[BT : 2 * BT, cols(h)]
        gain = skip_ref[h]
        col0, col1 = run0[:, h : h + 1], run1[:, h : h + 1]
        row0, row1 = run0_t[h : h + 1, :], run1_t[h : h + 1, :]
        last0 = end0[:, h : h + 1]

        def part(spread, cb, xs, gs, total, diagonal):
            if diagonal:
                decay = jnp.where(lower, jnp.exp(jnp.where(lower, spread, 0.0)), 0.0)
            else:
                decay = jnp.exp(spread)
            mixed = decay * cb
            outer = nt(gs, xs)
            total[...] += decay * outer
            terms = spread * (mixed * outer)
            mixed = mixed.astype(BF)
            return nn(mixed, xs), tn(mixed, gs), jnp.sum(terms, axis=0, keepdims=True)

        y00, dx00, r00 = part(col0 - row0, cb00, x0, g0, sum00, True)
        y11, dx11, r11 = part(col1 - row1, cb11, x1, g1, sum11, True)
        y10, dx10, r10 = part(col1 + (last0 - row0), cb10, x0, g1, sum10, False)
        rate_out[h : h + 1, :] = r00 + r11 + r10
        xf0, xf1, gf0, gf1 = x0.astype(F32), x1.astype(F32), g0.astype(F32), g1.astype(F32)
        skip_out[h : h + 1, :] = jnp.sum(xf0 * gf0 + xf1 * gf1, axis=0, keepdims=True)
        y_ref[0:BT, cols(h)] = y00 + gain * xf0
        y_ref[BT : 2 * BT, cols(h)] = y11 + y10 + gain * xf1
        dx_ref[0:BT, cols(h)] = dx00 + dx10 + gain * gf0
        dx_ref[BT : 2 * BT, cols(h)] = dx11 + gain * gf1
        start = jnp.exp(from_start[:, h : h + 1])
        tail = jnp.exp(to_end[:, h : h + 1])
        xt = (tail * jnp.concatenate([xf0, xf1], axis=0)).astype(BF)
        eg = (start * jnp.concatenate([gf0, gf1], axis=0)).astype(BF)
        xt_ref[:, cols(h)] = xt
        eg_ref[:, cols(h)] = eg
        end_state = nn(b_t, xt).astype(BF)
        start_grad = nn(c_t, eg).astype(BF)
        for quarter in range(4):
            at = slice(quarter * 32, quarter * 32 + 32)
            send_ref[h * 4 + quarter, 0] = end_state[at]
            send_ref[h * 4 + quarter, 1] = start_grad[at]
    s00, s11, s10 = sum00[...].astype(BF), sum11[...].astype(BF), sum10[...].astype(BF)
    dc_ref[0:BT, :] = nn(s00, b0)
    dc_ref[BT : 2 * BT, :] = nn(s11, b1) + nn(s10, b0)
    db_ref[0:BT, :] = tn(s00, c0) + tn(s10, c1)
    db_ref[BT : 2 * BT, :] = tn(s11, c1)


def ssm_local(x, g, b, c, step, rate_log, skip):
    local, wide = x.shape
    sds = jax.ShapeDtypeStruct
    return pl.pallas_call(
        ssm_local_kernel,
        out_shape=(
            sds((local, wide), F32),
            sds((local, wide), F32),
            sds((local, wide), BF),
            sds((local, wide), BF),
            sds((32, 2, 32, HW), BF),
            sds((8, HW), F32),
            sds((local, HW), F32),
            sds((local, HW), F32),
            sds((2, local, HW), F32),
            sds((HEADS, HW), F32),
            sds((HEADS, HW), F32),
        ),
        in_specs=[VM, VM, VM, VM, VM, SM, SM],
        out_specs=(VM,) * 11,
        scratch_shapes=[
            pltpu.VMEM((local, HW), F32),
            pltpu.VMEM((BT, BT), F32),
            pltpu.VMEM((BT, BT), F32),
            pltpu.VMEM((BT, BT), F32),
        ],
        compiler_params=pltpu.CompilerParams(vmem_limit_bytes=32 << 20),
        cost_estimate=pl.CostEstimate(flops=1 << 30, bytes_accessed=6 << 20, transcendentals=1 << 19),
        name="ssm_local",
    )(x, g, b, c, step, rate_log, skip)


def exchange_kernel(
    send_ref, decay_ref, out_ref,
    got, decays, back, s1, r1, s2, r2, s3, r3,
):
    n = 32
    me = lax.axis_index("seq")
    barrier = pltpu.get_barrier_semaphore()

    @pl.loop(1, n)
    def _(r):
        to = lax.rem(me + r, n)
        pl.semaphore_signal(barrier, inc=1, device_id={"seq": to}, device_id_type=MESH)

    pl.semaphore_wait(barrier, n - 1)

    def state_copy(r):
        to = lax.rem(me + r, n)
        return pltpu.make_async_remote_copy(
            src_ref=send_ref.at[to], dst_ref=got.at[me],
            send_sem=s1.at[r], recv_sem=r1.at[r],
            device_id={"seq": to}, device_id_type=MESH,
        )

    def decay_copy(r):
        to = lax.rem(me + r, n)
        return pltpu.make_async_remote_copy(
            src_ref=decay_ref, dst_ref=decays.at[me],
            send_sem=s2.at[r], recv_sem=r2.at[r],
            device_id={"seq": to}, device_id_type=MESH,
        )

    def back_copy(r):
        to = lax.rem(me + r, n)
        return pltpu.make_async_remote_copy(
            src_ref=back.at[to], dst_ref=out_ref.at[me],
            send_sem=s3.at[r], recv_sem=r3.at[r],
            device_id={"seq": to}, device_id_type=MESH,
        )

    @pl.loop(1, n)
    def _(r):
        decay_copy(r).start()
        state_copy(r).start()

    got[me] = send_ref[me]
    decays[me] = decay_ref[...]

    @pl.loop(1, n)
    def _(r):
        decay_copy(r).wait()
        state_copy(r).wait()

    head = me // 4
    lanes = lax.broadcasted_iota(jnp.int32, (8, HW), 1)

    def decay_of(d):
        only = jnp.where(lanes == head, decays[d], 0.0)
        return jnp.exp(jnp.sum(only, axis=1, keepdims=True))[0:1, :]

    def forward(d, state):
        back[d, 0] = state.astype(BF)
        return decay_of(d) * state + got[d, 0].astype(F32)

    def backward(k, state):
        d = n - 1 - k
        back[d, 1] = state.astype(BF)
        return decay_of(d) * state + got[d, 1].astype(F32)

    zero = jnp.zeros((32, HW), F32)
    lax.fori_loop(0, n, forward, zero)
    lax.fori_loop(0, n, backward, zero)

    @pl.loop(1, n)
    def _(r):
        back_copy(r).start()

    out_ref[me] = back[me]

    @pl.loop(1, n)
    def _(r):
        back_copy(r).wait()


def exchange(send, decay):
    n = 32
    dma = pltpu.SemaphoreType.DMA((n,))
    return pl.pallas_call(
        exchange_kernel,
        out_shape=jax.ShapeDtypeStruct((n, 2, 32, HW), BF),
        in_specs=[VM, VM],
        out_specs=VM,
        scratch_shapes=[
            pltpu.VMEM((n, 2, 32, HW), BF),
            pltpu.VMEM((n, 8, HW), F32),
            pltpu.VMEM((n, 2, 32, HW), BF),
            dma, dma, dma, dma, dma, dma,
        ],
        compiler_params=pltpu.CompilerParams(
            collective_id=1, has_side_effects=True, vmem_limit_bytes=16 << 20
        ),
        cost_estimate=pl.CostEstimate(flops=1 << 20, bytes_accessed=8 << 20, transcendentals=0),
        name="exchange",
    )(send, decay)


def ssm_finish_kernel(
    st_ref, y_ref, dx_ref, xt_ref, eg_ref, send_ref, decay_ref, db_ref, dc_ref, cum_ref,
    rate_in, b_ref, c_ref, x_ref, g_ref,
    yo_ref, dxo_ref, dbo_ref, dco_ref, rate_out,
):
    del send_ref
    dc = dc_ref[...]
    db = db_ref[...]
    for h in range(HEADS):
        s_in = jnp.concatenate([st_ref[h * 4 + i, 0] for i in range(4)], axis=0)
        g_out = jnp.concatenate([st_ref[h * 4 + i, 1] for i in range(4)], axis=0)
        log_start, log_tail = cum_ref[0][:, h : h + 1], cum_ref[1][:, h : h + 1]
        y_in = jnp.exp(log_start) * nn(c_ref[...], s_in)
        dx_in = jnp.exp(log_tail) * nn(b_ref[...], g_out)
        yo_ref[:, cols(h)] = y_ref[:, cols(h)] + y_in
        dxo_ref[:, cols(h)] = (dx_ref[:, cols(h)] + dx_in).astype(BF)
        dc = dc + nt(eg_ref[:, cols(h)], s_in)
        db = db + nt(xt_ref[:, cols(h)], g_out)
        gf, xf = g_ref[:, cols(h)].astype(F32), x_ref[:, cols(h)].astype(F32)
        terms = jnp.sum(log_start * (gf * y_in) + log_tail * (xf * dx_in), axis=0, keepdims=True)
        whole = decay_ref[0:1, h : h + 1]
        both = jnp.sum(s_in.astype(F32) * g_out.astype(F32), axis=0, keepdims=True)
        rate_out[h : h + 1, :] = rate_in[h : h + 1, :] + terms + whole * jnp.exp(whole) * both
    dco_ref[...] = dc.astype(BF)
    dbo_ref[...] = db.astype(BF)


def ssm_finish(states, y, dx, xt, eg, send, decay, db, dc, cum, rate, b, c, x, g):
    local, wide = x.shape
    sds = jax.ShapeDtypeStruct
    return pl.pallas_call(
        ssm_finish_kernel,
        out_shape=(
            sds((local, wide), F32),
            sds((local, wide), BF),
            sds((local, HW), BF),
            sds((local, HW), BF),
            sds((HEADS, HW), F32),
        ),
        in_specs=[VM] * 15,
        out_specs=(VM,) * 5,
        compiler_params=pltpu.CompilerParams(vmem_limit_bytes=32 << 20),
        cost_estimate=pl.CostEstimate(flops=1 << 28, bytes_accessed=6 << 20, transcendentals=1 << 10),
        name="ssm_finish",
    )(states, y, dx, xt, eg, send, decay, db, dc, cum, rate, b, c, x, g)


SIDE = 4
CHIPS = SIDE * SIDE


def place():
    me = lax.axis_index("seq")
    core = lax.rem(me, 2)
    chip = me // 2
    return me, chip // SIDE, lax.rem(chip, SIDE), core


def ring(a, step):
    return lax.rem(a + step + SIDE, SIDE)


def greet(me, x, y, core):
    barrier = pltpu.get_barrier_semaphore()
    friends = [
        (ring(x, 1), y, core), (ring(x, -1), y, core),
        (x, ring(y, 1), core), (x, ring(y, -1), core), (x, y, 1 - core),
    ]
    for a, b, c in friends:
        pl.semaphore_signal(
            barrier, inc=1, device_id={"seq": (a * SIDE + b) * 2 + c}, device_id_type=MESH
        )
    pl.semaphore_wait(barrier, len(friends))


class Copies:
    def __init__(self, send_sem, recv_sem):
        self.send_sem, self.recv_sem, self.made = send_sem, recv_sem, []

    def start(self, src, dst, device):
        at = len(self.made)
        copy = pltpu.make_async_remote_copy(
            src_ref=src, dst_ref=dst, send_sem=self.send_sem.at[at], recv_sem=self.recv_sem.at[at],
            device_id={"seq": device}, device_id_type=MESH,
        )
        copy.start()
        self.made.append(copy)
        return copy

    def finish(self):
        for copy in self.made:
            copy.wait_send()


LOW, UP = pl.ds(0, BT), pl.ds(BT, BT)
GATHER_COPIES = 2 * (22 + 16)


class GatherPart:
    def __init__(self, copies, own, out, first, second, at, core):
        self.c, self.own, self.out = copies, own, out
        self.f, self.s, self.at, self.core = first, second, at, core

    def dev(self, df, ds, other=False):
        core = 1 - self.core if other else self.core
        return self.at(ring(self.f, df), ring(self.s, ds)) * 2 + core

    def block(self, df, ds):
        return self.out.at[self.dev(df, ds)]

    def sibling(self, df, ds, src=None):
        here = self.block(df, ds)
        return self.c.start(here if src is None else src, here, self.dev(0, 0, True))

    def begin(self):
        mine = self.block(0, 0)
        self.a_up = self.c.start(self.own, mine, self.dev(1, 0))
        self.a_down = self.c.start(self.own, mine, self.dev(-1, 0))
        self.col = {0: self.column(0, self.own)}
        self.sib = [self.sibling(0, 0, self.own)]

    def column(self, df, src=None):
        here = self.block(df, 0)
        src = here if src is None else src
        return self.c.start(src, here, self.dev(0, 1)), self.c.start(src, here, self.dev(0, -1))

    def near(self):
        self.a_up.wait_recv()
        here = self.block(-1, 0)
        self.b_up = self.c.start(here.at[LOW], here.at[LOW], self.dev(1, 0))
        self.col[-1] = self.column(-1)
        self.sib.append(self.sibling(-1, 0))
        self.a_down.wait_recv()
        here = self.block(1, 0)
        self.b_down = self.c.start(here.at[UP], here.at[UP], self.dev(-1, 0))
        self.col[1] = self.column(1)
        self.sib.append(self.sibling(1, 0))
        self.last = []

    def pass_on(self, df):
        up, down = self.col[df]
        up.wait_recv()
        here = self.block(df, -1)
        one = self.c.start(here.at[LOW], here.at[LOW], self.dev(0, 1))
        self.sib.append(self.sibling(df, -1))
        down.wait_recv()
        here = self.block(df, 1)
        two = self.c.start(here.at[UP], here.at[UP], self.dev(0, -1))
        self.sib.append(self.sibling(df, 1))
        self.last.append((df, one, two))

    def far(self):
        self.b_up.wait_recv()
        self.b_down.wait_recv()
        self.col[2] = self.column(2)
        self.sib.append(self.sibling(2, 0))

    def end(self, i):
        df, one, two = self.last[i]
        one.wait_recv()
        two.wait_recv()
        self.sib.append(self.sibling(df, 2))


def gather_kernel(k_ref, v_ref, ko_ref, vo_ref, send_sem, recv_sem, own_sem):
    me, x, y, core = place()
    greet(me, x, y, core)
    copies = Copies(send_sem, recv_sem)
    parts = (
        GatherPart(copies, k_ref, ko_ref, x, y, lambda f, s: f * SIDE + s, core),
        GatherPart(copies, v_ref, vo_ref, y, x, lambda f, s: s * SIDE + f, core),
    )
    for part in parts:
        part.begin()
    own = [
        pltpu.make_async_copy(k_ref, ko_ref.at[me], own_sem.at[0]),
        pltpu.make_async_copy(v_ref, vo_ref.at[me], own_sem.at[1]),
    ]
    for copy in own:
        copy.start()
    for part in parts:
        part.near()
    for part in parts:
        part.pass_on(0)
    for part in parts:
        part.far()
    for df in (-1, 1, 2):
        for part in parts:
            part.pass_on(df)
    for i in range(4):
        for part in parts:
            part.end(i)
    for copy in own:
        copy.wait()
    for part in parts:
        for copy in part.sib:
            copy.wait_recv()
    copies.finish()


def gather(k, v):
    local = k.shape[0]
    full = jax.ShapeDtypeStruct((2 * CHIPS, local, HW), BF)
    dma = pltpu.SemaphoreType.DMA((GATHER_COPIES,))
    return pl.pallas_call(
        gather_kernel,
        out_shape=(full, full),
        in_specs=[VM, VM],
        out_specs=(VM, VM),
        scratch_shapes=[dma, dma, pltpu.SemaphoreType.DMA((2,))],
        compiler_params=pltpu.CompilerParams(
            collective_id=2, has_side_effects=True, vmem_limit_bytes=16 << 20
        ),
        cost_estimate=pl.CostEstimate(flops=1 << 20, bytes_accessed=8 << 20, transcendentals=0),
        name="gather",
    )(k, v)


SCATTER_COPIES = 2 * 16


class ScatterPart:
    def __init__(self, copies, terms, sib, acc, near, far, fin, near2, far2, out, first, second, x_first, core, dev):
        self.c, self.terms, self.sib, self.acc = copies, terms, sib, acc
        self.near, self.far, self.fin, self.near2, self.far2, self.out = near, far, fin, near2, far2, out
        self.f, self.s, self.x_first, self.core, self.dev = first, second, x_first, core, dev

    def chunk(self, ref, ds, core=None):
        s = ring(self.s, ds)
        ref = ref if core is None else ref.at[core]
        return ref.at[:, s] if self.x_first else ref.at[s]

    def begin(self):
        self.sibs = {}
        for ds in (2, 1, -1, 0):
            self.sibs[ds] = self.c.start(
                self.chunk(self.terms, ds, 1 - self.core), self.chunk(self.sib, ds), self.dev(0, 0, True)
            )

    def own(self, ds, rows):
        mine = self.chunk(self.terms, ds, self.core)[:, rows, :].astype(F32)
        return mine + self.chunk(self.sib, ds)[:, rows, :].astype(F32)

    def put(self, ds, rows, extra=None):
        value = self.own(ds, rows)
        if extra is not None:
            value = value + extra.astype(F32)
        self.chunk(self.acc, ds)[:, rows, :] = value.astype(BF)

    def one(self):
        self.sibs[2].wait_recv()
        for rows in (LOW, UP):
            self.put(2, rows)
        here = self.chunk(self.acc, 2)
        self.far_up = self.c.start(here.at[:, LOW], self.far.at[0], self.dev(0, 1))
        self.far_down = self.c.start(here.at[:, UP], self.far.at[1], self.dev(0, -1))

    def two(self):
        self.sibs[1].wait_recv()
        self.put(1, UP)
        self.up_a = self.c.start(
            self.chunk(self.acc, 1).at[:, UP], self.near.at[0, :, UP], self.dev(0, 1)
        )
        self.sibs[-1].wait_recv()
        self.put(-1, LOW)
        self.down_a = self.c.start(
            self.chunk(self.acc, -1).at[:, LOW], self.near.at[1, :, LOW], self.dev(0, -1)
        )

    def three(self):
        self.far_up.wait_recv()
        self.put(1, LOW, self.far[0])
        self.up_b = self.c.start(
            self.chunk(self.acc, 1).at[:, LOW], self.near.at[0, :, LOW], self.dev(0, 1)
        )
        self.far_down.wait_recv()
        self.put(-1, UP, self.far[1])
        self.down_b = self.c.start(
            self.chunk(self.acc, -1).at[:, UP], self.near.at[1, :, UP], self.dev(0, -1)
        )

    def four(self):
        self.sibs[0].wait_recv()
        for copy in (self.up_a, self.down_a, self.up_b, self.down_b):
            copy.wait_recv()
        for rows in (LOW, UP):
            total = self.own(0, rows) + self.near[0, :, rows, :].astype(F32) + self.near[1, :, rows, :].astype(F32)
            self.fin[:, rows, :] = total.astype(BF)
        here = self.fin.at[ring(self.f, 2)]
        self.far_up = self.c.start(here.at[LOW], self.far2.at[0], self.dev(1, 0))
        self.far_down = self.c.start(here.at[UP], self.far2.at[1], self.dev(-1, 0))
        self.up_a = self.c.start(
            self.fin.at[ring(self.f, 1)].at[UP], self.near2.at[0, UP], self.dev(1, 0)
        )
        self.down_a = self.c.start(
            self.fin.at[ring(self.f, -1)].at[LOW], self.near2.at[1, LOW], self.dev(-1, 0)
        )

    def five(self):
        self.far_up.wait_recv()
        here = self.fin.at[ring(self.f, 1)]
        here[LOW, :] = (here[LOW, :].astype(F32) + self.far2[0].astype(F32)).astype(BF)
        self.up_b = self.c.start(here.at[LOW], self.near2.at[0, LOW], self.dev(1, 0))
        self.far_down.wait_recv()
        here = self.fin.at[ring(self.f, -1)]
        here[UP, :] = (here[UP, :].astype(F32) + self.far2[1].astype(F32)).astype(BF)
        self.down_b = self.c.start(here.at[UP], self.near2.at[1, UP], self.dev(-1, 0))

    def six(self):
        for copy in (self.up_a, self.down_a, self.up_b, self.down_b):
            copy.wait_recv()
        mine = self.fin.at[self.f][...].astype(F32)
        self.out[...] = (mine + self.near2[0].astype(F32) + self.near2[1].astype(F32)).astype(BF)


def scatter_kernel(
    tk_ref, tv_ref, dk_ref, dv_ref,
    sib_k, sib_v, acc_k, acc_v, near_k, near_v, far_k, far_v, fin_k, fin_v,
    near2_k, near2_v, far2_k, far2_v, send_sem, recv_sem,
):
    me, x, y, core = place()
    greet(me, x, y, core)
    copies = Copies(send_sem, recv_sem)

    def dev_k(df, ds, other=False):
        c = 1 - core if other else core
        return (ring(x, df) * SIDE + ring(y, ds)) * 2 + c

    def dev_v(df, ds, other=False):
        c = 1 - core if other else core
        return (ring(x, ds) * SIDE + ring(y, df)) * 2 + c

    parts = (
        ScatterPart(copies, tk_ref, sib_k, acc_k, near_k, far_k, fin_k, near2_k, far2_k, dk_ref, x, y, True, core, dev_k),
        ScatterPart(copies, tv_ref, sib_v, acc_v, near_v, far_v, fin_v, near2_v, far2_v, dv_ref, y, x, False, core, dev_v),
    )
    for stage in ("begin", "one", "two", "three", "four", "five", "six"):
        for part in parts:
            getattr(part, stage)()
    copies.finish()


def scatter(tk, tv):
    local = tk.shape[3]
    out = jax.ShapeDtypeStruct((local, HW), BF)
    dma = pltpu.SemaphoreType.DMA((SCATTER_COPIES,))
    square = pltpu.VMEM((SIDE, SIDE, local, HW), BF)
    near = pltpu.VMEM((2, SIDE, local, HW), BF)
    far = pltpu.VMEM((2, SIDE, BT, HW), BF)
    fin = pltpu.VMEM((SIDE, local, HW), BF)
    near2 = pltpu.VMEM((2, local, HW), BF)
    far2 = pltpu.VMEM((2, BT, HW), BF)
    return pl.pallas_call(
        scatter_kernel,
        out_shape=(out, out),
        in_specs=[VM, VM],
        out_specs=(VM, VM),
        scratch_shapes=[
            square, square, square, square, near, near, far, far, fin, fin,
            near2, near2, far2, far2, dma, dma,
        ],
        compiler_params=pltpu.CompilerParams(
            collective_id=3, has_side_effects=True, vmem_limit_bytes=32 << 20
        ),
        cost_estimate=pl.CostEstimate(flops=1 << 20, bytes_accessed=8 << 20, transcendentals=0),
        name="scatter",
    )(tk, tv)


def body(query, key, value, ssm_input, in_b, in_c, step, rate_log, skip, block_mask, grad_out):
    q, k, v, x, b, c, g = (
        a[0] for a in (query, key, value, ssm_input, in_b, in_c, grad_out)
    )
    local = q.shape[0]
    keys, values = gather(k, v)
    keys, values = keys.reshape(-1, HW), values.reshape(-1, HW)
    y, dx, xt, eg, send, decay, db, dc, cum, rate, skip_terms = ssm_local(
        x, g, b, c, step[0], rate_log, skip
    )
    states = exchange(send, decay)
    y, dx, db, dc, rate = ssm_finish(
        states, y, dx, xt, eg, send, decay, db, dc, cum, rate, b, c, x, g
    )
    attended, dq, terms_k, terms_v = attention(block_mask[0], q, g, keys, values)
    dk, dv = scatter(terms_k, terms_v)
    rate_sum, skip_sum = lax.psum(
        (jnp.sum(rate, axis=1), jnp.sum(skip_terms, axis=1)), ("dp", "seq")
    )
    tokens = lax.axis_size("dp") * lax.axis_size("seq") * local
    layer_out = (attended + y).astype(BF)
    return (
        layer_out[None],
        dq[None],
        dk[None],
        dv[None],
        dx[None],
        db[None],
        dc[None],
        rate_sum / tokens,
        skip_sum / (tokens * HW),
    )


def solution(mesh):
    row = P("dp", "seq", None)
    in_specs = (row,) * 7 + (P(), P(), P("dp", None, None), row)
    out_specs = (row,) * 7 + (P(), P())
    return jax.shard_map(body, mesh=mesh, in_specs=in_specs, out_specs=out_specs, check_vma=False)
```

```python
import functools

import jax
import jax.numpy as jnp
from jax import lax
from jax.experimental import pallas as pl
from jax.experimental.pallas import tpu as pltpu
from jax.sharding import PartitionSpec as P

HW = 128
HEADS = 8
BT = 128
MOST = 24
MOST_PAIRS = MOST // 2
FACTOR = HW ** (-0.5)
LOG2E = 1.4426950408889634
BF = jnp.bfloat16
F32 = jnp.float32
MESH = pl.DeviceIdType.MESH
HIGH = lax.Precision.HIGHEST

VM = pl.BlockSpec(memory_space=pltpu.VMEM)
HB = pl.BlockSpec(memory_space=pltpu.HBM)
SM = pl.BlockSpec(memory_space=pltpu.SMEM)


def nn(a, b):
    return lax.dot_general(a, b, (((1,), (0,)), ((), ())), preferred_element_type=F32)


def nt(a, b):
    return lax.dot_general(a, b, (((1,), (1,)), ((), ())), preferred_element_type=F32)


def tn(a, b):
    return lax.dot_general(a, b, (((0,), (0,)), ((), ())), preferred_element_type=F32)


def cols(h):
    return pl.ds(h * HW, HW)


def attention_kernel(
    mask_ref, q_ref, g_ref, k_ref, v_ref,
    o_ref, dq_ref, tk_ref, tv_ref,
    s_buf, acc_k, acc_v, qs, gs, g_t, o_t, dq_t, picked,
):
    total_blocks = mask_ref.shape[1]
    seq_at = lax.axis_index("seq")
    per_device = q_ref.shape[0] // BT
    acc_k[...] = jnp.zeros_like(acc_k)
    acc_v[...] = jnp.zeros_like(acc_v)

    @pl.loop(0, per_device)
    def _(block):
        row = seq_at * per_device + block

        def note(j, n):
            picked[n] = j
            return n + mask_ref[row, j]

        count = lax.fori_loop(0, total_blocks, note, jnp.int32(0))
        picked[count] = picked[0]
        pairs = (count + 1) // 2
        rows = pl.ds(pl.multiple_of(block * BT, BT), BT)
        for h in range(HEADS):
            qs[cols(h), :] = q_ref[rows, cols(h)]
            g_head = g_ref[rows, cols(h)]
            gs[cols(h), :] = g_head
            g_t[:, cols(h)] = g_head.astype(F32).T

        def starts(p):
            return tuple(pl.multiple_of(picked[2 * p + i] * BT, BT) for i in range(2))

        def pair_of(ref, p):
            first, second = starts(p)
            return jnp.concatenate([ref[pl.ds(first, BT), :], ref[pl.ds(second, BT), :]], axis=0)

        def score_step(p, top):
            s = nt(pair_of(k_ref, p), qs[...])
            bias = jnp.where(2 * p + 1 < count, 0.0, -1e30).astype(F32)
            s = jnp.concatenate([s[:BT], s[BT:] + bias], axis=0)
            s_buf[p] = s
            return jnp.maximum(top, jnp.max(s.reshape(-1, 8, s.shape[1]), axis=0))

        top = lax.fori_loop(
            0, pairs, score_step, jnp.full((8, HEADS * BT), -3e38, F32)
        )
        top = jnp.max(top, axis=0, keepdims=True)
        o_t[...] = jnp.zeros_like(o_t)

        def weight_step(p, total):
            w = jnp.exp2((s_buf[p] - top) * (FACTOR * LOG2E))
            s_buf[p] = w
            o_t[...] += nn(pair_of(v_ref, p).T, w.astype(BF))
            return total + jnp.sum(w.reshape(-1, 8, w.shape[1]), axis=0)

        total = lax.fori_loop(0, pairs, weight_step, jnp.zeros((8, HEADS * BT), F32))
        inverse = 1.0 / jnp.sum(total, axis=0, keepdims=True)
        o_t[...] = o_t[...] * inverse
        delta = jnp.sum(o_t[...] * g_t[...], axis=0, keepdims=True)
        for h in range(HEADS):
            o_ref[rows, cols(h)] = o_t[:, cols(h)].T
        dq_t[...] = jnp.zeros_like(dq_t)

        def gradient_step(p, carry):
            probs = s_buf[p] * inverse
            dprobs = nt(pair_of(v_ref, p), gs[...])
            ds = (probs * (dprobs - delta)).astype(BF)
            dq_t[...] += nn(pair_of(k_ref, p).T, ds)
            dk = nn(ds, qs[...])
            dv = nn(probs.astype(BF), gs[...])
            for i, first in enumerate(starts(p)):
                here = pl.ds(first, BT)
                acc_k[here, :] += dk[i * BT : (i + 1) * BT]
                acc_v[here, :] += dv[i * BT : (i + 1) * BT]
            return carry

        lax.fori_loop(0, pairs, gradient_step, 0)
        for h in range(HEADS):
            dq_ref[rows, cols(h)] = (dq_t[:, cols(h)] * FACTOR).T.astype(BF)

    @pl.loop(0, total_blocks)
    def _(j):
        here = pl.ds(pl.multiple_of(j * BT, BT), BT)
        chip = j // 4
        at = (
            lax.rem(j // 2, 2), chip // SIDE, lax.rem(chip, SIDE),
            pl.ds(pl.multiple_of(lax.rem(j, 2) * BT, BT), BT),
        )
        tk_ref[at] = (acc_k[here, :] * FACTOR).astype(BF)
        tv_ref[at] = acc_v[here, :].astype(BF)


def attention(mask, q, g, keys, values):
    local, wide = q.shape
    total = keys.shape[0]
    width = HEADS * BT
    return pl.pallas_call(
        attention_kernel,
        out_shape=(
            jax.ShapeDtypeStruct((local, wide), F32),
            jax.ShapeDtypeStruct((local, wide), BF),
            jax.ShapeDtypeStruct((2, SIDE, SIDE, local, HW), BF),
            jax.ShapeDtypeStruct((2, SIDE, SIDE, local, HW), BF),
        ),
        in_specs=[SM, VM, VM, VM, VM],
        out_specs=(VM, VM, VM, VM),
        scratch_shapes=[
            pltpu.VMEM((MOST_PAIRS, 2 * BT, width), F32),
            pltpu.VMEM((total, HW), F32),
            pltpu.VMEM((total, HW), F32),
            pltpu.VMEM((width, HW), BF),
            pltpu.VMEM((width, HW), BF),
            pltpu.VMEM((HW, width), F32),
            pltpu.VMEM((HW, width), F32),
            pltpu.VMEM((HW, width), F32),
            pltpu.SMEM((total // BT + 8,), jnp.int32),
        ],
        compiler_params=pltpu.CompilerParams(vmem_limit_bytes=36 << 20),
        cost_estimate=pl.CostEstimate(
            flops=12 * 24 * 1024 * 128 * 128 * 2, bytes_accessed=12 << 20, transcendentals=1 << 22
        ),
        name="attention",
    )(mask, q, g, keys, values)


SIDE = 4
CHIPS = SIDE * SIDE
PEERS = 2 * CHIPS
LAYERS = 8
QUARTER = 32
LOG_ROWS = 16
PACKED = 2 * QUARTER + LOG_ROWS


def place():
    me = lax.axis_index("seq")
    core = lax.rem(me, 2)
    chip = me // 2
    return me, chip // SIDE, lax.rem(chip, SIDE), core


def ring(a, step):
    return lax.rem(a + step + SIDE, SIDE)


def greet(me, also_dp):
    barrier = pltpu.get_barrier_semaphore()

    @pl.loop(1, PEERS)
    def _(r):
        to = lax.rem(me + r, PEERS)
        pl.semaphore_signal(barrier, inc=1, device_id={"seq": to}, device_id_type=MESH)

    waits = PEERS - 1
    if also_dp:
        layer = lax.axis_index("dp")

        @pl.loop(1, LAYERS)
        def _(r):
            to = lax.rem(layer + r, LAYERS)
            pl.semaphore_signal(barrier, inc=1, device_id={"dp": to}, device_id_type=MESH)

        waits += LAYERS - 1
    pl.semaphore_wait(barrier, waits)


def to_peers(me, src, dst, send_sem, recv_sem):
    def copy(r):
        to = lax.rem(me + r, PEERS)
        return pltpu.make_async_remote_copy(
            src_ref=src(to), dst_ref=dst, send_sem=send_sem.at[r], recv_sem=recv_sem.at[r],
            device_id={"seq": to}, device_id_type=MESH,
        )

    def start():
        @pl.loop(1, PEERS)
        def _(r):
            copy(r).start()

    def wait():
        @pl.loop(1, PEERS)
        def _(r):
            copy(r).wait()

    return start, wait


class Copies:
    def __init__(self, send_sem, recv_sem):
        self.send_sem, self.recv_sem, self.made = send_sem, recv_sem, []

    def start(self, src, dst, device):
        at = len(self.made)
        copy = pltpu.make_async_remote_copy(
            src_ref=src, dst_ref=dst, send_sem=self.send_sem.at[at], recv_sem=self.recv_sem.at[at],
            device_id={"seq": device}, device_id_type=MESH,
        )
        copy.start()
        self.made.append(copy)
        return copy

    def finish(self):
        for copy in self.made:
            copy.wait_send()


LOW, UP = pl.ds(0, BT), pl.ds(BT, BT)
GATHER_COPIES = 2 * (22 + 16)


class GatherPart:
    def __init__(self, copies, own, out, first, second, at, core):
        self.c, self.own, self.out = copies, own, out
        self.f, self.s, self.at, self.core = first, second, at, core

    def dev(self, df, ds, other=False):
        core = 1 - self.core if other else self.core
        return self.at(ring(self.f, df), ring(self.s, ds)) * 2 + core

    def block(self, df, ds):
        return self.out.at[self.dev(df, ds)]

    def sibling(self, df, ds, src=None):
        here = self.block(df, ds)
        return self.c.start(here if src is None else src, here, self.dev(0, 0, True))

    def begin(self):
        mine = self.block(0, 0)
        self.a_up = self.c.start(self.own, mine, self.dev(1, 0))
        self.a_down = self.c.start(self.own, mine, self.dev(-1, 0))
        self.col = {0: self.column(0, self.own)}
        self.sib = [self.sibling(0, 0, self.own)]

    def column(self, df, src=None):
        here = self.block(df, 0)
        src = here if src is None else src
        return self.c.start(src, here, self.dev(0, 1)), self.c.start(src, here, self.dev(0, -1))

    def near(self):
        self.a_up.wait_recv()
        here = self.block(-1, 0)
        self.b_up = self.c.start(here.at[LOW], here.at[LOW], self.dev(1, 0))
        self.col[-1] = self.column(-1)
        self.sib.append(self.sibling(-1, 0))
        self.a_down.wait_recv()
        here = self.block(1, 0)
        self.b_down = self.c.start(here.at[UP], here.at[UP], self.dev(-1, 0))
        self.col[1] = self.column(1)
        self.sib.append(self.sibling(1, 0))
        self.last = []

    def pass_on(self, df):
        up, down = self.col[df]
        up.wait_recv()
        here = self.block(df, -1)
        one = self.c.start(here.at[LOW], here.at[LOW], self.dev(0, 1))
        self.sib.append(self.sibling(df, -1))
        down.wait_recv()
        here = self.block(df, 1)
        two = self.c.start(here.at[UP], here.at[UP], self.dev(0, -1))
        self.sib.append(self.sibling(df, 1))
        self.last.append((df, one, two))

    def far(self):
        self.b_up.wait_recv()
        self.b_down.wait_recv()
        self.col[2] = self.column(2)
        self.sib.append(self.sibling(2, 0))

    def end(self, i):
        df, one, two = self.last[i]
        one.wait_recv()
        two.wait_recv()
        self.sib.append(self.sibling(df, 2))


def ssm_prepare(x_ref, step_ref, rate_ref, b_ref, c_ref, cum_ref, dl, bt_ref, ct_ref, sums):
    lanes = lax.broadcasted_iota(jnp.int32, (BT, BT), 1)
    subs = lax.broadcasted_iota(jnp.int32, (BT, BT), 0)
    upper = (subs <= lanes).astype(F32)
    dl[...] = jnp.zeros_like(dl)
    for h in range(HEADS):
        rate = jnp.exp(jnp.full((1, 1), rate_ref[h], F32))
        dl[h : h + 1, :] = -step_ref[h : h + 1, :] * rate
    run_t = []
    for i in range(2):
        run_t.append(
            lax.dot_general(
                dl[:, i * BT : (i + 1) * BT], upper, (((1,), (0,)), ((), ())),
                precision=HIGH, preferred_element_type=F32,
            )
        )
    run0, run1 = run_t[0].T, run_t[1].T
    end0, end1 = run0[BT - 1 : BT, :], run1[BT - 1 : BT, :]
    cum_ref[0] = jnp.concatenate([run0, run1 + end0], axis=0)
    cum_ref[1] = jnp.concatenate([end0 - run0 + end1, end1 - run1], axis=0)
    bt_ref[...] = b_ref[...].T
    ct_ref[...] = c_ref[...].T
    for total in sums:
        total[...] = jnp.zeros_like(total)
    b0, b1 = b_ref[0:BT, :], b_ref[BT : 2 * BT, :]
    c0, c1 = c_ref[0:BT, :], c_ref[BT : 2 * BT, :]
    return run0, run1, run_t[0], run_t[1], end0, end1, nt(c0, b0), nt(c1, b1), nt(c1, b0)


def split3(value):
    rows = lax.broadcasted_iota(jnp.int32, (LOG_ROWS, HW), 0)
    hi = value.astype(BF).astype(F32)
    mid = (value - hi).astype(BF).astype(F32)
    low = value - hi - mid
    out = jnp.where(rows == 0, hi, jnp.where(rows == 1, mid, jnp.where(rows == 2, low, 0.0)))
    return out.astype(BF)


def ssm_head(
    h, ready, x_ref, g_ref, skip_ref, cum_ref, bt_ref, ct_ref, sums,
    y_ref, dx_ref, xt_ref, eg_ref, send_ref, sums_ref,
):
    run0, run1, run0_t, run1_t, end0, end1, cb00, cb11, cb10 = ready
    sum00, sum11, sum10 = sums
    lanes = lax.broadcasted_iota(jnp.int32, (BT, BT), 1)
    subs = lax.broadcasted_iota(jnp.int32, (BT, BT), 0)
    lower = subs >= lanes
    x0, x1 = x_ref[0:BT, cols(h)], x_ref[BT : 2 * BT, cols(h)]
    g0, g1 = g_ref[0:BT, cols(h)], g_ref[BT : 2 * BT, cols(h)]
    gain = skip_ref[h]
    col0, col1 = run0[:, h : h + 1], run1[:, h : h + 1]
    row0, row1 = run0_t[h : h + 1, :], run1_t[h : h + 1, :]
    last0, last1 = end0[:, h : h + 1], end1[:, h : h + 1]

    def part(spread, cb, xs, gs, total, diagonal):
        if diagonal:
            decay = jnp.where(lower, jnp.exp(jnp.where(lower, spread, 0.0)), 0.0)
        else:
            decay = jnp.exp(spread)
        mixed = decay * cb
        outer = nt(gs, xs)
        total[...] += decay * outer
        terms = spread * (mixed * outer)
        mixed = mixed.astype(BF)
        return nn(mixed, xs), tn(mixed, gs), jnp.sum(terms, axis=0, keepdims=True)

    y00, dx00, r00 = part(col0 - row0, cb00, x0, g0, sum00, True)
    y11, dx11, r11 = part(col1 - row1, cb11, x1, g1, sum11, True)
    y10, dx10, r10 = part(col1 + (last0 - row0), cb10, x0, g1, sum10, False)
    xf0, xf1, gf0, gf1 = x0.astype(F32), x1.astype(F32), g0.astype(F32), g1.astype(F32)
    sums_ref[h : h + 1, :] = r00 + r11 + r10
    sums_ref[HEADS + h : HEADS + h + 1, :] = jnp.sum(xf0 * gf0 + xf1 * gf1, axis=0, keepdims=True)
    y_ref[0:BT, cols(h)] = y00 + gain * xf0
    y_ref[BT : 2 * BT, cols(h)] = y11 + y10 + gain * xf1
    dx_ref[0:BT, cols(h)] = dx00 + dx10 + gain * gf0
    dx_ref[BT : 2 * BT, cols(h)] = dx11 + gain * gf1
    start = jnp.exp(cum_ref[0][:, h : h + 1])
    tail = jnp.exp(cum_ref[1][:, h : h + 1])

    def state(turned, scaled, keep_ref):
        high = scaled.astype(BF)
        keep_ref[:, cols(h)] = high
        low = (scaled - high.astype(F32)).astype(BF)
        return (nn(turned, high) + nn(turned, low)).astype(BF)

    end_state = state(bt_ref[...], tail * jnp.concatenate([xf0, xf1], axis=0), xt_ref)
    start_grad = state(ct_ref[...], start * jnp.concatenate([gf0, gf1], axis=0), eg_ref)
    logs = split3(last0 + last1)
    for i in range(4):
        at = slice(i * QUARTER, (i + 1) * QUARTER)
        to = send_ref.at[h * 4 + i]
        to[0:QUARTER, :] = end_state[at]
        to[QUARTER : 2 * QUARTER, :] = start_grad[at]
        to[2 * QUARTER : PACKED, :] = logs


def ssm_end(b_ref, c_ref, sums, db_ref, dc_ref):
    s00, s11, s10 = (total[...].astype(BF) for total in sums)
    b0, b1 = b_ref[0:BT, :], b_ref[BT : 2 * BT, :]
    c0, c1 = c_ref[0:BT, :], c_ref[BT : 2 * BT, :]
    dc_ref[0:BT, :] = nn(s00, b0)
    dc_ref[BT : 2 * BT, :] = nn(s11, b1) + nn(s10, b0)
    db_ref[0:BT, :] = tn(s00, c0) + tn(s10, c1)
    db_ref[BT : 2 * BT, :] = tn(s11, c1)


def front_kernel(
    k_hbm, v_hbm, x_hbm, g_hbm, b_hbm, c_hbm, step_hbm, rate_hbm, skip_hbm,
    ko_ref, vo_ref, got_ref, y_ref, dx_ref, xt_ref, eg_ref, db_ref, dc_ref, cum_ref, sums_ref,
    x_ref, g_ref, b_ref, c_ref, step_ref, rate_ref, skip_ref, send_ref, dl, bt_ref, ct_ref, sum00, sum11, sum10,
    send_sem, recv_sem, own_sem, s1, r1,
):
    me, x, y, core = place()
    sources = (x_hbm, g_hbm, b_hbm, c_hbm, step_hbm, rate_hbm, skip_hbm)
    targets = (x_ref, g_ref, b_ref, c_ref, step_ref, rate_ref, skip_ref)
    loads = [
        pltpu.make_async_copy(src, dst, own_sem.at[i])
        for i, (src, dst) in enumerate(zip(sources, targets))
    ]
    for copy in loads:
        copy.start()
    greet(me, False)
    copies = Copies(send_sem, recv_sem)
    parts = (
        GatherPart(copies, k_hbm, ko_ref, x, y, lambda f, s: f * SIDE + s, core),
        GatherPart(copies, v_hbm, vo_ref, y, x, lambda f, s: s * SIDE + f, core),
    )
    for part in parts:
        part.begin()
    own = [
        pltpu.make_async_copy(k_hbm, ko_ref.at[me], own_sem.at[7]),
        pltpu.make_async_copy(v_hbm, vo_ref.at[me], own_sem.at[8]),
    ]
    for copy in own:
        copy.start()
    for copy in loads:
        copy.wait()

    def all_parts(name, *args):
        return lambda: [getattr(part, name)(*args) for part in parts]

    stages = {
        1: all_parts("near"), 3: all_parts("pass_on", 0), 5: all_parts("far"),
    }
    sums = (sum00, sum11, sum10)
    ready = ssm_prepare(x_ref, step_ref, rate_ref, b_ref, c_ref, cum_ref, dl, bt_ref, ct_ref, sums)
    for h in range(HEADS):
        ssm_head(
            h, ready, x_ref, g_ref, skip_ref, cum_ref, bt_ref, ct_ref, sums,
            y_ref, dx_ref, xt_ref, eg_ref, send_ref, sums_ref,
        )
        if h in stages:
            stages[h]()
    start, wait = to_peers(me, lambda to: send_ref.at[to], got_ref.at[me], s1, r1)
    start()
    got_ref[me] = send_ref[me]
    for df in (-1, 1, 2):
        for part in parts:
            part.pass_on(df)
    ssm_end(b_ref, c_ref, sums, db_ref, dc_ref)
    for i in range(4):
        for part in parts:
            part.end(i)
    for copy in own:
        copy.wait()
    for part in parts:
        for copy in part.sib:
            copy.wait_recv()
    copies.finish()
    wait()


def front(k, v, x, g, b, c, step_t, rate_log, skip):
    local, wide = x.shape
    sds = jax.ShapeDtypeStruct
    full = sds((PEERS, local, HW), BF)
    dma = pltpu.SemaphoreType.DMA
    return pl.pallas_call(
        front_kernel,
        out_shape=(
            full,
            full,
            sds((PEERS, PACKED, HW), BF),
            sds((local, wide), F32),
            sds((local, wide), F32),
            sds((local, wide), BF),
            sds((local, wide), BF),
            sds((local, HW), F32),
            sds((local, HW), F32),
            sds((2, local, HW), F32),
            sds((2 * HEADS, HW), F32),
        ),
        in_specs=[HB] * 9,
        out_specs=(VM,) * 11,
        scratch_shapes=[
            pltpu.VMEM((local, wide), BF),
            pltpu.VMEM((local, wide), BF),
            pltpu.VMEM((local, HW), BF),
            pltpu.VMEM((local, HW), BF),
            pltpu.VMEM((HEADS, local), F32),
            pltpu.SMEM((HEADS,), F32),
            pltpu.SMEM((HEADS,), F32),
            pltpu.VMEM((PEERS, PACKED, HW), BF),
            pltpu.VMEM((HW, local), F32),
            pltpu.VMEM((HW, local), BF),
            pltpu.VMEM((HW, local), BF),
            pltpu.VMEM((BT, BT), F32),
            pltpu.VMEM((BT, BT), F32),
            pltpu.VMEM((BT, BT), F32),
            dma((GATHER_COPIES,)),
            dma((GATHER_COPIES,)),
            dma((9,)),
            dma((PEERS,)),
            dma((PEERS,)),
        ],
        compiler_params=pltpu.CompilerParams(
            collective_id=1, has_side_effects=True, vmem_limit_bytes=14 << 20
        ),
        cost_estimate=pl.CostEstimate(flops=1 << 30, bytes_accessed=16 << 20, transcendentals=1 << 19),
        name="front",
    )(k, v, x, g, b, c, step_t, rate_log, skip)


SCATTER_COPIES = 2 * 16


class ScatterPart:
    def __init__(self, copies, terms, sib, acc, near, far, fin, near2, far2, out, first, second, x_first, core, dev):
        self.c, self.terms, self.sib, self.acc = copies, terms, sib, acc
        self.near, self.far, self.fin, self.near2, self.far2, self.out = near, far, fin, near2, far2, out
        self.f, self.s, self.x_first, self.core, self.dev = first, second, x_first, core, dev

    def chunk(self, ref, ds, core=None):
        s = ring(self.s, ds)
        ref = ref if core is None else ref.at[core]
        return ref.at[:, s] if self.x_first else ref.at[s]

    def begin(self):
        self.sibs = {}
        for ds in (2, 1, -1, 0):
            self.sibs[ds] = self.c.start(
                self.chunk(self.terms, ds, 1 - self.core), self.chunk(self.sib, ds), self.dev(0, 0, True)
            )

    def own(self, ds, rows):
        mine = self.chunk(self.terms, ds, self.core)[:, rows, :].astype(F32)
        return mine + self.chunk(self.sib, ds)[:, rows, :].astype(F32)

    def put(self, ds, rows, extra=None):
        value = self.own(ds, rows)
        if extra is not None:
            value = value + extra.astype(F32)
        self.chunk(self.acc, ds)[:, rows, :] = value.astype(BF)

    def one(self):
        self.sibs[2].wait_recv()
        for rows in (LOW, UP):
            self.put(2, rows)
        here = self.chunk(self.acc, 2)
        self.far_up = self.c.start(here.at[:, LOW], self.far.at[0], self.dev(0, 1))
        self.far_down = self.c.start(here.at[:, UP], self.far.at[1], self.dev(0, -1))

    def two(self):
        self.sibs[1].wait_recv()
        self.put(1, UP)
        self.up_a = self.c.start(
            self.chunk(self.acc, 1).at[:, UP], self.near.at[0, :, UP], self.dev(0, 1)
        )
        self.sibs[-1].wait_recv()
        self.put(-1, LOW)
        self.down_a = self.c.start(
            self.chunk(self.acc, -1).at[:, LOW], self.near.at[1, :, LOW], self.dev(0, -1)
        )

    def three(self):
        self.far_up.wait_recv()
        self.put(1, LOW, self.far[0])
        self.up_b = self.c.start(
            self.chunk(self.acc, 1).at[:, LOW], self.near.at[0, :, LOW], self.dev(0, 1)
        )
        self.far_down.wait_recv()
        self.put(-1, UP, self.far[1])
        self.down_b = self.c.start(
            self.chunk(self.acc, -1).at[:, UP], self.near.at[1, :, UP], self.dev(0, -1)
        )

    def four(self):
        self.sibs[0].wait_recv()
        for copy in (self.up_a, self.down_a, self.up_b, self.down_b):
            copy.wait_recv()
        for rows in (LOW, UP):
            total = self.own(0, rows) + self.near[0, :, rows, :].astype(F32) + self.near[1, :, rows, :].astype(F32)
            self.fin[:, rows, :] = total.astype(BF)
        here = self.fin.at[ring(self.f, 2)]
        self.far_up = self.c.start(here.at[LOW], self.far2.at[0], self.dev(1, 0))
        self.far_down = self.c.start(here.at[UP], self.far2.at[1], self.dev(-1, 0))
        self.up_a = self.c.start(
            self.fin.at[ring(self.f, 1)].at[UP], self.near2.at[0, UP], self.dev(1, 0)
        )
        self.down_a = self.c.start(
            self.fin.at[ring(self.f, -1)].at[LOW], self.near2.at[1, LOW], self.dev(-1, 0)
        )

    def five(self):
        self.far_up.wait_recv()
        here = self.fin.at[ring(self.f, 1)]
        here[LOW, :] = (here[LOW, :].astype(F32) + self.far2[0].astype(F32)).astype(BF)
        self.up_b = self.c.start(here.at[LOW], self.near2.at[0, LOW], self.dev(1, 0))
        self.far_down.wait_recv()
        here = self.fin.at[ring(self.f, -1)]
        here[UP, :] = (here[UP, :].astype(F32) + self.far2[1].astype(F32)).astype(BF)
        self.down_b = self.c.start(here.at[UP], self.near2.at[1, UP], self.dev(-1, 0))

    def six(self):
        for copy in (self.up_a, self.down_a, self.up_b, self.down_b):
            copy.wait_recv()
        mine = self.fin.at[self.f][...].astype(F32)
        self.out[...] = (mine + self.near2[0].astype(F32) + self.near2[1].astype(F32)).astype(BF)


def scan_states(me, got_ref, back_ref, kept, decays, logs, sums_ref):
    log_sum = jnp.sum(got_ref[:, 2 * QUARTER : PACKED, :].astype(F32), axis=1)
    logs[...] = log_sum
    decays[...] = jnp.exp(log_sum)

    def forward(d, state):
        kept[d] = state
        back_ref[d, 0] = state.astype(BF)
        return decays[pl.ds(d, 1), :] * state + got_ref[d, 0:QUARTER, :].astype(F32)

    def backward(k, carry):
        grad, rate = carry
        d = PEERS - 1 - k
        back_ref[d, 1] = grad.astype(BF)
        decay = decays[pl.ds(d, 1), :]
        rate = rate + (logs[pl.ds(d, 1), :] * decay) * (kept[d] * grad)
        return decay * grad + got_ref[d, QUARTER : 2 * QUARTER, :].astype(F32), rate

    zero = jnp.zeros((QUARTER, HW), F32)
    lax.fori_loop(0, PEERS, forward, zero)
    _, rate = lax.fori_loop(0, PEERS, backward, (zero, zero))
    rate = jnp.sum(rate, axis=0, keepdims=True)
    rows = lax.broadcasted_iota(jnp.int32, (2 * HEADS, HW), 0)
    sums_ref[...] += jnp.where(rows == me // 4, rate, 0.0)


def ssm_finish(
    st_ref, o_ref, y_ref, dx_ref, xt_ref, eg_ref, db_ref, dc_ref, cum_ref,
    b_ref, c_ref, x_ref, g_ref, out_ref, dxo_ref, dbo_ref, dco_ref, sums_ref,
):
    dc = dc_ref[...]
    db = db_ref[...]
    for h in range(HEADS):
        s_in = jnp.concatenate([st_ref[h * 4 + i, 0] for i in range(4)], axis=0)
        g_out = jnp.concatenate([st_ref[h * 4 + i, 1] for i in range(4)], axis=0)
        log_start, log_tail = cum_ref[0][:, h : h + 1], cum_ref[1][:, h : h + 1]
        y_in = jnp.exp(log_start) * nn(c_ref[...], s_in)
        dx_in = jnp.exp(log_tail) * nn(b_ref[...], g_out)
        out_ref[:, cols(h)] = (o_ref[:, cols(h)] + (y_ref[:, cols(h)] + y_in)).astype(BF)
        dxo_ref[:, cols(h)] = (dx_ref[:, cols(h)] + dx_in).astype(BF)
        dc = dc + nt(eg_ref[:, cols(h)], s_in)
        db = db + nt(xt_ref[:, cols(h)], g_out)
        gf, xf = g_ref[:, cols(h)].astype(F32), x_ref[:, cols(h)].astype(F32)
        terms = log_start * (gf * y_in) + log_tail * (xf * dx_in)
        sums_ref[h : h + 1, :] += jnp.sum(terms, axis=0, keepdims=True)
    dco_ref[...] = dc.astype(BF)
    dbo_ref[...] = db.astype(BF)


def back_kernel(
    tk_ref, tv_ref, got_ref, o_ref, y_ref, dx_ref, xt_ref, eg_ref, db_ref, dc_ref, cum_ref, sums_in,
    b_ref, c_ref, x_ref, g_ref,
    dk_ref, dv_ref, out_ref, dxo_ref, dbo_ref, dco_ref, total_ref,
    sib_k, sib_v, acc_k, acc_v, near_k, near_v, far_k, far_v, fin_k, fin_v,
    near2_k, near2_v, far2_k, far2_v,
    back_ref, st_ref, kept, decays, logs, sums_ref, seq_sums, seq_total, dp_sums,
    send_sem, recv_sem, s1, r1, s2, r2, s3, r3,
):
    me, x, y, core = place()
    layer = lax.axis_index("dp")
    greet(me, True)
    copies = Copies(send_sem, recv_sem)

    def dev_k(df, ds, other=False):
        c = 1 - core if other else core
        return (ring(x, df) * SIDE + ring(y, ds)) * 2 + c

    def dev_v(df, ds, other=False):
        c = 1 - core if other else core
        return (ring(x, ds) * SIDE + ring(y, df)) * 2 + c

    parts = (
        ScatterPart(copies, tk_ref, sib_k, acc_k, near_k, far_k, fin_k, near2_k, far2_k, dk_ref, x, y, True, core, dev_k),
        ScatterPart(copies, tv_ref, sib_v, acc_v, near_v, far_v, fin_v, near2_v, far2_v, dv_ref, y, x, False, core, dev_v),
    )

    def stage(name):
        for part in parts:
            getattr(part, name)()

    stage("begin")
    sums_ref[...] = sums_in[...]
    scan_states(me, got_ref, back_ref, kept, decays, logs, sums_ref)
    start, wait_states = to_peers(me, lambda to: back_ref.at[to], st_ref.at[me], s1, r1)
    stage("one")
    start()
    st_ref[me] = back_ref[me]
    stage("two")
    stage("three")
    wait_states()
    ssm_finish(
        st_ref, o_ref, y_ref, dx_ref, xt_ref, eg_ref, db_ref, dc_ref, cum_ref,
        b_ref, c_ref, x_ref, g_ref, out_ref, dxo_ref, dbo_ref, dco_ref, sums_ref,
    )
    start, wait_sums = to_peers(me, lambda to: sums_ref, seq_sums.at[me], s2, r2)
    start()
    seq_sums[me] = sums_ref[...]
    stage("four")
    stage("five")
    wait_sums()
    seq_total[...] = jnp.sum(seq_sums[...], axis=0)

    def dp_copy(r):
        to = lax.rem(layer + r, LAYERS)
        return pltpu.make_async_remote_copy(
            src_ref=seq_total, dst_ref=dp_sums.at[layer], send_sem=s3.at[r], recv_sem=r3.at[r],
            device_id={"dp": to}, device_id_type=MESH,
        )

    @pl.loop(1, LAYERS)
    def _(r):
        dp_copy(r).start()

    dp_sums[layer] = seq_total[...]
    stage("six")

    @pl.loop(1, LAYERS)
    def _(r):
        dp_copy(r).wait()

    total = jnp.sum(jnp.sum(dp_sums[...], axis=0), axis=1, keepdims=True)
    total_ref[...] = jnp.broadcast_to(total, total_ref.shape)
    copies.finish()


def back(tk, tv, got, o, y, dx, xt, eg, db, dc, cum, sums, b, c, x, g):
    local, wide = x.shape
    sds = jax.ShapeDtypeStruct
    small = sds((local, HW), BF)
    dma = pltpu.SemaphoreType.DMA
    square = pltpu.VMEM((SIDE, SIDE, local, HW), BF)
    near = pltpu.VMEM((2, SIDE, local, HW), BF)
    far = pltpu.VMEM((2, SIDE, BT, HW), BF)
    fin = pltpu.VMEM((SIDE, local, HW), BF)
    near2 = pltpu.VMEM((2, local, HW), BF)
    far2 = pltpu.VMEM((2, BT, HW), BF)
    states = pltpu.VMEM((PEERS, 2, QUARTER, HW), BF)
    tile = pltpu.VMEM((2 * HEADS, HW), F32)
    return pl.pallas_call(
        back_kernel,
        out_shape=(
            small, small, sds((local, wide), BF), sds((local, wide), BF), small, small,
            sds((2 * HEADS, HW), F32),
        ),
        in_specs=[VM] * 16,
        out_specs=(VM,) * 7,
        scratch_shapes=[
            square, square, square, square, near, near, far, far, fin, fin,
            near2, near2, far2, far2,
            states, states,
            pltpu.VMEM((PEERS, QUARTER, HW), F32),
            pltpu.VMEM((PEERS, HW), F32),
            pltpu.VMEM((PEERS, HW), F32),
            tile,
            pltpu.VMEM((PEERS, 2 * HEADS, HW), F32),
            tile,
            pltpu.VMEM((LAYERS, 2 * HEADS, HW), F32),
            dma((SCATTER_COPIES,)), dma((SCATTER_COPIES,)),
            dma((PEERS,)), dma((PEERS,)), dma((PEERS,)), dma((PEERS,)),
            dma((LAYERS,)), dma((LAYERS,)),
        ],
        compiler_params=pltpu.CompilerParams(
            collective_id=2, has_side_effects=True, vmem_limit_bytes=23 << 20
        ),
        cost_estimate=pl.CostEstimate(flops=1 << 29, bytes_accessed=16 << 20, transcendentals=1 << 12),
        name="back",
    )(tk, tv, got, o, y, dx, xt, eg, db, dc, cum, sums, b, c, x, g)


def emit_kernel(*refs):
    count = (len(refs) - 2) // 2
    total_ref, rate_ref = refs[count], refs[2 * count + 1]
    sem = refs[-1]
    moves = [
        pltpu.make_async_copy(refs[i], refs[count + 1 + i], sem.at[i]) for i in range(count)
    ]
    for move in moves:
        move.start()
    rate_ref[...] = total_ref[...]
    for move in moves:
        move.wait()


def emit(arrays, total):
    count = len(arrays)
    return pl.pallas_call(
        emit_kernel,
        out_shape=tuple(pltpu.HBM(a.shape, a.dtype) for a in arrays)
        + (jax.ShapeDtypeStruct(total.shape, total.dtype),),
        in_specs=[VM] * (count + 1),
        out_specs=(HB,) * count + (VM,),
        scratch_shapes=[pltpu.SemaphoreType.DMA((count,))],
        compiler_params=pltpu.CompilerParams(vmem_limit_bytes=4 << 20),
        cost_estimate=pl.CostEstimate(flops=0, bytes_accessed=3 << 20, transcendentals=0),
        name="emit",
    )(*arrays, total)


def body(query, key, value, ssm_input, in_b, in_c, step, rate_log, skip, block_mask, grad_out):
    q, k, v, x, b, c, g = (
        a[0] for a in (query, key, value, ssm_input, in_b, in_c, grad_out)
    )
    local = q.shape[0]
    fixed = [pltpu.with_memory_space_constraint(a, pltpu.HBM) for a in (k, v, x, g, b, c, step[0].T, rate_log, skip)]
    keys, values, got, *local_terms = front(*fixed)
    keys, values = keys.reshape(-1, HW), values.reshape(-1, HW)
    attended, dq, terms_k, terms_v = attention(block_mask[0], q, g, keys, values)
    dk, dv, layer_out, dx, db, dc, total = back(
        terms_k, terms_v, got, attended, *local_terms, b, c, x, g
    )
    layer_out, dx, dk, dv, db, dc, total = emit((layer_out, dx, dk, dv, db, dc), total)
    tokens = lax.axis_size("dp") * lax.axis_size("seq") * local
    return (
        layer_out[None],
        dq[None],
        dk[None],
        dv[None],
        dx[None],
        db[None],
        dc[None],
        total[:HEADS, 0] / tokens,
        total[HEADS:, 0] / (tokens * HW),
    )


def solution(mesh):
    row = P("dp", "seq", None)
    in_specs = (row,) * 7 + (P(), P(), P("dp", None, None), row)
    out_specs = (row,) * 7 + (P(), P())
    return jax.shard_map(body, mesh=mesh, in_specs=in_specs, out_specs=out_specs, check_vma=False)
```

```python
import functools

import jax
import jax.numpy as jnp
from jax import lax
from jax.experimental import pallas as pl
from jax.experimental.pallas import tpu as pltpu
from jax.sharding import PartitionSpec as P

HW = 128
HEADS = 8
BT = 128
MOST = 24
WIDE = 8
NARROW = 4
FACTOR = HW ** (-0.5)
LOG2E = 1.4426950408889634
BF = jnp.bfloat16
F32 = jnp.float32
MESH = pl.DeviceIdType.MESH
HIGH = lax.Precision.HIGHEST

VM = pl.BlockSpec(memory_space=pltpu.VMEM)
HB = pl.BlockSpec(memory_space=pltpu.HBM)
SM = pl.BlockSpec(memory_space=pltpu.SMEM)


def nn(a, b):
    return lax.dot_general(a, b, (((1,), (0,)), ((), ())), preferred_element_type=F32)


def nt(a, b):
    return lax.dot_general(a, b, (((1,), (1,)), ((), ())), preferred_element_type=F32)


def tn(a, b):
    return lax.dot_general(a, b, (((0,), (0,)), ((), ())), preferred_element_type=F32)


def cols(h):
    return pl.ds(h * HW, HW)


def attention_kernel(
    mask_ref, q_ref, g_ref, k_ref, v_ref,
    o_ref, dq_ref, tk_ref, tv_ref,
    s_buf, acc_k, acc_v, qs, gs, g_t, o_t, dq_t, picked,
):
    total_blocks = mask_ref.shape[1]
    seq_at = lax.axis_index("seq")
    per_device = q_ref.shape[0] // BT
    acc_k[...] = jnp.zeros_like(acc_k)
    acc_v[...] = jnp.zeros_like(acc_v)

    @pl.loop(0, per_device)
    def _(block):
        row = seq_at * per_device + block

        def note(j, n):
            picked[n] = j
            return n + mask_ref[row, j]

        count = lax.fori_loop(0, total_blocks, note, jnp.int32(0), unroll=8)
        for i in range(WIDE - 1):
            picked[count + i] = picked[0]
        rest = lax.rem(count, WIDE)
        wide = count // WIDE + (rest > NARROW).astype(jnp.int32)
        narrow = jnp.logical_and(rest > 0, rest <= NARROW).astype(jnp.int32)
        rows = pl.ds(pl.multiple_of(block * BT, BT), BT)
        for h in range(HEADS):
            qs[cols(h), :] = q_ref[rows, cols(h)]
            g_head = g_ref[rows, cols(h)]
            gs[cols(h), :] = g_head
            g_t[:, cols(h)] = g_head.astype(F32).T

        def starts(at, size):
            return tuple(pl.multiple_of(picked[at + i] * BT, BT) for i in range(size))

        def group_of(ref, at, size):
            return jnp.concatenate([ref[pl.ds(first, BT), :] for first in starts(at, size)], axis=0)

        def over_groups(step, carry):
            carry = lax.fori_loop(0, wide, lambda p, c: step(p * WIDE, WIDE, c), carry)
            return lax.fori_loop(0, narrow, lambda p, c: step(wide * WIDE, NARROW, c), carry)

        def flat(value):
            return value.reshape(-1, value.shape[-1])

        def score_step(at, size, top):
            s = nt(group_of(k_ref, at, size), qs[...])
            parts = [s[:BT]]
            for i in range(1, size):
                bias = jnp.where(at + i < count, 0.0, -1e30).astype(F32)
                parts.append(s[i * BT : (i + 1) * BT] + bias)
            s = jnp.concatenate(parts, axis=0)
            s_buf[pl.ds(at, size)] = s.reshape(size, BT, -1)
            return jnp.maximum(top, jnp.max(s.reshape(-1, 8, s.shape[1]), axis=0))

        top = over_groups(score_step, jnp.full((8, HEADS * BT), -3e38, F32))
        top = jnp.max(top, axis=0, keepdims=True)
        o_t[...] = jnp.zeros_like(o_t)

        def weight_step(at, size, total):
            w = jnp.exp2((flat(s_buf[pl.ds(at, size)]) - top) * (FACTOR * LOG2E))
            s_buf[pl.ds(at, size)] = w.reshape(size, BT, -1)
            o_t[...] += tn(group_of(v_ref, at, size), w.astype(BF))
            return total + jnp.sum(w.reshape(-1, 8, w.shape[1]), axis=0)

        total = over_groups(weight_step, jnp.zeros((8, HEADS * BT), F32))
        inverse = 1.0 / jnp.sum(total, axis=0, keepdims=True)
        o_t[...] = o_t[...] * inverse
        delta = jnp.sum(o_t[...] * g_t[...], axis=0, keepdims=True)
        for h in range(HEADS):
            o_ref[rows, cols(h)] = o_t[:, cols(h)].T
        dq_t[...] = jnp.zeros_like(dq_t)

        def gradient_step(at, size, carry):
            probs = flat(s_buf[pl.ds(at, size)]) * inverse
            dprobs = nt(group_of(v_ref, at, size), gs[...])
            ds = (probs * (dprobs - delta)).astype(BF)
            dq_t[...] += tn(group_of(k_ref, at, size), ds)
            dk = nn(ds, qs[...])
            dv = nn(probs.astype(BF), gs[...])
            for i, first in enumerate(starts(at, size)):
                here = pl.ds(first, BT)
                acc_k[here, :] += dk[i * BT : (i + 1) * BT]
                acc_v[here, :] += dv[i * BT : (i + 1) * BT]
            return carry

        over_groups(gradient_step, 0)
        for h in range(HEADS):
            dq_ref[rows, cols(h)] = (dq_t[:, cols(h)] * FACTOR).T.astype(BF)

    @pl.loop(0, total_blocks)
    def _(j):
        here = pl.ds(pl.multiple_of(j * BT, BT), BT)
        chip = j // 4
        at = (
            lax.rem(j // 2, 2), chip // SIDE, lax.rem(chip, SIDE),
            pl.ds(pl.multiple_of(lax.rem(j, 2) * BT, BT), BT),
        )
        tk_ref[at] = (acc_k[here, :] * FACTOR).astype(BF)
        tv_ref[at] = acc_v[here, :].astype(BF)


def attention(mask, q, g, keys, values):
    local, wide = q.shape
    total = keys.shape[0]
    width = HEADS * BT
    return pl.pallas_call(
        attention_kernel,
        out_shape=(
            jax.ShapeDtypeStruct((local, wide), F32),
            jax.ShapeDtypeStruct((local, wide), BF),
            jax.ShapeDtypeStruct((2, SIDE, SIDE, local, HW), BF),
            jax.ShapeDtypeStruct((2, SIDE, SIDE, local, HW), BF),
        ),
        in_specs=[SM, VM, VM, VM, VM],
        out_specs=(VM, VM, VM, VM),
        scratch_shapes=[
            pltpu.VMEM((MOST, BT, width), F32),
            pltpu.VMEM((total, HW), F32),
            pltpu.VMEM((total, HW), F32),
            pltpu.VMEM((width, HW), BF),
            pltpu.VMEM((width, HW), BF),
            pltpu.VMEM((HW, width), F32),
            pltpu.VMEM((HW, width), F32),
            pltpu.VMEM((HW, width), F32),
            pltpu.SMEM((total // BT + 8,), jnp.int32),
        ],
        compiler_params=pltpu.CompilerParams(vmem_limit_bytes=38 << 20),
        cost_estimate=pl.CostEstimate(
            flops=12 * 24 * 1024 * 128 * 128 * 2, bytes_accessed=12 << 20, transcendentals=1 << 22
        ),
        name="attention",
    )(mask, q, g, keys, values)


SIDE = 4
CHIPS = SIDE * SIDE
PEERS = 2 * CHIPS
LAYERS = 8
QUARTER = 32
LOG_ROWS = 16
PACKED = 2 * QUARTER + LOG_ROWS


def place():
    me = lax.axis_index("seq")
    core = lax.rem(me, 2)
    chip = me // 2
    return me, chip // SIDE, lax.rem(chip, SIDE), core


def ring(a, step):
    return lax.rem(a + step + SIDE, SIDE)


def greet(me, also_dp):
    barrier = pltpu.get_barrier_semaphore()

    @pl.loop(1, PEERS)
    def _(r):
        to = lax.rem(me + r, PEERS)
        pl.semaphore_signal(barrier, inc=1, device_id={"seq": to}, device_id_type=MESH)

    waits = PEERS - 1
    if also_dp:
        layer = lax.axis_index("dp")

        @pl.loop(1, LAYERS)
        def _(r):
            to = lax.rem(layer + r, LAYERS)
            pl.semaphore_signal(barrier, inc=1, device_id={"dp": to}, device_id_type=MESH)

        waits += LAYERS - 1
    pl.semaphore_wait(barrier, waits)


def to_peers(me, src, dst, send_sem, recv_sem):
    def copy(r):
        to = lax.rem(me + r, PEERS)
        return pltpu.make_async_remote_copy(
            src_ref=src(to), dst_ref=dst, send_sem=send_sem.at[r], recv_sem=recv_sem.at[r],
            device_id={"seq": to}, device_id_type=MESH,
        )

    def start():
        @pl.loop(1, PEERS)
        def _(r):
            copy(r).start()

    def wait():
        @pl.loop(1, PEERS)
        def _(r):
            copy(r).wait()

    return start, wait


class Copies:
    def __init__(self, send_sem, recv_sem):
        self.send_sem, self.recv_sem, self.made = send_sem, recv_sem, []

    def start(self, src, dst, device):
        at = len(self.made)
        copy = pltpu.make_async_remote_copy(
            src_ref=src, dst_ref=dst, send_sem=self.send_sem.at[at], recv_sem=self.recv_sem.at[at],
            device_id={"seq": device}, device_id_type=MESH,
        )
        copy.start()
        self.made.append(copy)
        return copy

    def finish(self):
        for copy in self.made:
            copy.wait_send()


LOW, UP = pl.ds(0, BT), pl.ds(BT, BT)
GATHER_COPIES = 2 * (22 + 16)


class GatherPart:
    def __init__(self, copies, own, out, first, second, at, core):
        self.c, self.own, self.out = copies, own, out
        self.f, self.s, self.at, self.core = first, second, at, core

    def dev(self, df, ds, other=False):
        core = 1 - self.core if other else self.core
        return self.at(ring(self.f, df), ring(self.s, ds)) * 2 + core

    def block(self, df, ds):
        return self.out.at[self.dev(df, ds)]

    def sibling(self, df, ds, src=None):
        here = self.block(df, ds)
        return self.c.start(here if src is None else src, here, self.dev(0, 0, True))

    def begin(self):
        mine = self.block(0, 0)
        self.a_up = self.c.start(self.own, mine, self.dev(1, 0))
        self.a_down = self.c.start(self.own, mine, self.dev(-1, 0))
        self.col = {0: self.column(0, self.own)}
        self.sib = [self.sibling(0, 0, self.own)]

    def column(self, df, src=None):
        here = self.block(df, 0)
        src = here if src is None else src
        return self.c.start(src, here, self.dev(0, 1)), self.c.start(src, here, self.dev(0, -1))

    def near(self):
        self.a_up.wait_recv()
        here = self.block(-1, 0)
        self.b_up = self.c.start(here.at[LOW], here.at[LOW], self.dev(1, 0))
        self.col[-1] = self.column(-1)
        self.sib.append(self.sibling(-1, 0))
        self.a_down.wait_recv()
        here = self.block(1, 0)
        self.b_down = self.c.start(here.at[UP], here.at[UP], self.dev(-1, 0))
        self.col[1] = self.column(1)
        self.sib.append(self.sibling(1, 0))
        self.last = []

    def pass_on(self, df):
        up, down = self.col[df]
        up.wait_recv()
        here = self.block(df, -1)
        one = self.c.start(here.at[LOW], here.at[LOW], self.dev(0, 1))
        self.sib.append(self.sibling(df, -1))
        down.wait_recv()
        here = self.block(df, 1)
        two = self.c.start(here.at[UP], here.at[UP], self.dev(0, -1))
        self.sib.append(self.sibling(df, 1))
        self.last.append((df, one, two))

    def far(self):
        self.b_up.wait_recv()
        self.b_down.wait_recv()
        self.col[2] = self.column(2)
        self.sib.append(self.sibling(2, 0))

    def end(self, i):
        df, one, two = self.last[i]
        one.wait_recv()
        two.wait_recv()
        self.sib.append(self.sibling(df, 2))


def ssm_prepare(x_ref, step_ref, rate_ref, b_ref, c_ref, cum_ref, dl, bt_ref, ct_ref, sums):
    lanes = lax.broadcasted_iota(jnp.int32, (BT, BT), 1)
    subs = lax.broadcasted_iota(jnp.int32, (BT, BT), 0)
    upper = (subs <= lanes).astype(F32)
    dl[...] = jnp.zeros_like(dl)
    for h in range(HEADS):
        rate = jnp.exp(jnp.full((1, 1), rate_ref[h], F32))
        dl[h : h + 1, :] = -step_ref[h : h + 1, :] * rate
    run_t = []
    for i in range(2):
        run_t.append(
            lax.dot_general(
                dl[:, i * BT : (i + 1) * BT], upper, (((1,), (0,)), ((), ())),
                precision=HIGH, preferred_element_type=F32,
            )
        )
    run0, run1 = run_t[0].T, run_t[1].T
    end0, end1 = run0[BT - 1 : BT, :], run1[BT - 1 : BT, :]
    cum_ref[0] = jnp.concatenate([run0, run1 + end0], axis=0)
    cum_ref[1] = jnp.concatenate([end0 - run0 + end1, end1 - run1], axis=0)
    bt_ref[...] = b_ref[...].T
    ct_ref[...] = c_ref[...].T
    for total in sums:
        total[...] = jnp.zeros_like(total)
    b0, b1 = b_ref[0:BT, :], b_ref[BT : 2 * BT, :]
    c0, c1 = c_ref[0:BT, :], c_ref[BT : 2 * BT, :]
    return run0, run1, run_t[0], run_t[1], end0, end1, nt(c0, b0), nt(c1, b1), nt(c1, b0)


def split3(value):
    rows = lax.broadcasted_iota(jnp.int32, (LOG_ROWS, HW), 0)
    hi = value.astype(BF).astype(F32)
    mid = (value - hi).astype(BF).astype(F32)
    low = value - hi - mid
    out = jnp.where(rows == 0, hi, jnp.where(rows == 1, mid, jnp.where(rows == 2, low, 0.0)))
    return out.astype(BF)


def ssm_head(
    h, ready, x_ref, g_ref, skip_ref, cum_ref, bt_ref, ct_ref, sums,
    y_ref, dx_ref, xt_ref, eg_ref, send_ref, sums_ref,
):
    run0, run1, run0_t, run1_t, end0, end1, cb00, cb11, cb10 = ready
    sum00, sum11, sum10 = sums
    lanes = lax.broadcasted_iota(jnp.int32, (BT, BT), 1)
    subs = lax.broadcasted_iota(jnp.int32, (BT, BT), 0)
    lower = subs >= lanes
    x0, x1 = x_ref[0:BT, cols(h)], x_ref[BT : 2 * BT, cols(h)]
    g0, g1 = g_ref[0:BT, cols(h)], g_ref[BT : 2 * BT, cols(h)]
    gain = skip_ref[h]
    col0, col1 = run0[:, h : h + 1], run1[:, h : h + 1]
    row0, row1 = run0_t[h : h + 1, :], run1_t[h : h + 1, :]
    last0, last1 = end0[:, h : h + 1], end1[:, h : h + 1]

    def part(spread, cb, xs, gs, total, diagonal):
        if diagonal:
            decay = jnp.where(lower, jnp.exp(jnp.where(lower, spread, 0.0)), 0.0)
        else:
            decay = jnp.exp(spread)
        mixed = decay * cb
        outer = nt(gs, xs)
        total[...] += decay * outer
        terms = spread * (mixed * outer)
        mixed = mixed.astype(BF)
        return nn(mixed, xs), tn(mixed, gs), jnp.sum(terms, axis=0, keepdims=True)

    y00, dx00, r00 = part(col0 - row0, cb00, x0, g0, sum00, True)
    y11, dx11, r11 = part(col1 - row1, cb11, x1, g1, sum11, True)
    y10, dx10, r10 = part(col1 + (last0 - row0), cb10, x0, g1, sum10, False)
    xf0, xf1, gf0, gf1 = x0.astype(F32), x1.astype(F32), g0.astype(F32), g1.astype(F32)
    sums_ref[h : h + 1, :] = r00 + r11 + r10
    sums_ref[HEADS + h : HEADS + h + 1, :] = jnp.sum(xf0 * gf0 + xf1 * gf1, axis=0, keepdims=True)
    y_ref[0:BT, cols(h)] = y00 + gain * xf0
    y_ref[BT : 2 * BT, cols(h)] = y11 + y10 + gain * xf1
    dx_ref[0:BT, cols(h)] = dx00 + dx10 + gain * gf0
    dx_ref[BT : 2 * BT, cols(h)] = dx11 + gain * gf1
    start = jnp.exp(cum_ref[0][:, h : h + 1])
    tail = jnp.exp(cum_ref[1][:, h : h + 1])

    def state(turned, scaled, keep_ref):
        high = scaled.astype(BF)
        keep_ref[:, cols(h)] = high
        low = (scaled - high.astype(F32)).astype(BF)
        return (nn(turned, high) + nn(turned, low)).astype(BF)

    end_state = state(bt_ref[...], tail * jnp.concatenate([xf0, xf1], axis=0), xt_ref)
    start_grad = state(ct_ref[...], start * jnp.concatenate([gf0, gf1], axis=0), eg_ref)
    logs = split3(last0 + last1)
    for i in range(4):
        at = slice(i * QUARTER, (i + 1) * QUARTER)
        to = send_ref.at[h * 4 + i]
        to[0:QUARTER, :] = end_state[at]
        to[QUARTER : 2 * QUARTER, :] = start_grad[at]
        to[2 * QUARTER : PACKED, :] = logs


def ssm_end(b_ref, c_ref, sums, db_ref, dc_ref):
    s00, s11, s10 = (total[...].astype(BF) for total in sums)
    b0, b1 = b_ref[0:BT, :], b_ref[BT : 2 * BT, :]
    c0, c1 = c_ref[0:BT, :], c_ref[BT : 2 * BT, :]
    dc_ref[0:BT, :] = nn(s00, b0)
    dc_ref[BT : 2 * BT, :] = nn(s11, b1) + nn(s10, b0)
    db_ref[0:BT, :] = tn(s00, c0) + tn(s10, c1)
    db_ref[BT : 2 * BT, :] = tn(s11, c1)


def front_kernel(
    k_hbm, v_hbm, x_hbm, g_hbm, b_hbm, c_hbm, step_hbm, rate_hbm, skip_hbm,
    ko_ref, vo_ref, got_ref, y_ref, dx_ref, xt_ref, eg_ref, db_ref, dc_ref, cum_ref, sums_ref,
    x_ref, g_ref, b_ref, c_ref, step_ref, rate_ref, skip_ref, send_ref, dl, bt_ref, ct_ref, sum00, sum11, sum10,
    send_sem, recv_sem, own_sem, s1, r1,
):
    me, x, y, core = place()
    sources = (x_hbm, g_hbm, b_hbm, c_hbm, step_hbm, rate_hbm, skip_hbm)
    targets = (x_ref, g_ref, b_ref, c_ref, step_ref, rate_ref, skip_ref)
    loads = [
        pltpu.make_async_copy(src, dst, own_sem.at[i])
        for i, (src, dst) in enumerate(zip(sources, targets))
    ]
    for copy in loads:
        copy.start()
    greet(me, False)
    copies = Copies(send_sem, recv_sem)
    parts = (
        GatherPart(copies, k_hbm, ko_ref, x, y, lambda f, s: f * SIDE + s, core),
        GatherPart(copies, v_hbm, vo_ref, y, x, lambda f, s: s * SIDE + f, core),
    )
    for part in parts:
        part.begin()
    own = [
        pltpu.make_async_copy(k_hbm, ko_ref.at[me], own_sem.at[7]),
        pltpu.make_async_copy(v_hbm, vo_ref.at[me], own_sem.at[8]),
    ]
    for copy in own:
        copy.start()
    for copy in loads:
        copy.wait()

    def all_parts(name, *args):
        return lambda: [getattr(part, name)(*args) for part in parts]

    stages = {
        1: all_parts("near"), 3: all_parts("pass_on", 0), 5: all_parts("far"),
    }
    sums = (sum00, sum11, sum10)
    ready = ssm_prepare(x_ref, step_ref, rate_ref, b_ref, c_ref, cum_ref, dl, bt_ref, ct_ref, sums)
    for h in range(HEADS):
        ssm_head(
            h, ready, x_ref, g_ref, skip_ref, cum_ref, bt_ref, ct_ref, sums,
            y_ref, dx_ref, xt_ref, eg_ref, send_ref, sums_ref,
        )
        if h in stages:
            stages[h]()
    start, wait = to_peers(me, lambda to: send_ref.at[to], got_ref.at[me], s1, r1)
    start()
    got_ref[me] = send_ref[me]
    for df in (-1, 1, 2):
        for part in parts:
            part.pass_on(df)
    ssm_end(b_ref, c_ref, sums, db_ref, dc_ref)
    for i in range(4):
        for part in parts:
            part.end(i)
    for copy in own:
        copy.wait()
    for part in parts:
        for copy in part.sib:
            copy.wait_recv()
    copies.finish()
    wait()


def front(k, v, x, g, b, c, step_t, rate_log, skip):
    local, wide = x.shape
    sds = jax.ShapeDtypeStruct
    full = sds((PEERS, local, HW), BF)
    dma = pltpu.SemaphoreType.DMA
    return pl.pallas_call(
        front_kernel,
        out_shape=(
            full,
            full,
            sds((PEERS, PACKED, HW), BF),
            sds((local, wide), F32),
            sds((local, wide), F32),
            sds((local, wide), BF),
            sds((local, wide), BF),
            sds((local, HW), F32),
            sds((local, HW), F32),
            sds((2, local, HW), F32),
            sds((2 * HEADS, HW), F32),
        ),
        in_specs=[HB] * 9,
        out_specs=(VM,) * 11,
        scratch_shapes=[
            pltpu.VMEM((local, wide), BF),
            pltpu.VMEM((local, wide), BF),
            pltpu.VMEM((local, HW), BF),
            pltpu.VMEM((local, HW), BF),
            pltpu.VMEM((HEADS, local), F32),
            pltpu.SMEM((HEADS,), F32),
            pltpu.SMEM((HEADS,), F32),
            pltpu.VMEM((PEERS, PACKED, HW), BF),
            pltpu.VMEM((HW, local), F32),
            pltpu.VMEM((HW, local), BF),
            pltpu.VMEM((HW, local), BF),
            pltpu.VMEM((BT, BT), F32),
            pltpu.VMEM((BT, BT), F32),
            pltpu.VMEM((BT, BT), F32),
            dma((GATHER_COPIES,)),
            dma((GATHER_COPIES,)),
            dma((9,)),
            dma((PEERS,)),
            dma((PEERS,)),
        ],
        compiler_params=pltpu.CompilerParams(
            collective_id=1, has_side_effects=True, vmem_limit_bytes=14 << 20
        ),
        cost_estimate=pl.CostEstimate(flops=1 << 30, bytes_accessed=16 << 20, transcendentals=1 << 19),
        name="front",
    )(k, v, x, g, b, c, step_t, rate_log, skip)


SCATTER_COPIES = 2 * 16


class ScatterPart:
    def __init__(self, copies, terms, sib, acc, near, far, fin, near2, far2, out, first, second, x_first, core, dev):
        self.c, self.terms, self.sib, self.acc = copies, terms, sib, acc
        self.near, self.far, self.fin, self.near2, self.far2, self.out = near, far, fin, near2, far2, out
        self.f, self.s, self.x_first, self.core, self.dev = first, second, x_first, core, dev

    def chunk(self, ref, ds, core=None):
        s = ring(self.s, ds)
        ref = ref if core is None else ref.at[core]
        return ref.at[:, s] if self.x_first else ref.at[s]

    def begin(self):
        self.sibs = {}
        for ds in (2, 1, -1, 0):
            self.sibs[ds] = self.c.start(
                self.chunk(self.terms, ds, 1 - self.core), self.chunk(self.sib, ds), self.dev(0, 0, True)
            )

    def own(self, ds, rows):
        mine = self.chunk(self.terms, ds, self.core)[:, rows, :].astype(F32)
        return mine + self.chunk(self.sib, ds)[:, rows, :].astype(F32)

    def put(self, ds, rows, extra=None):
        value = self.own(ds, rows)
        if extra is not None:
            value = value + extra.astype(F32)
        self.chunk(self.acc, ds)[:, rows, :] = value.astype(BF)

    def one(self):
        self.sibs[2].wait_recv()
        for rows in (LOW, UP):
            self.put(2, rows)
        here = self.chunk(self.acc, 2)
        self.far_up = self.c.start(here.at[:, LOW], self.far.at[0], self.dev(0, 1))
        self.far_down = self.c.start(here.at[:, UP], self.far.at[1], self.dev(0, -1))

    def two(self):
        self.sibs[1].wait_recv()
        self.put(1, UP)
        self.up_a = self.c.start(
            self.chunk(self.acc, 1).at[:, UP], self.near.at[0, :, UP], self.dev(0, 1)
        )
        self.sibs[-1].wait_recv()
        self.put(-1, LOW)
        self.down_a = self.c.start(
            self.chunk(self.acc, -1).at[:, LOW], self.near.at[1, :, LOW], self.dev(0, -1)
        )

    def three(self):
        self.far_up.wait_recv()
        self.put(1, LOW, self.far[0])
        self.up_b = self.c.start(
            self.chunk(self.acc, 1).at[:, LOW], self.near.at[0, :, LOW], self.dev(0, 1)
        )
        self.far_down.wait_recv()
        self.put(-1, UP, self.far[1])
        self.down_b = self.c.start(
            self.chunk(self.acc, -1).at[:, UP], self.near.at[1, :, UP], self.dev(0, -1)
        )

    def four(self):
        self.sibs[0].wait_recv()
        for copy in (self.up_a, self.down_a, self.up_b, self.down_b):
            copy.wait_recv()
        for rows in (LOW, UP):
            total = self.own(0, rows) + self.near[0, :, rows, :].astype(F32) + self.near[1, :, rows, :].astype(F32)
            self.fin[:, rows, :] = total.astype(BF)
        here = self.fin.at[ring(self.f, 2)]
        self.far_up = self.c.start(here.at[LOW], self.far2.at[0], self.dev(1, 0))
        self.far_down = self.c.start(here.at[UP], self.far2.at[1], self.dev(-1, 0))
        self.up_a = self.c.start(
            self.fin.at[ring(self.f, 1)].at[UP], self.near2.at[0, UP], self.dev(1, 0)
        )
        self.down_a = self.c.start(
            self.fin.at[ring(self.f, -1)].at[LOW], self.near2.at[1, LOW], self.dev(-1, 0)
        )

    def five(self):
        self.far_up.wait_recv()
        here = self.fin.at[ring(self.f, 1)]
        here[LOW, :] = (here[LOW, :].astype(F32) + self.far2[0].astype(F32)).astype(BF)
        self.up_b = self.c.start(here.at[LOW], self.near2.at[0, LOW], self.dev(1, 0))
        self.far_down.wait_recv()
        here = self.fin.at[ring(self.f, -1)]
        here[UP, :] = (here[UP, :].astype(F32) + self.far2[1].astype(F32)).astype(BF)
        self.down_b = self.c.start(here.at[UP], self.near2.at[1, UP], self.dev(-1, 0))

    def six(self):
        for copy in (self.up_a, self.down_a, self.up_b, self.down_b):
            copy.wait_recv()
        mine = self.fin.at[self.f][...].astype(F32)
        self.out[...] = (mine + self.near2[0].astype(F32) + self.near2[1].astype(F32)).astype(BF)


def scan_states(me, got_ref, back_ref, kept, decays, logs, sums_ref):
    log_sum = jnp.sum(got_ref[:, 2 * QUARTER : PACKED, :].astype(F32), axis=1)
    logs[...] = log_sum
    decays[...] = jnp.exp(log_sum)

    def forward(d, state):
        kept[d] = state
        back_ref[d, 0] = state.astype(BF)
        return decays[pl.ds(d, 1), :] * state + got_ref[d, 0:QUARTER, :].astype(F32)

    def backward(k, carry):
        grad, rate = carry
        d = PEERS - 1 - k
        back_ref[d, 1] = grad.astype(BF)
        decay = decays[pl.ds(d, 1), :]
        rate = rate + (logs[pl.ds(d, 1), :] * decay) * (kept[d] * grad)
        return decay * grad + got_ref[d, QUARTER : 2 * QUARTER, :].astype(F32), rate

    zero = jnp.zeros((QUARTER, HW), F32)
    lax.fori_loop(0, PEERS, forward, zero)
    _, rate = lax.fori_loop(0, PEERS, backward, (zero, zero))
    rate = jnp.sum(rate, axis=0, keepdims=True)
    rows = lax.broadcasted_iota(jnp.int32, (2 * HEADS, HW), 0)
    sums_ref[...] += jnp.where(rows == me // 4, rate, 0.0)


def ssm_finish(
    st_ref, o_ref, y_ref, dx_ref, xt_ref, eg_ref, db_ref, dc_ref, cum_ref,
    b_ref, c_ref, x_ref, g_ref, out_ref, dxo_ref, dbo_ref, dco_ref, sums_ref,
):
    dc = dc_ref[...]
    db = db_ref[...]
    for h in range(HEADS):
        s_in = jnp.concatenate([st_ref[h * 4 + i, 0] for i in range(4)], axis=0)
        g_out = jnp.concatenate([st_ref[h * 4 + i, 1] for i in range(4)], axis=0)
        log_start, log_tail = cum_ref[0][:, h : h + 1], cum_ref[1][:, h : h + 1]
        y_in = jnp.exp(log_start) * nn(c_ref[...], s_in)
        dx_in = jnp.exp(log_tail) * nn(b_ref[...], g_out)
        out_ref[:, cols(h)] = (o_ref[:, cols(h)] + (y_ref[:, cols(h)] + y_in)).astype(BF)
        dxo_ref[:, cols(h)] = (dx_ref[:, cols(h)] + dx_in).astype(BF)
        dc = dc + nt(eg_ref[:, cols(h)], s_in)
        db = db + nt(xt_ref[:, cols(h)], g_out)
        gf, xf = g_ref[:, cols(h)].astype(F32), x_ref[:, cols(h)].astype(F32)
        terms = log_start * (gf * y_in) + log_tail * (xf * dx_in)
        sums_ref[h : h + 1, :] += jnp.sum(terms, axis=0, keepdims=True)
    dco_ref[...] = dc.astype(BF)
    dbo_ref[...] = db.astype(BF)


def back_kernel(
    tk_ref, tv_ref, got_ref, o_ref, y_ref, dx_ref, xt_ref, eg_ref, db_ref, dc_ref, cum_ref, sums_in,
    b_ref, c_ref, x_ref, g_ref,
    dk_ref, dv_ref, out_ref, dxo_ref, dbo_ref, dco_ref, total_ref,
    sib_k, sib_v, acc_k, acc_v, near_k, near_v, far_k, far_v, fin_k, fin_v,
    near2_k, near2_v, far2_k, far2_v,
    back_ref, st_ref, kept, decays, logs, sums_ref, seq_sums, seq_total, dp_sums,
    send_sem, recv_sem, s1, r1, s2, r2, s3, r3,
):
    me, x, y, core = place()
    layer = lax.axis_index("dp")
    greet(me, True)
    copies = Copies(send_sem, recv_sem)

    def dev_k(df, ds, other=False):
        c = 1 - core if other else core
        return (ring(x, df) * SIDE + ring(y, ds)) * 2 + c

    def dev_v(df, ds, other=False):
        c = 1 - core if other else core
        return (ring(x, ds) * SIDE + ring(y, df)) * 2 + c

    parts = (
        ScatterPart(copies, tk_ref, sib_k, acc_k, near_k, far_k, fin_k, near2_k, far2_k, dk_ref, x, y, True, core, dev_k),
        ScatterPart(copies, tv_ref, sib_v, acc_v, near_v, far_v, fin_v, near2_v, far2_v, dv_ref, y, x, False, core, dev_v),
    )

    def stage(name):
        for part in parts:
            getattr(part, name)()

    stage("begin")
    sums_ref[...] = sums_in[...]
    scan_states(me, got_ref, back_ref, kept, decays, logs, sums_ref)
    start, wait_states = to_peers(me, lambda to: back_ref.at[to], st_ref.at[me], s1, r1)
    stage("one")
    start()
    st_ref[me] = back_ref[me]
    stage("two")
    stage("three")
    wait_states()
    ssm_finish(
        st_ref, o_ref, y_ref, dx_ref, xt_ref, eg_ref, db_ref, dc_ref, cum_ref,
        b_ref, c_ref, x_ref, g_ref, out_ref, dxo_ref, dbo_ref, dco_ref, sums_ref,
    )
    start, wait_sums = to_peers(me, lambda to: sums_ref, seq_sums.at[me], s2, r2)
    start()
    seq_sums[me] = sums_ref[...]
    stage("four")
    wait_sums()
    seq_total[...] = jnp.sum(seq_sums[...], axis=0)

    def dp_copy(r):
        to = lax.rem(layer + r, LAYERS)
        return pltpu.make_async_remote_copy(
            src_ref=seq_total, dst_ref=dp_sums.at[layer], send_sem=s3.at[r], recv_sem=r3.at[r],
            device_id={"dp": to}, device_id_type=MESH,
        )

    @pl.loop(1, LAYERS)
    def _(r):
        dp_copy(r).start()

    dp_sums[layer] = seq_total[...]
    stage("five")
    stage("six")

    @pl.loop(1, LAYERS)
    def _(r):
        dp_copy(r).wait()

    total = jnp.sum(jnp.sum(dp_sums[...], axis=0), axis=1, keepdims=True)
    total_ref[...] = jnp.broadcast_to(total, total_ref.shape)
    copies.finish()


def back(tk, tv, got, o, y, dx, xt, eg, db, dc, cum, sums, b, c, x, g):
    local, wide = x.shape
    sds = jax.ShapeDtypeStruct
    small = sds((local, HW), BF)
    dma = pltpu.SemaphoreType.DMA
    square = pltpu.VMEM((SIDE, SIDE, local, HW), BF)
    near = pltpu.VMEM((2, SIDE, local, HW), BF)
    far = pltpu.VMEM((2, SIDE, BT, HW), BF)
    fin = pltpu.VMEM((SIDE, local, HW), BF)
    near2 = pltpu.VMEM((2, local, HW), BF)
    far2 = pltpu.VMEM((2, BT, HW), BF)
    states = pltpu.VMEM((PEERS, 2, QUARTER, HW), BF)
    tile = pltpu.VMEM((2 * HEADS, HW), F32)
    return pl.pallas_call(
        back_kernel,
        out_shape=(
            small, small, sds((local, wide), BF), sds((local, wide), BF), small, small,
            sds((2 * HEADS, HW), F32),
        ),
        in_specs=[VM] * 16,
        out_specs=(VM,) * 7,
        scratch_shapes=[
            square, square, square, square, near, near, far, far, fin, fin,
            near2, near2, far2, far2,
            states, states,
            pltpu.VMEM((PEERS, QUARTER, HW), F32),
            pltpu.VMEM((PEERS, HW), F32),
            pltpu.VMEM((PEERS, HW), F32),
            tile,
            pltpu.VMEM((PEERS, 2 * HEADS, HW), F32),
            tile,
            pltpu.VMEM((LAYERS, 2 * HEADS, HW), F32),
            dma((SCATTER_COPIES,)), dma((SCATTER_COPIES,)),
            dma((PEERS,)), dma((PEERS,)), dma((PEERS,)), dma((PEERS,)),
            dma((LAYERS,)), dma((LAYERS,)),
        ],
        compiler_params=pltpu.CompilerParams(
            collective_id=2, has_side_effects=True, vmem_limit_bytes=23 << 20
        ),
        cost_estimate=pl.CostEstimate(flops=1 << 29, bytes_accessed=16 << 20, transcendentals=1 << 12),
        name="back",
    )(tk, tv, got, o, y, dx, xt, eg, db, dc, cum, sums, b, c, x, g)


def emit_kernel(*refs):
    count = (len(refs) - 2) // 2
    total_ref, rate_ref = refs[count], refs[2 * count + 1]
    sem = refs[-1]
    moves = [
        pltpu.make_async_copy(refs[i], refs[count + 1 + i], sem.at[i]) for i in range(count)
    ]
    for move in moves:
        move.start()
    rate_ref[...] = total_ref[...]
    for move in moves:
        move.wait()


def emit(arrays, total):
    count = len(arrays)
    return pl.pallas_call(
        emit_kernel,
        out_shape=tuple(pltpu.HBM(a.shape, a.dtype) for a in arrays)
        + (jax.ShapeDtypeStruct(total.shape, total.dtype),),
        in_specs=[VM] * (count + 1),
        out_specs=(HB,) * count + (VM,),
        scratch_shapes=[pltpu.SemaphoreType.DMA((count,))],
        compiler_params=pltpu.CompilerParams(vmem_limit_bytes=4 << 20),
        cost_estimate=pl.CostEstimate(flops=0, bytes_accessed=3 << 20, transcendentals=0),
        name="emit",
    )(*arrays, total)


def body(query, key, value, ssm_input, in_b, in_c, step, rate_log, skip, block_mask, grad_out):
    q, k, v, x, b, c, g = (
        a[0] for a in (query, key, value, ssm_input, in_b, in_c, grad_out)
    )
    local = q.shape[0]
    fixed = [pltpu.with_memory_space_constraint(a, pltpu.HBM) for a in (k, v, x, g, b, c, step[0].T, rate_log, skip)]
    keys, values, got, *local_terms = front(*fixed)
    keys, values = keys.reshape(-1, HW), values.reshape(-1, HW)
    attended, dq, terms_k, terms_v = attention(block_mask[0], q, g, keys, values)
    dk, dv, layer_out, dx, db, dc, total = back(
        terms_k, terms_v, got, attended, *local_terms, b, c, x, g
    )
    layer_out, dx, dk, dv, db, dc, total = emit((layer_out, dx, dk, dv, db, dc), total)
    tokens = lax.axis_size("dp") * lax.axis_size("seq") * local
    return (
        layer_out[None],
        dq[None],
        dk[None],
        dv[None],
        dx[None],
        db[None],
        dc[None],
        total[:HEADS, 0] / tokens,
        total[HEADS:, 0] / (tokens * HW),
    )


def solution(mesh):
    row = P("dp", "seq", None)
    in_specs = (row,) * 7 + (P(), P(), P("dp", None, None), row)
    out_specs = (row,) * 7 + (P(), P())
    return jax.shard_map(body, mesh=mesh, in_specs=in_specs, out_specs=out_specs, check_vma=False)
```

```python
import functools

import jax
import jax.numpy as jnp
from jax import lax
from jax.experimental import pallas as pl
from jax.experimental.pallas import tpu as pltpu
from jax.sharding import PartitionSpec as P

HW = 128
HEADS = 8
BT = 128
MOST = 24
WIDE = 8
NARROW = 4
FACTOR = HW ** (-0.5)
LOG2E = 1.4426950408889634
BF = jnp.bfloat16
F32 = jnp.float32
MESH = pl.DeviceIdType.MESH
HIGH = lax.Precision.HIGHEST

VM = pl.BlockSpec(memory_space=pltpu.VMEM)
HB = pl.BlockSpec(memory_space=pltpu.HBM)
SM = pl.BlockSpec(memory_space=pltpu.SMEM)


def nn(a, b):
    return lax.dot_general(a, b, (((1,), (0,)), ((), ())), preferred_element_type=F32)


def nt(a, b):
    return lax.dot_general(a, b, (((1,), (1,)), ((), ())), preferred_element_type=F32)


def tn(a, b):
    return lax.dot_general(a, b, (((0,), (0,)), ((), ())), preferred_element_type=F32)


def cols(h):
    return pl.ds(h * HW, HW)


def attention_kernel(
    mask_ref, q_ref, g_ref, k_ref, v_ref,
    o_ref, dq_ref, tk_ref, tv_ref,
    s_buf, acc_k, acc_v, qs, gs, g_t, o_t, dq_t, picked,
):
    total_blocks = mask_ref.shape[1]
    seq_at = lax.axis_index("seq")
    per_device = q_ref.shape[0] // BT
    acc_k[...] = jnp.zeros_like(acc_k)
    acc_v[...] = jnp.zeros_like(acc_v)

    @pl.loop(0, per_device)
    def _(block):
        row = seq_at * per_device + block

        def note(j, n):
            picked[n] = j
            return n + mask_ref[row, j]

        count = lax.fori_loop(0, total_blocks, note, jnp.int32(0), unroll=8)
        for i in range(WIDE - 1):
            picked[count + i] = picked[0]
        rest = lax.rem(count, WIDE)
        wide = count // WIDE + (rest > NARROW).astype(jnp.int32)
        narrow = jnp.logical_and(rest > 0, rest <= NARROW).astype(jnp.int32)
        rows = pl.ds(pl.multiple_of(block * BT, BT), BT)
        for h in range(HEADS):
            qs[cols(h), :] = q_ref[rows, cols(h)]
            g_head = g_ref[rows, cols(h)]
            gs[cols(h), :] = g_head
            g_t[:, cols(h)] = g_head.astype(F32).T

        def starts(at, size):
            return tuple(pl.multiple_of(picked[at + i] * BT, BT) for i in range(size))

        def group_of(ref, at, size):
            return jnp.concatenate([ref[pl.ds(first, BT), :] for first in starts(at, size)], axis=0)

        def over_groups(step, carry):
            carry = lax.fori_loop(0, wide, lambda p, c: step(p * WIDE, WIDE, c), carry)
            return lax.fori_loop(0, narrow, lambda p, c: step(wide * WIDE, NARROW, c), carry)

        def flat(value):
            return value.reshape(-1, value.shape[-1])

        def score_step(at, size, top):
            s = nt(group_of(k_ref, at, size), qs[...])
            parts = [s[:BT]]
            for i in range(1, size):
                bias = jnp.where(at + i < count, 0.0, -1e30).astype(F32)
                parts.append(s[i * BT : (i + 1) * BT] + bias)
            s = jnp.concatenate(parts, axis=0)
            s_buf[pl.ds(at, size)] = s.reshape(size, BT, -1)
            return jnp.maximum(top, jnp.max(s.reshape(-1, 8, s.shape[1]), axis=0))

        top = over_groups(score_step, jnp.full((8, HEADS * BT), -3e38, F32))
        top = jnp.max(top, axis=0, keepdims=True)
        o_t[...] = jnp.zeros_like(o_t)

        def weight_step(at, size, total):
            w = jnp.exp2((flat(s_buf[pl.ds(at, size)]) - top) * (FACTOR * LOG2E))
            s_buf[pl.ds(at, size)] = w.reshape(size, BT, -1)
            o_t[...] += tn(group_of(v_ref, at, size), w.astype(BF))
            return total + jnp.sum(w.reshape(-1, 8, w.shape[1]), axis=0)

        total = over_groups(weight_step, jnp.zeros((8, HEADS * BT), F32))
        inverse = 1.0 / jnp.sum(total, axis=0, keepdims=True)
        o_t[...] = o_t[...] * inverse
        delta = jnp.sum(o_t[...] * g_t[...], axis=0, keepdims=True)
        for h in range(HEADS):
            o_ref[rows, cols(h)] = o_t[:, cols(h)].T
        dq_t[...] = jnp.zeros_like(dq_t)

        def gradient_step(at, size, carry):
            probs = flat(s_buf[pl.ds(at, size)]) * inverse
            dprobs = nt(group_of(v_ref, at, size), gs[...])
            ds = (probs * (dprobs - delta)).astype(BF)
            dq_t[...] += tn(group_of(k_ref, at, size), ds)
            dk = nn(ds, qs[...])
            dv = nn(probs.astype(BF), gs[...])
            for i, first in enumerate(starts(at, size)):
                here = pl.ds(first, BT)
                acc_k[here, :] += dk[i * BT : (i + 1) * BT]
                acc_v[here, :] += dv[i * BT : (i + 1) * BT]
            return carry

        over_groups(gradient_step, 0)
        for h in range(HEADS):
            dq_ref[rows, cols(h)] = (dq_t[:, cols(h)] * FACTOR).T.astype(BF)

    @pl.loop(0, total_blocks)
    def _(j):
        here = pl.ds(pl.multiple_of(j * BT, BT), BT)
        chip = j // 4
        at = (
            lax.rem(j // 2, 2), chip // SIDE, lax.rem(chip, SIDE),
            pl.ds(pl.multiple_of(lax.rem(j, 2) * BT, BT), BT),
        )
        tk_ref[at] = (acc_k[here, :] * FACTOR).astype(BF)
        tv_ref[at] = acc_v[here, :].astype(BF)


def attention(mask, q, g, keys, values):
    local, wide = q.shape
    total = keys.shape[0]
    width = HEADS * BT
    return pl.pallas_call(
        attention_kernel,
        out_shape=(
            jax.ShapeDtypeStruct((local, wide), F32),
            jax.ShapeDtypeStruct((local, wide), BF),
            jax.ShapeDtypeStruct((2, SIDE, SIDE, local, HW), BF),
            jax.ShapeDtypeStruct((2, SIDE, SIDE, local, HW), BF),
        ),
        in_specs=[SM, VM, VM, VM, VM],
        out_specs=(VM, VM, VM, VM),
        scratch_shapes=[
            pltpu.VMEM((MOST, BT, width), F32),
            pltpu.VMEM((total, HW), F32),
            pltpu.VMEM((total, HW), F32),
            pltpu.VMEM((width, HW), BF),
            pltpu.VMEM((width, HW), BF),
            pltpu.VMEM((HW, width), F32),
            pltpu.VMEM((HW, width), F32),
            pltpu.VMEM((HW, width), F32),
            pltpu.SMEM((total // BT + 8,), jnp.int32),
        ],
        compiler_params=pltpu.CompilerParams(vmem_limit_bytes=38 << 20),
        cost_estimate=pl.CostEstimate(
            flops=12 * 24 * 1024 * 128 * 128 * 2, bytes_accessed=12 << 20, transcendentals=1 << 22
        ),
        name="attention",
    )(mask, q, g, keys, values)


SIDE = 4
CHIPS = SIDE * SIDE
PEERS = 2 * CHIPS
LAYERS = 8
QUARTER = 32
LOG_ROWS = 16
PACKED = 2 * QUARTER + LOG_ROWS


def place():
    me = lax.axis_index("seq")
    core = lax.rem(me, 2)
    chip = me // 2
    return me, chip // SIDE, lax.rem(chip, SIDE), core


def ring(a, step):
    return lax.rem(a + step + SIDE, SIDE)


def greet(chip, core, also_dp):
    barrier = pltpu.get_barrier_semaphore()

    @pl.loop(1, CHIPS)
    def _(r):
        to = lax.rem(chip + r, CHIPS) * 2 + core
        pl.semaphore_signal(barrier, inc=1, device_id={"seq": to}, device_id_type=MESH)

    pl.semaphore_signal(
        barrier, inc=1, device_id={"seq": chip * 2 + 1 - core}, device_id_type=MESH
    )
    waits = CHIPS
    if also_dp:
        layer = lax.axis_index("dp")

        @pl.loop(1, LAYERS)
        def _(r):
            to = lax.rem(layer + r, LAYERS)
            pl.semaphore_signal(barrier, inc=1, device_id={"dp": to}, device_id_type=MESH)

        waits += LAYERS - 1
    pl.semaphore_wait(barrier, waits)


def to_peers(chip, core, src, dst, send_sem, recv_sem):
    def copy(r):
        to = lax.rem(chip + r, CHIPS)
        return pltpu.make_async_remote_copy(
            src_ref=src(to), dst_ref=dst, send_sem=send_sem.at[r], recv_sem=recv_sem.at[r],
            device_id={"seq": to * 2 + core}, device_id_type=MESH,
        )

    def start():
        @pl.loop(1, CHIPS)
        def _(r):
            copy(r).start()

    def wait():
        @pl.loop(1, CHIPS)
        def _(r):
            copy(r).wait()

    return start, wait


def to_sibling(chip, core, src, dst, sems):
    return pltpu.make_async_remote_copy(
        src_ref=src, dst_ref=dst, send_sem=sems.at[0], recv_sem=sems.at[1],
        device_id={"seq": chip * 2 + 1 - core}, device_id_type=MESH,
    )


class Copies:
    def __init__(self, send_sem, recv_sem):
        self.send_sem, self.recv_sem, self.made = send_sem, recv_sem, []

    def start(self, src, dst, device):
        at = len(self.made)
        copy = pltpu.make_async_remote_copy(
            src_ref=src, dst_ref=dst, send_sem=self.send_sem.at[at], recv_sem=self.recv_sem.at[at],
            device_id={"seq": device}, device_id_type=MESH,
        )
        copy.start()
        self.made.append(copy)
        return copy

    def finish(self):
        for copy in self.made:
            copy.wait_send()


LOW, UP = pl.ds(0, BT), pl.ds(BT, BT)
GATHER_COPIES = 2 * (22 + 16)


class GatherPart:
    def __init__(self, copies, own, out, first, second, at, core):
        self.c, self.own, self.out = copies, own, out
        self.f, self.s, self.at, self.core = first, second, at, core

    def dev(self, df, ds, other=False):
        core = 1 - self.core if other else self.core
        return self.at(ring(self.f, df), ring(self.s, ds)) * 2 + core

    def block(self, df, ds):
        return self.out.at[self.dev(df, ds)]

    def sibling(self, df, ds, src=None):
        here = self.block(df, ds)
        return self.c.start(here if src is None else src, here, self.dev(0, 0, True))

    def begin(self):
        mine = self.block(0, 0)
        self.a_up = self.c.start(self.own, mine, self.dev(1, 0))
        self.a_down = self.c.start(self.own, mine, self.dev(-1, 0))
        self.col = {0: self.column(0, self.own)}
        self.sib = [self.sibling(0, 0, self.own)]

    def column(self, df, src=None):
        here = self.block(df, 0)
        src = here if src is None else src
        return self.c.start(src, here, self.dev(0, 1)), self.c.start(src, here, self.dev(0, -1))

    def near(self):
        self.a_up.wait_recv()
        here = self.block(-1, 0)
        self.b_up = self.c.start(here.at[LOW], here.at[LOW], self.dev(1, 0))
        self.col[-1] = self.column(-1)
        self.sib.append(self.sibling(-1, 0))
        self.a_down.wait_recv()
        here = self.block(1, 0)
        self.b_down = self.c.start(here.at[UP], here.at[UP], self.dev(-1, 0))
        self.col[1] = self.column(1)
        self.sib.append(self.sibling(1, 0))
        self.last = []

    def pass_on(self, df):
        up, down = self.col[df]
        up.wait_recv()
        here = self.block(df, -1)
        one = self.c.start(here.at[LOW], here.at[LOW], self.dev(0, 1))
        self.sib.append(self.sibling(df, -1))
        down.wait_recv()
        here = self.block(df, 1)
        two = self.c.start(here.at[UP], here.at[UP], self.dev(0, -1))
        self.sib.append(self.sibling(df, 1))
        self.last.append((df, one, two))

    def far(self):
        self.b_up.wait_recv()
        self.b_down.wait_recv()
        self.col[2] = self.column(2)
        self.sib.append(self.sibling(2, 0))

    def end(self, i):
        df, one, two = self.last[i]
        one.wait_recv()
        two.wait_recv()
        self.sib.append(self.sibling(df, 2))


def ssm_prepare(x_ref, step_ref, rate_ref, b_ref, c_ref, cum_ref, dl, bt_ref, ct_ref, sums):
    lanes = lax.broadcasted_iota(jnp.int32, (BT, BT), 1)
    subs = lax.broadcasted_iota(jnp.int32, (BT, BT), 0)
    upper = (subs <= lanes).astype(F32)
    dl[...] = jnp.zeros_like(dl)
    for h in range(HEADS):
        rate = jnp.exp(jnp.full((1, 1), rate_ref[h], F32))
        dl[h : h + 1, :] = -step_ref[h : h + 1, :] * rate
    run_t = []
    for i in range(2):
        run_t.append(
            lax.dot_general(
                dl[:, i * BT : (i + 1) * BT], upper, (((1,), (0,)), ((), ())),
                precision=HIGH, preferred_element_type=F32,
            )
        )
    run0, run1 = run_t[0].T, run_t[1].T
    end0, end1 = run0[BT - 1 : BT, :], run1[BT - 1 : BT, :]
    cum_ref[0] = jnp.concatenate([run0, run1 + end0], axis=0)
    cum_ref[1] = jnp.concatenate([end0 - run0 + end1, end1 - run1], axis=0)
    bt_ref[...] = b_ref[...].T
    ct_ref[...] = c_ref[...].T
    for total in sums:
        total[...] = jnp.zeros_like(total)
    b0, b1 = b_ref[0:BT, :], b_ref[BT : 2 * BT, :]
    c0, c1 = c_ref[0:BT, :], c_ref[BT : 2 * BT, :]
    return run0, run1, run_t[0], run_t[1], end0, end1, nt(c0, b0), nt(c1, b1), nt(c1, b0)


def split3(value):
    rows = lax.broadcasted_iota(jnp.int32, (LOG_ROWS, HW), 0)
    hi = value.astype(BF).astype(F32)
    mid = (value - hi).astype(BF).astype(F32)
    low = value - hi - mid
    out = jnp.where(rows == 0, hi, jnp.where(rows == 1, mid, jnp.where(rows == 2, low, 0.0)))
    return out.astype(BF)


def ssm_head(
    h, ready, x_ref, g_ref, skip_ref, cum_ref, bt_ref, ct_ref, sums,
    y_ref, dx_ref, xt_ref, eg_ref, send_ref, sums_ref,
):
    run0, run1, run0_t, run1_t, end0, end1, cb00, cb11, cb10 = ready
    sum00, sum11, sum10 = sums
    lanes = lax.broadcasted_iota(jnp.int32, (BT, BT), 1)
    subs = lax.broadcasted_iota(jnp.int32, (BT, BT), 0)
    lower = subs >= lanes
    x0, x1 = x_ref[0:BT, cols(h)], x_ref[BT : 2 * BT, cols(h)]
    g0, g1 = g_ref[0:BT, cols(h)], g_ref[BT : 2 * BT, cols(h)]
    gain = skip_ref[h]
    col0, col1 = run0[:, h : h + 1], run1[:, h : h + 1]
    row0, row1 = run0_t[h : h + 1, :], run1_t[h : h + 1, :]
    last0, last1 = end0[:, h : h + 1], end1[:, h : h + 1]

    def part(spread, cb, xs, gs, total, diagonal):
        if diagonal:
            decay = jnp.where(lower, jnp.exp(jnp.where(lower, spread, 0.0)), 0.0)
        else:
            decay = jnp.exp(spread)
        mixed = decay * cb
        outer = nt(gs, xs)
        total[...] += decay * outer
        terms = spread * (mixed * outer)
        mixed = mixed.astype(BF)
        return nn(mixed, xs), tn(mixed, gs), jnp.sum(terms, axis=0, keepdims=True)

    y00, dx00, r00 = part(col0 - row0, cb00, x0, g0, sum00, True)
    y11, dx11, r11 = part(col1 - row1, cb11, x1, g1, sum11, True)
    y10, dx10, r10 = part(col1 + (last0 - row0), cb10, x0, g1, sum10, False)
    xf0, xf1, gf0, gf1 = x0.astype(F32), x1.astype(F32), g0.astype(F32), g1.astype(F32)
    sums_ref[h : h + 1, :] = r00 + r11 + r10
    sums_ref[HEADS + h : HEADS + h + 1, :] = jnp.sum(xf0 * gf0 + xf1 * gf1, axis=0, keepdims=True)
    y_ref[0:BT, cols(h)] = y00 + gain * xf0
    y_ref[BT : 2 * BT, cols(h)] = y11 + y10 + gain * xf1
    dx_ref[0:BT, cols(h)] = dx00 + dx10 + gain * gf0
    dx_ref[BT : 2 * BT, cols(h)] = dx11 + gain * gf1
    start = jnp.exp(cum_ref[0][:, h : h + 1])
    tail = jnp.exp(cum_ref[1][:, h : h + 1])

    def state(turned, scaled, keep_ref):
        high = scaled.astype(BF)
        keep_ref[:, cols(h)] = high
        low = (scaled - high.astype(F32)).astype(BF)
        return (nn(turned, high) + nn(turned, low)).astype(BF)

    end_state = state(bt_ref[...], tail * jnp.concatenate([xf0, xf1], axis=0), xt_ref)
    start_grad = state(ct_ref[...], start * jnp.concatenate([gf0, gf1], axis=0), eg_ref)
    logs = split3(last0 + last1)
    for i in range(4):
        at = slice(i * QUARTER, (i + 1) * QUARTER)
        to = send_ref.at[(h * 4 + i) % 2, (h * 4 + i) // 2]
        to[0:QUARTER, :] = end_state[at]
        to[QUARTER : 2 * QUARTER, :] = start_grad[at]
        to[2 * QUARTER : PACKED, :] = logs


def ssm_end(b_ref, c_ref, sums, db_ref, dc_ref):
    s00, s11, s10 = (total[...].astype(BF) for total in sums)
    b0, b1 = b_ref[0:BT, :], b_ref[BT : 2 * BT, :]
    c0, c1 = c_ref[0:BT, :], c_ref[BT : 2 * BT, :]
    dc_ref[0:BT, :] = nn(s00, b0)
    dc_ref[BT : 2 * BT, :] = nn(s11, b1) + nn(s10, b0)
    db_ref[0:BT, :] = tn(s00, c0) + tn(s10, c1)
    db_ref[BT : 2 * BT, :] = tn(s11, c1)


def combine(core, send_ref, sib_ref, comb_ref):
    first = (core == 0).astype(F32)
    second = 1.0 - first
    for h in range(HEADS):
        at = pl.ds(2 * h, 2)
        mine, other = send_ref[core, at].astype(F32), sib_ref[core, at].astype(F32)
        log_mine = jnp.sum(mine[0, 2 * QUARTER :], axis=0, keepdims=True)
        log_other = jnp.sum(other[0, 2 * QUARTER :], axis=0, keepdims=True)
        by_mine, by_other = jnp.exp(log_mine), jnp.exp(log_other)
        ends = slice(0, QUARTER)
        comb_ref[at, ends, :] = (
            (first * by_other + second) * mine[:, ends] + (first + second * by_mine) * other[:, ends]
        ).astype(BF)
        grads = slice(QUARTER, 2 * QUARTER)
        comb_ref[at, grads, :] = (
            (first + second * by_other) * mine[:, grads] + (first * by_mine + second) * other[:, grads]
        ).astype(BF)
        logs = split3(log_mine + log_other)
        for i in range(2):
            comb_ref[2 * h + i, 2 * QUARTER : PACKED, :] = logs


def front_kernel(
    k_hbm, v_hbm, x_hbm, g_hbm, b_hbm, c_hbm, step_hbm, rate_hbm, skip_hbm,
    ko_ref, vo_ref, got_ref, sib_ref, y_ref, dx_ref, xt_ref, eg_ref, db_ref, dc_ref, cum_ref, sums_ref,
    x_ref, g_ref, b_ref, c_ref, step_ref, rate_ref, skip_ref, send_ref, comb_ref, dl, bt_ref, ct_ref, sum00, sum11, sum10,
    send_sem, recv_sem, own_sem, s1, r1, pair_sem,
):
    me, x, y, core = place()
    sources = (x_hbm, g_hbm, b_hbm, c_hbm, step_hbm, rate_hbm, skip_hbm)
    targets = (x_ref, g_ref, b_ref, c_ref, step_ref, rate_ref, skip_ref)
    loads = [
        pltpu.make_async_copy(src, dst, own_sem.at[i])
        for i, (src, dst) in enumerate(zip(sources, targets))
    ]
    for copy in loads:
        copy.start()
    chip = me // 2
    greet(chip, core, False)
    copies = Copies(send_sem, recv_sem)
    parts = (
        GatherPart(copies, k_hbm, ko_ref, x, y, lambda f, s: f * SIDE + s, core),
        GatherPart(copies, v_hbm, vo_ref, y, x, lambda f, s: s * SIDE + f, core),
    )
    for part in parts:
        part.begin()
    own = [
        pltpu.make_async_copy(k_hbm, ko_ref.at[me], own_sem.at[7]),
        pltpu.make_async_copy(v_hbm, vo_ref.at[me], own_sem.at[8]),
    ]
    for copy in own:
        copy.start()
    for copy in loads:
        copy.wait()

    def all_parts(name, *args):
        return lambda: [getattr(part, name)(*args) for part in parts]

    stages = {
        1: all_parts("near"), 3: all_parts("pass_on", 0), 5: all_parts("far"),
    }
    sums = (sum00, sum11, sum10)
    ready = ssm_prepare(x_ref, step_ref, rate_ref, b_ref, c_ref, cum_ref, dl, bt_ref, ct_ref, sums)
    for h in range(HEADS):
        ssm_head(
            h, ready, x_ref, g_ref, skip_ref, cum_ref, bt_ref, ct_ref, sums,
            y_ref, dx_ref, xt_ref, eg_ref, send_ref, sums_ref,
        )
        if h in stages:
            stages[h]()
    pair = to_sibling(chip, core, send_ref, sib_ref, pair_sem)
    pair.start()
    for part in parts:
        part.pass_on(-1)
    ssm_end(b_ref, c_ref, sums, db_ref, dc_ref)
    pair.wait()
    combine(core, send_ref, sib_ref, comb_ref)
    start, wait = to_peers(chip, core, lambda to: comb_ref.at[to], got_ref.at[chip], s1, r1)
    start()
    got_ref[chip] = comb_ref[chip]
    for df in (1, 2):
        for part in parts:
            part.pass_on(df)
    for i in range(4):
        for part in parts:
            part.end(i)
    for copy in own:
        copy.wait()
    for part in parts:
        for copy in part.sib:
            copy.wait_recv()
    copies.finish()
    wait()


def front(k, v, x, g, b, c, step_t, rate_log, skip):
    local, wide = x.shape
    sds = jax.ShapeDtypeStruct
    full = sds((PEERS, local, HW), BF)
    dma = pltpu.SemaphoreType.DMA
    return pl.pallas_call(
        front_kernel,
        out_shape=(
            full,
            full,
            sds((CHIPS, PACKED, HW), BF),
            sds((2, CHIPS, PACKED, HW), BF),
            sds((local, wide), F32),
            sds((local, wide), F32),
            sds((local, wide), BF),
            sds((local, wide), BF),
            sds((local, HW), F32),
            sds((local, HW), F32),
            sds((2, local, HW), F32),
            sds((2 * HEADS, HW), F32),
        ),
        in_specs=[HB] * 9,
        out_specs=(VM,) * 12,
        scratch_shapes=[
            pltpu.VMEM((local, wide), BF),
            pltpu.VMEM((local, wide), BF),
            pltpu.VMEM((local, HW), BF),
            pltpu.VMEM((local, HW), BF),
            pltpu.VMEM((HEADS, local), F32),
            pltpu.SMEM((HEADS,), F32),
            pltpu.SMEM((HEADS,), F32),
            pltpu.VMEM((2, CHIPS, PACKED, HW), BF),
            pltpu.VMEM((CHIPS, PACKED, HW), BF),
            pltpu.VMEM((HW, local), F32),
            pltpu.VMEM((HW, local), BF),
            pltpu.VMEM((HW, local), BF),
            pltpu.VMEM((BT, BT), F32),
            pltpu.VMEM((BT, BT), F32),
            pltpu.VMEM((BT, BT), F32),
            dma((GATHER_COPIES,)),
            dma((GATHER_COPIES,)),
            dma((9,)),
            dma((CHIPS,)),
            dma((CHIPS,)),
            dma((2,)),
        ],
        compiler_params=pltpu.CompilerParams(
            collective_id=1, has_side_effects=True, vmem_limit_bytes=14 << 20
        ),
        cost_estimate=pl.CostEstimate(flops=1 << 30, bytes_accessed=16 << 20, transcendentals=1 << 19),
        name="front",
    )(k, v, x, g, b, c, step_t, rate_log, skip)


SCATTER_COPIES = 2 * 16


class ScatterPart:
    def __init__(self, copies, terms, sib, acc, near, far, fin, near2, far2, out, first, second, x_first, core, dev):
        self.c, self.terms, self.sib, self.acc = copies, terms, sib, acc
        self.near, self.far, self.fin, self.near2, self.far2, self.out = near, far, fin, near2, far2, out
        self.f, self.s, self.x_first, self.core, self.dev = first, second, x_first, core, dev

    def chunk(self, ref, ds, core=None):
        s = ring(self.s, ds)
        ref = ref if core is None else ref.at[core]
        return ref.at[:, s] if self.x_first else ref.at[s]

    def begin(self):
        self.sibs = {}
        for ds in (2, 1, -1, 0):
            self.sibs[ds] = self.c.start(
                self.chunk(self.terms, ds, 1 - self.core), self.chunk(self.sib, ds), self.dev(0, 0, True)
            )

    def own(self, ds, rows):
        mine = self.chunk(self.terms, ds, self.core)[:, rows, :].astype(F32)
        return mine + self.chunk(self.sib, ds)[:, rows, :].astype(F32)

    def put(self, ds, rows, extra=None):
        value = self.own(ds, rows)
        if extra is not None:
            value = value + extra.astype(F32)
        self.chunk(self.acc, ds)[:, rows, :] = value.astype(BF)

    def one(self):
        self.sibs[2].wait_recv()
        for rows in (LOW, UP):
            self.put(2, rows)
        here = self.chunk(self.acc, 2)
        self.far_up = self.c.start(here.at[:, LOW], self.far.at[0], self.dev(0, 1))
        self.far_down = self.c.start(here.at[:, UP], self.far.at[1], self.dev(0, -1))

    def two(self):
        self.sibs[1].wait_recv()
        self.put(1, UP)
        self.up_a = self.c.start(
            self.chunk(self.acc, 1).at[:, UP], self.near.at[0, :, UP], self.dev(0, 1)
        )
        self.sibs[-1].wait_recv()
        self.put(-1, LOW)
        self.down_a = self.c.start(
            self.chunk(self.acc, -1).at[:, LOW], self.near.at[1, :, LOW], self.dev(0, -1)
        )

    def three(self):
        self.far_up.wait_recv()
        self.put(1, LOW, self.far[0])
        self.up_b = self.c.start(
            self.chunk(self.acc, 1).at[:, LOW], self.near.at[0, :, LOW], self.dev(0, 1)
        )
        self.far_down.wait_recv()
        self.put(-1, UP, self.far[1])
        self.down_b = self.c.start(
            self.chunk(self.acc, -1).at[:, UP], self.near.at[1, :, UP], self.dev(0, -1)
        )

    def four(self):
        self.sibs[0].wait_recv()
        for copy in (self.up_a, self.down_a, self.up_b, self.down_b):
            copy.wait_recv()
        for rows in (LOW, UP):
            total = self.own(0, rows) + self.near[0, :, rows, :].astype(F32) + self.near[1, :, rows, :].astype(F32)
            self.fin[:, rows, :] = total.astype(BF)
        here = self.fin.at[ring(self.f, 2)]
        self.far_up = self.c.start(here.at[LOW], self.far2.at[0], self.dev(1, 0))
        self.far_down = self.c.start(here.at[UP], self.far2.at[1], self.dev(-1, 0))
        self.up_a = self.c.start(
            self.fin.at[ring(self.f, 1)].at[UP], self.near2.at[0, UP], self.dev(1, 0)
        )
        self.down_a = self.c.start(
            self.fin.at[ring(self.f, -1)].at[LOW], self.near2.at[1, LOW], self.dev(-1, 0)
        )

    def five(self):
        self.far_up.wait_recv()
        here = self.fin.at[ring(self.f, 1)]
        here[LOW, :] = (here[LOW, :].astype(F32) + self.far2[0].astype(F32)).astype(BF)
        self.up_b = self.c.start(here.at[LOW], self.near2.at[0, LOW], self.dev(1, 0))
        self.far_down.wait_recv()
        here = self.fin.at[ring(self.f, -1)]
        here[UP, :] = (here[UP, :].astype(F32) + self.far2[1].astype(F32)).astype(BF)
        self.down_b = self.c.start(here.at[UP], self.near2.at[1, UP], self.dev(-1, 0))

    def six(self):
        for copy in (self.up_a, self.down_a, self.up_b, self.down_b):
            copy.wait_recv()
        mine = self.fin.at[self.f][...].astype(F32)
        self.out[...] = (mine + self.near2[0].astype(F32) + self.near2[1].astype(F32)).astype(BF)


def scan_states(me, got_ref, back_ref, kept, decays, logs, sums_ref):
    log_sum = jnp.sum(got_ref[:, 2 * QUARTER : PACKED, :].astype(F32), axis=1)
    logs[...] = log_sum
    decays[...] = jnp.exp(log_sum)

    def forward(d, state):
        kept[d] = state
        back_ref[d, 0] = state.astype(BF)
        return decays[pl.ds(d, 1), :] * state + got_ref[d, 0:QUARTER, :].astype(F32)

    def backward(k, carry):
        grad, rate = carry
        d = CHIPS - 1 - k
        back_ref[d, 1] = grad.astype(BF)
        decay = decays[pl.ds(d, 1), :]
        rate = rate + (logs[pl.ds(d, 1), :] * decay) * (kept[d] * grad)
        return decay * grad + got_ref[d, QUARTER : 2 * QUARTER, :].astype(F32), rate

    zero = jnp.zeros((QUARTER, HW), F32)
    lax.fori_loop(0, CHIPS, forward, zero)
    _, rate = lax.fori_loop(0, CHIPS, backward, (zero, zero))
    rate = jnp.sum(rate, axis=0, keepdims=True)
    rows = lax.broadcasted_iota(jnp.int32, (2 * HEADS, HW), 0)
    sums_ref[...] += jnp.where(rows == me // 4, rate, 0.0)


def ssm_finish(
    core, st_ref, sib_ref, o_ref, y_ref, dx_ref, xt_ref, eg_ref, db_ref, dc_ref, cum_ref,
    b_ref, c_ref, x_ref, g_ref, out_ref, dxo_ref, dbo_ref, dco_ref, sums_ref,
):
    dc = dc_ref[...]
    db = db_ref[...]
    first = (core == 0).astype(F32)
    second = 1.0 - first
    for h in range(HEADS):
        owners = [((h * 4 + i) % 2, (h * 4 + i) // 2) for i in range(4)]

        def joined(pick):
            return jnp.concatenate([pick(*at) for at in owners], axis=0).astype(F32)

        chip_state = joined(lambda a, b: st_ref[a, b, 0])
        chip_grad = joined(lambda a, b: st_ref[a, b, 1])
        sib_state = joined(lambda a, b: sib_ref[a, b, 0:QUARTER, :])
        sib_grad = joined(lambda a, b: sib_ref[a, b, QUARTER : 2 * QUARTER, :])
        sib_logs = sib_ref[0, 2 * h, 2 * QUARTER : PACKED, :].astype(F32)
        sib_decay = jnp.exp(jnp.sum(sib_logs, axis=0, keepdims=True))
        s_in = (first * chip_state + second * (sib_decay * chip_state + sib_state)).astype(BF)
        g_out = (first * (sib_decay * chip_grad + sib_grad) + second * chip_grad).astype(BF)
        across = jnp.sum(
            first * (sib_grad * chip_state) + second * (chip_grad * sib_state), axis=0, keepdims=True
        )
        log_start, log_tail = cum_ref[0][:, h : h + 1], cum_ref[1][:, h : h + 1]
        y_in = jnp.exp(log_start) * nn(c_ref[...], s_in)
        dx_in = jnp.exp(log_tail) * nn(b_ref[...], g_out)
        out_ref[:, cols(h)] = (o_ref[:, cols(h)] + (y_ref[:, cols(h)] + y_in)).astype(BF)
        dxo_ref[:, cols(h)] = (dx_ref[:, cols(h)] + dx_in).astype(BF)
        dc = dc + nt(eg_ref[:, cols(h)], s_in)
        db = db + nt(xt_ref[:, cols(h)], g_out)
        gf, xf = g_ref[:, cols(h)].astype(F32), x_ref[:, cols(h)].astype(F32)
        terms = log_start * (gf * y_in) + log_tail * (xf * dx_in)
        whole = log_start[-1:, :]
        sums_ref[h : h + 1, :] += (
            jnp.sum(terms, axis=0, keepdims=True) + (whole * jnp.exp(whole)) * across
        )
    dco_ref[...] = dc.astype(BF)
    dbo_ref[...] = db.astype(BF)


def back_kernel(
    tk_ref, tv_ref, got_ref, sib_ref, o_ref, y_ref, dx_ref, xt_ref, eg_ref, db_ref, dc_ref, cum_ref, sums_in,
    b_ref, c_ref, x_ref, g_ref,
    dk_ref, dv_ref, out_ref, dxo_ref, dbo_ref, dco_ref, total_ref,
    sib_k, sib_v, acc_k, acc_v, near_k, near_v, far_k, far_v, fin_k, fin_v,
    near2_k, near2_v, far2_k, far2_v,
    back_ref, st_ref, kept, decays, logs, sums_ref, sib_sums, chip_sums, seq_sums, seq_total, dp_sums,
    send_sem, recv_sem, s1, r1, s2, r2, s3, r3, pair_sem, pair_sem2,
):
    me, x, y, core = place()
    layer = lax.axis_index("dp")
    chip = me // 2
    greet(chip, core, True)
    copies = Copies(send_sem, recv_sem)

    def dev_k(df, ds, other=False):
        c = 1 - core if other else core
        return (ring(x, df) * SIDE + ring(y, ds)) * 2 + c

    def dev_v(df, ds, other=False):
        c = 1 - core if other else core
        return (ring(x, ds) * SIDE + ring(y, df)) * 2 + c

    parts = (
        ScatterPart(copies, tk_ref, sib_k, acc_k, near_k, far_k, fin_k, near2_k, far2_k, dk_ref, x, y, True, core, dev_k),
        ScatterPart(copies, tv_ref, sib_v, acc_v, near_v, far_v, fin_v, near2_v, far2_v, dv_ref, y, x, False, core, dev_v),
    )

    def stage(name):
        for part in parts:
            getattr(part, name)()

    stage("begin")
    sums_ref[...] = sums_in[...]
    scan_states(me, got_ref, back_ref, kept, decays, logs, sums_ref)
    start, wait_states = to_peers(
        chip, core, lambda to: back_ref.at[to], st_ref.at[core, chip], s1, r1
    )
    stage("one")
    start()
    st_ref[core, chip] = back_ref[chip]
    stage("two")
    wait_states()
    pair = to_sibling(chip, core, st_ref.at[core], st_ref.at[core], pair_sem)
    pair.start()
    stage("three")
    pair.wait()
    ssm_finish(
        core, st_ref, sib_ref, o_ref, y_ref, dx_ref, xt_ref, eg_ref, db_ref, dc_ref, cum_ref,
        b_ref, c_ref, x_ref, g_ref, out_ref, dxo_ref, dbo_ref, dco_ref, sums_ref,
    )
    pair = to_sibling(chip, core, sums_ref, sib_sums, pair_sem2)
    pair.start()
    stage("four")
    pair.wait()
    chip_sums[...] = sums_ref[...] + sib_sums[...]
    start, wait_sums = to_peers(chip, core, lambda to: chip_sums, seq_sums.at[chip], s2, r2)
    start()
    seq_sums[chip] = chip_sums[...]
    stage("five")
    wait_sums()
    seq_total[...] = jnp.sum(seq_sums[...], axis=0)

    def dp_copy(r):
        to = lax.rem(layer + r, LAYERS)
        return pltpu.make_async_remote_copy(
            src_ref=seq_total, dst_ref=dp_sums.at[layer], send_sem=s3.at[r], recv_sem=r3.at[r],
            device_id={"dp": to}, device_id_type=MESH,
        )

    @pl.loop(1, LAYERS)
    def _(r):
        dp_copy(r).start()

    dp_sums[layer] = seq_total[...]
    stage("six")

    @pl.loop(1, LAYERS)
    def _(r):
        dp_copy(r).wait()

    total = jnp.sum(jnp.sum(dp_sums[...], axis=0), axis=1, keepdims=True)
    total_ref[...] = jnp.broadcast_to(total, total_ref.shape)
    copies.finish()


def back(tk, tv, got, sib, o, y, dx, xt, eg, db, dc, cum, sums, b, c, x, g):
    local, wide = x.shape
    sds = jax.ShapeDtypeStruct
    small = sds((local, HW), BF)
    dma = pltpu.SemaphoreType.DMA
    square = pltpu.VMEM((SIDE, SIDE, local, HW), BF)
    near = pltpu.VMEM((2, SIDE, local, HW), BF)
    far = pltpu.VMEM((2, SIDE, BT, HW), BF)
    fin = pltpu.VMEM((SIDE, local, HW), BF)
    near2 = pltpu.VMEM((2, local, HW), BF)
    far2 = pltpu.VMEM((2, BT, HW), BF)
    tile = pltpu.VMEM((2 * HEADS, HW), F32)
    return pl.pallas_call(
        back_kernel,
        out_shape=(
            small, small, sds((local, wide), BF), sds((local, wide), BF), small, small,
            sds((2 * HEADS, HW), F32),
        ),
        in_specs=[VM] * 17,
        out_specs=(VM,) * 7,
        scratch_shapes=[
            square, square, square, square, near, near, far, far, fin, fin,
            near2, near2, far2, far2,
            pltpu.VMEM((CHIPS, 2, QUARTER, HW), BF),
            pltpu.VMEM((2, CHIPS, 2, QUARTER, HW), BF),
            pltpu.VMEM((CHIPS, QUARTER, HW), F32),
            pltpu.VMEM((CHIPS, HW), F32),
            pltpu.VMEM((CHIPS, HW), F32),
            tile, tile, tile,
            pltpu.VMEM((CHIPS, 2 * HEADS, HW), F32),
            tile,
            pltpu.VMEM((LAYERS, 2 * HEADS, HW), F32),
            dma((SCATTER_COPIES,)), dma((SCATTER_COPIES,)),
            dma((CHIPS,)), dma((CHIPS,)), dma((CHIPS,)), dma((CHIPS,)),
            dma((LAYERS,)), dma((LAYERS,)), dma((2,)), dma((2,)),
        ],
        compiler_params=pltpu.CompilerParams(
            collective_id=2, has_side_effects=True, vmem_limit_bytes=23 << 20
        ),
        cost_estimate=pl.CostEstimate(flops=1 << 29, bytes_accessed=16 << 20, transcendentals=1 << 12),
        name="back",
    )(tk, tv, got, sib, o, y, dx, xt, eg, db, dc, cum, sums, b, c, x, g)


def emit_kernel(*refs):
    count = (len(refs) - 2) // 2
    total_ref, rate_ref = refs[count], refs[2 * count + 1]
    sem = refs[-1]
    moves = [
        pltpu.make_async_copy(refs[i], refs[count + 1 + i], sem.at[i]) for i in range(count)
    ]
    for move in moves:
        move.start()
    rate_ref[...] = total_ref[...]
    for move in moves:
        move.wait()


def emit(arrays, total):
    count = len(arrays)
    return pl.pallas_call(
        emit_kernel,
        out_shape=tuple(pltpu.HBM(a.shape, a.dtype) for a in arrays)
        + (jax.ShapeDtypeStruct(total.shape, total.dtype),),
        in_specs=[VM] * (count + 1),
        out_specs=(HB,) * count + (VM,),
        scratch_shapes=[pltpu.SemaphoreType.DMA((count,))],
        compiler_params=pltpu.CompilerParams(vmem_limit_bytes=4 << 20),
        cost_estimate=pl.CostEstimate(flops=0, bytes_accessed=3 << 20, transcendentals=0),
        name="emit",
    )(*arrays, total)


def body(query, key, value, ssm_input, in_b, in_c, step, rate_log, skip, block_mask, grad_out):
    q, k, v, x, b, c, g = (
        a[0] for a in (query, key, value, ssm_input, in_b, in_c, grad_out)
    )
    local = q.shape[0]
    fixed = [pltpu.with_memory_space_constraint(a, pltpu.HBM) for a in (k, v, x, g, b, c, step[0].T, rate_log, skip)]
    keys, values, got, sib, *local_terms = front(*fixed)
    keys, values = keys.reshape(-1, HW), values.reshape(-1, HW)
    attended, dq, terms_k, terms_v = attention(block_mask[0], q, g, keys, values)
    dk, dv, layer_out, dx, db, dc, total = back(
        terms_k, terms_v, got, sib, attended, *local_terms, b, c, x, g
    )
    layer_out, dx, dk, dv, db, dc, total = emit((layer_out, dx, dk, dv, db, dc), total)
    tokens = lax.axis_size("dp") * lax.axis_size("seq") * local
    return (
        layer_out[None],
        dq[None],
        dk[None],
        dv[None],
        dx[None],
        db[None],
        dc[None],
        total[:HEADS, 0] / tokens,
        total[HEADS:, 0] / (tokens * HW),
    )


def solution(mesh):
    row = P("dp", "seq", None)
    in_specs = (row,) * 7 + (P(), P(), P("dp", None, None), row)
    out_specs = (row,) * 7 + (P(), P())
    return jax.shard_map(body, mesh=mesh, in_specs=in_specs, out_specs=out_specs, check_vma=False)
```

```python
import functools

import jax
import jax.numpy as jnp
from jax import lax
from jax.experimental import pallas as pl
from jax.experimental.pallas import tpu as pltpu
from jax.sharding import PartitionSpec as P

HW = 128
HEADS = 8
BT = 128
MOST = 24
WIDE = 8
NARROW = 4
FACTOR = HW ** (-0.5)
LOG2E = 1.4426950408889634
BF = jnp.bfloat16
F32 = jnp.float32
MESH = pl.DeviceIdType.MESH
HIGH = lax.Precision.HIGHEST

VM = pl.BlockSpec(memory_space=pltpu.VMEM)
HB = pl.BlockSpec(memory_space=pltpu.HBM)
SM = pl.BlockSpec(memory_space=pltpu.SMEM)


def nn(a, b):
    return lax.dot_general(a, b, (((1,), (0,)), ((), ())), preferred_element_type=F32)


def nt(a, b):
    return lax.dot_general(a, b, (((1,), (1,)), ((), ())), preferred_element_type=F32)


def tn(a, b):
    return lax.dot_general(a, b, (((0,), (0,)), ((), ())), preferred_element_type=F32)


def cols(h):
    return pl.ds(h * HW, HW)


def attention_kernel(
    mask_ref, q_ref, g_ref, k_ref, v_ref,
    o_ref, dq_ref, tk_ref, tv_ref,
    s_buf, acc_k, acc_v, qs, gs, g_t, o_t, dq_t, picked,
):
    total_blocks = mask_ref.shape[1]
    seq_at = lax.axis_index("seq")
    per_device = q_ref.shape[0] // BT
    acc_k[...] = jnp.zeros_like(acc_k)
    acc_v[...] = jnp.zeros_like(acc_v)

    @pl.loop(0, per_device)
    def _(block):
        row = seq_at * per_device + block

        def note(j, n):
            picked[n] = j
            return n + mask_ref[row, j]

        count = lax.fori_loop(0, total_blocks, note, jnp.int32(0), unroll=8)
        for i in range(WIDE - 1):
            picked[count + i] = picked[0]
        rest = lax.rem(count, WIDE)
        wide = count // WIDE + (rest > NARROW).astype(jnp.int32)
        narrow = jnp.logical_and(rest > 0, rest <= NARROW).astype(jnp.int32)
        rows = pl.ds(pl.multiple_of(block * BT, BT), BT)
        for h in range(HEADS):
            qs[cols(h), :] = q_ref[rows, cols(h)]
            g_head = g_ref[rows, cols(h)]
            gs[cols(h), :] = g_head
            g_t[:, cols(h)] = g_head.astype(F32).T

        def starts(at, size):
            return tuple(pl.multiple_of(picked[at + i] * BT, BT) for i in range(size))

        def group_of(ref, at, size):
            return jnp.concatenate([ref[pl.ds(first, BT), :] for first in starts(at, size)], axis=0)

        def over_groups(step, carry):
            carry = lax.fori_loop(0, wide, lambda p, c: step(p * WIDE, WIDE, c), carry)
            return lax.fori_loop(0, narrow, lambda p, c: step(wide * WIDE, NARROW, c), carry)

        def flat(value):
            return value.reshape(-1, value.shape[-1])

        def score_step(at, size, top):
            s = nt(group_of(k_ref, at, size), qs[...])
            parts = [s[:BT]]
            for i in range(1, size):
                bias = jnp.where(at + i < count, 0.0, -1e30).astype(F32)
                parts.append(s[i * BT : (i + 1) * BT] + bias)
            s = jnp.concatenate(parts, axis=0)
            s_buf[pl.ds(at, size)] = s.reshape(size, BT, -1)
            return jnp.maximum(top, jnp.max(s.reshape(-1, 8, s.shape[1]), axis=0))

        top = over_groups(score_step, jnp.full((8, HEADS * BT), -3e38, F32))
        top = jnp.max(top, axis=0, keepdims=True)
        o_t[...] = jnp.zeros_like(o_t)

        def weight_step(at, size, total):
            w = jnp.exp2((flat(s_buf[pl.ds(at, size)]) - top) * (FACTOR * LOG2E))
            s_buf[pl.ds(at, size)] = w.reshape(size, BT, -1)
            o_t[...] += tn(group_of(v_ref, at, size), w.astype(BF))
            return total + jnp.sum(w.reshape(-1, 8, w.shape[1]), axis=0)

        total = over_groups(weight_step, jnp.zeros((8, HEADS * BT), F32))
        inverse = 1.0 / jnp.sum(total, axis=0, keepdims=True)
        o_t[...] = o_t[...] * inverse
        delta = jnp.sum(o_t[...] * g_t[...], axis=0, keepdims=True)
        for h in range(HEADS):
            o_ref[rows, cols(h)] = o_t[:, cols(h)].T
        dq_t[...] = jnp.zeros_like(dq_t)

        def gradient_step(at, size, carry):
            probs = flat(s_buf[pl.ds(at, size)]) * inverse
            dprobs = nt(group_of(v_ref, at, size), gs[...])
            ds = (probs * (dprobs - delta)).astype(BF)
            dq_t[...] += tn(group_of(k_ref, at, size), ds)
            dk = nn(ds, qs[...])
            dv = nn(probs.astype(BF), gs[...])
            for i, first in enumerate(starts(at, size)):
                here = pl.ds(first, BT)
                acc_k[here, :] += dk[i * BT : (i + 1) * BT]
                acc_v[here, :] += dv[i * BT : (i + 1) * BT]
            return carry

        over_groups(gradient_step, 0)
        for h in range(HEADS):
            dq_ref[rows, cols(h)] = (dq_t[:, cols(h)] * FACTOR).T.astype(BF)

    @pl.loop(0, total_blocks, unroll=4)
    def _(j):
        here = pl.ds(pl.multiple_of(j * BT, BT), BT)
        chip = j // 4
        at = (
            lax.rem(j // 2, 2), chip // SIDE, lax.rem(chip, SIDE),
            pl.ds(pl.multiple_of(lax.rem(j, 2) * BT, BT), BT),
        )
        tk_ref[at] = (acc_k[here, :] * FACTOR).astype(BF)
        tv_ref[at] = acc_v[here, :].astype(BF)


def attention(mask, q, g, keys, values):
    local, wide = q.shape
    total = keys.shape[0]
    width = HEADS * BT
    return pl.pallas_call(
        attention_kernel,
        out_shape=(
            jax.ShapeDtypeStruct((local, wide), F32),
            jax.ShapeDtypeStruct((local, wide), BF),
            jax.ShapeDtypeStruct((2, SIDE, SIDE, local, HW), BF),
            jax.ShapeDtypeStruct((2, SIDE, SIDE, local, HW), BF),
        ),
        in_specs=[SM, VM, VM, VM, VM],
        out_specs=(VM, VM, VM, VM),
        scratch_shapes=[
            pltpu.VMEM((MOST, BT, width), F32),
            pltpu.VMEM((total, HW), F32),
            pltpu.VMEM((total, HW), F32),
            pltpu.VMEM((width, HW), BF),
            pltpu.VMEM((width, HW), BF),
            pltpu.VMEM((HW, width), F32),
            pltpu.VMEM((HW, width), F32),
            pltpu.VMEM((HW, width), F32),
            pltpu.SMEM((total // BT + 8,), jnp.int32),
        ],
        compiler_params=pltpu.CompilerParams(vmem_limit_bytes=38 << 20),
        cost_estimate=pl.CostEstimate(
            flops=12 * 24 * 1024 * 128 * 128 * 2, bytes_accessed=12 << 20, transcendentals=1 << 22
        ),
        name="attention",
    )(mask, q, g, keys, values)


SIDE = 4
CHIPS = SIDE * SIDE
PEERS = 2 * CHIPS
LAYERS = 8
QUARTER = 32
LOG_ROWS = 16
PACKED = 2 * QUARTER + LOG_ROWS


def place():
    me = lax.axis_index("seq")
    core = lax.rem(me, 2)
    chip = me // 2
    return me, chip // SIDE, lax.rem(chip, SIDE), core


def ring(a, step):
    return lax.rem(a + step + SIDE, SIDE)


def greet(chip, core, also_dp, between=None):
    barrier = pltpu.get_barrier_semaphore()

    @pl.loop(1, CHIPS)
    def _(r):
        to = lax.rem(chip + r, CHIPS) * 2 + core
        pl.semaphore_signal(barrier, inc=1, device_id={"seq": to}, device_id_type=MESH)

    pl.semaphore_signal(
        barrier, inc=1, device_id={"seq": chip * 2 + 1 - core}, device_id_type=MESH
    )
    waits = CHIPS
    if also_dp:
        layer = lax.axis_index("dp")

        @pl.loop(1, LAYERS)
        def _(r):
            to = lax.rem(layer + r, LAYERS)
            pl.semaphore_signal(barrier, inc=1, device_id={"dp": to}, device_id_type=MESH)

        waits += LAYERS - 1
    if between is not None:
        between()
    pl.semaphore_wait(barrier, waits)


def to_peers(chip, core, src, dst, send_sem, recv_sem):
    def copy(r):
        to = lax.rem(chip + r, CHIPS)
        return pltpu.make_async_remote_copy(
            src_ref=src(to), dst_ref=dst, send_sem=send_sem.at[r], recv_sem=recv_sem.at[r],
            device_id={"seq": to * 2 + core}, device_id_type=MESH,
        )

    def start():
        @pl.loop(1, CHIPS)
        def _(r):
            copy(r).start()

    def wait():
        @pl.loop(1, CHIPS)
        def _(r):
            copy(r).wait()

    return start, wait


def to_sibling(chip, core, src, dst, sems):
    return pltpu.make_async_remote_copy(
        src_ref=src, dst_ref=dst, send_sem=sems.at[0], recv_sem=sems.at[1],
        device_id={"seq": chip * 2 + 1 - core}, device_id_type=MESH,
    )


class Copies:
    def __init__(self, send_sem, recv_sem):
        self.send_sem, self.recv_sem, self.made = send_sem, recv_sem, []

    def start(self, src, dst, device):
        at = len(self.made)
        copy = pltpu.make_async_remote_copy(
            src_ref=src, dst_ref=dst, send_sem=self.send_sem.at[at], recv_sem=self.recv_sem.at[at],
            device_id={"seq": device}, device_id_type=MESH,
        )
        copy.start()
        self.made.append(copy)
        return copy

    def finish(self):
        for copy in self.made:
            copy.wait_send()


LOW, UP = pl.ds(0, BT), pl.ds(BT, BT)
GATHER_COPIES = 2 * (22 + 16)


class GatherPart:
    def __init__(self, copies, own, out, first, second, at, core):
        self.c, self.own, self.out = copies, own, out
        self.f, self.s, self.at, self.core = first, second, at, core

    def dev(self, df, ds, other=False):
        core = 1 - self.core if other else self.core
        return self.at(ring(self.f, df), ring(self.s, ds)) * 2 + core

    def block(self, df, ds):
        return self.out.at[self.dev(df, ds)]

    def sibling(self, df, ds, src=None):
        here = self.block(df, ds)
        return self.c.start(here if src is None else src, here, self.dev(0, 0, True))

    def begin(self):
        mine = self.block(0, 0)
        self.a_up = self.c.start(self.own, mine, self.dev(1, 0))
        self.a_down = self.c.start(self.own, mine, self.dev(-1, 0))
        self.col = {0: self.column(0, self.own)}
        self.sib = [self.sibling(0, 0, self.own)]

    def column(self, df, src=None):
        here = self.block(df, 0)
        src = here if src is None else src
        return self.c.start(src, here, self.dev(0, 1)), self.c.start(src, here, self.dev(0, -1))

    def near(self):
        self.a_up.wait_recv()
        here = self.block(-1, 0)
        self.b_up = self.c.start(here.at[LOW], here.at[LOW], self.dev(1, 0))
        self.col[-1] = self.column(-1)
        self.sib.append(self.sibling(-1, 0))
        self.a_down.wait_recv()
        here = self.block(1, 0)
        self.b_down = self.c.start(here.at[UP], here.at[UP], self.dev(-1, 0))
        self.col[1] = self.column(1)
        self.sib.append(self.sibling(1, 0))
        self.last = []

    def pass_on(self, df):
        up, down = self.col[df]
        up.wait_recv()
        here = self.block(df, -1)
        one = self.c.start(here.at[LOW], here.at[LOW], self.dev(0, 1))
        self.sib.append(self.sibling(df, -1))
        down.wait_recv()
        here = self.block(df, 1)
        two = self.c.start(here.at[UP], here.at[UP], self.dev(0, -1))
        self.sib.append(self.sibling(df, 1))
        self.last.append((df, one, two))

    def far(self):
        self.b_up.wait_recv()
        self.b_down.wait_recv()
        self.col[2] = self.column(2)
        self.sib.append(self.sibling(2, 0))

    def end(self, i):
        df, one, two = self.last[i]
        one.wait_recv()
        two.wait_recv()
        self.sib.append(self.sibling(df, 2))


def ssm_prepare(x_ref, step_ref, rate_ref, b_ref, c_ref, cum_ref, dl, bt_ref, ct_ref, sums):
    lanes = lax.broadcasted_iota(jnp.int32, (BT, BT), 1)
    subs = lax.broadcasted_iota(jnp.int32, (BT, BT), 0)
    upper = (subs <= lanes).astype(F32)
    dl[...] = jnp.zeros_like(dl)
    for h in range(HEADS):
        rate = jnp.exp(jnp.full((1, 1), rate_ref[h], F32))
        dl[h : h + 1, :] = -step_ref[h : h + 1, :] * rate
    run_t = []
    for i in range(2):
        run_t.append(
            lax.dot_general(
                dl[:, i * BT : (i + 1) * BT], upper, (((1,), (0,)), ((), ())),
                precision=HIGH, preferred_element_type=F32,
            )
        )
    run0, run1 = run_t[0].T, run_t[1].T
    end0, end1 = run0[BT - 1 : BT, :], run1[BT - 1 : BT, :]
    cum_ref[0] = jnp.concatenate([run0, run1 + end0], axis=0)
    cum_ref[1] = jnp.concatenate([end0 - run0 + end1, end1 - run1], axis=0)
    bt_ref[...] = b_ref[...].T
    ct_ref[...] = c_ref[...].T
    for total in sums:
        total[...] = jnp.zeros_like(total)
    b0, b1 = b_ref[0:BT, :], b_ref[BT : 2 * BT, :]
    c0, c1 = c_ref[0:BT, :], c_ref[BT : 2 * BT, :]
    return run0, run1, run_t[0], run_t[1], end0, end1, nt(c0, b0), nt(c1, b1), nt(c1, b0)


def split3(value):
    rows = lax.broadcasted_iota(jnp.int32, (LOG_ROWS, HW), 0)
    hi = value.astype(BF).astype(F32)
    mid = (value - hi).astype(BF).astype(F32)
    low = value - hi - mid
    out = jnp.where(rows == 0, hi, jnp.where(rows == 1, mid, jnp.where(rows == 2, low, 0.0)))
    return out.astype(BF)


def ssm_head(
    h, ready, x_ref, g_ref, skip_ref, cum_ref, bt_ref, ct_ref, sums,
    y_ref, dx_ref, xt_ref, eg_ref, send_ref, sums_ref,
):
    run0, run1, run0_t, run1_t, end0, end1, cb00, cb11, cb10 = ready
    sum00, sum11, sum10 = sums
    lanes = lax.broadcasted_iota(jnp.int32, (BT, BT), 1)
    subs = lax.broadcasted_iota(jnp.int32, (BT, BT), 0)
    lower = subs >= lanes
    x0, x1 = x_ref[0:BT, cols(h)], x_ref[BT : 2 * BT, cols(h)]
    g0, g1 = g_ref[0:BT, cols(h)], g_ref[BT : 2 * BT, cols(h)]
    gain = skip_ref[h]
    col0, col1 = run0[:, h : h + 1], run1[:, h : h + 1]
    row0, row1 = run0_t[h : h + 1, :], run1_t[h : h + 1, :]
    last0, last1 = end0[:, h : h + 1], end1[:, h : h + 1]

    def part(spread, cb, xs, gs, total, diagonal):
        if diagonal:
            decay = jnp.where(lower, jnp.exp(jnp.where(lower, spread, 0.0)), 0.0)
        else:
            decay = jnp.exp(spread)
        mixed = decay * cb
        outer = nt(gs, xs)
        total[...] += decay * outer
        terms = spread * (mixed * outer)
        mixed = mixed.astype(BF)
        return nn(mixed, xs), tn(mixed, gs), jnp.sum(terms, axis=0, keepdims=True)

    y00, dx00, r00 = part(col0 - row0, cb00, x0, g0, sum00, True)
    y11, dx11, r11 = part(col1 - row1, cb11, x1, g1, sum11, True)
    y10, dx10, r10 = part(col1 + (last0 - row0), cb10, x0, g1, sum10, False)
    xf0, xf1, gf0, gf1 = x0.astype(F32), x1.astype(F32), g0.astype(F32), g1.astype(F32)
    sums_ref[h : h + 1, :] = r00 + r11 + r10
    sums_ref[HEADS + h : HEADS + h + 1, :] = jnp.sum(xf0 * gf0 + xf1 * gf1, axis=0, keepdims=True)
    y_ref[0:BT, cols(h)] = y00 + gain * xf0
    y_ref[BT : 2 * BT, cols(h)] = y11 + y10 + gain * xf1
    dx_ref[0:BT, cols(h)] = dx00 + dx10 + gain * gf0
    dx_ref[BT : 2 * BT, cols(h)] = dx11 + gain * gf1
    start = jnp.exp(cum_ref[0][:, h : h + 1])
    tail = jnp.exp(cum_ref[1][:, h : h + 1])

    def state(turned, scaled, keep_ref):
        high = scaled.astype(BF)
        keep_ref[:, cols(h)] = high
        low = (scaled - high.astype(F32)).astype(BF)
        return (nn(turned, high) + nn(turned, low)).astype(BF)

    end_state = state(bt_ref[...], tail * jnp.concatenate([xf0, xf1], axis=0), xt_ref)
    start_grad = state(ct_ref[...], start * jnp.concatenate([gf0, gf1], axis=0), eg_ref)
    logs = split3(last0 + last1)
    for i in range(4):
        at = slice(i * QUARTER, (i + 1) * QUARTER)
        to = send_ref.at[(h * 4 + i) % 2, (h * 4 + i) // 2]
        to[0:QUARTER, :] = end_state[at]
        to[QUARTER : 2 * QUARTER, :] = start_grad[at]
        to[2 * QUARTER : PACKED, :] = logs


def ssm_end(b_ref, c_ref, sums, db_ref, dc_ref):
    s00, s11, s10 = (total[...].astype(BF) for total in sums)
    b0, b1 = b_ref[0:BT, :], b_ref[BT : 2 * BT, :]
    c0, c1 = c_ref[0:BT, :], c_ref[BT : 2 * BT, :]
    dc_ref[0:BT, :] = nn(s00, b0)
    dc_ref[BT : 2 * BT, :] = nn(s11, b1) + nn(s10, b0)
    db_ref[0:BT, :] = tn(s00, c0) + tn(s10, c1)
    db_ref[BT : 2 * BT, :] = tn(s11, c1)


def combine(core, send_ref, sib_ref, comb_ref):
    first = (core == 0).astype(F32)
    second = 1.0 - first
    for h in range(HEADS):
        at = pl.ds(2 * h, 2)
        mine, other = send_ref[core, at].astype(F32), sib_ref[core, at].astype(F32)
        log_mine = jnp.sum(mine[0, 2 * QUARTER :], axis=0, keepdims=True)
        log_other = jnp.sum(other[0, 2 * QUARTER :], axis=0, keepdims=True)
        by_mine, by_other = jnp.exp(log_mine), jnp.exp(log_other)
        ends = slice(0, QUARTER)
        comb_ref[at, ends, :] = (
            (first * by_other + second) * mine[:, ends] + (first + second * by_mine) * other[:, ends]
        ).astype(BF)
        grads = slice(QUARTER, 2 * QUARTER)
        comb_ref[at, grads, :] = (
            (first + second * by_other) * mine[:, grads] + (first * by_mine + second) * other[:, grads]
        ).astype(BF)
        logs = split3(log_mine + log_other)
        for i in range(2):
            comb_ref[2 * h + i, 2 * QUARTER : PACKED, :] = logs


def front_kernel(
    k_hbm, v_hbm, x_hbm, g_hbm, b_hbm, c_hbm, step_hbm, rate_hbm, skip_hbm,
    ko_ref, vo_ref, got_ref, sib_ref, y_ref, dx_ref, xt_ref, eg_ref, db_ref, dc_ref, cum_ref, sums_ref,
    x_ref, g_ref, b_ref, c_ref, step_ref, rate_ref, skip_ref, send_ref, comb_ref, dl, bt_ref, ct_ref, sum00, sum11, sum10,
    send_sem, recv_sem, own_sem, s1, r1, pair_sem,
):
    me, x, y, core = place()
    sources = (x_hbm, g_hbm, b_hbm, c_hbm, step_hbm, rate_hbm, skip_hbm)
    targets = (x_ref, g_ref, b_ref, c_ref, step_ref, rate_ref, skip_ref)
    loads = [
        pltpu.make_async_copy(src, dst, own_sem.at[i])
        for i, (src, dst) in enumerate(zip(sources, targets))
    ]
    for copy in loads:
        copy.start()
    chip = me // 2
    greet(chip, core, False)
    copies = Copies(send_sem, recv_sem)
    parts = (
        GatherPart(copies, k_hbm, ko_ref, x, y, lambda f, s: f * SIDE + s, core),
        GatherPart(copies, v_hbm, vo_ref, y, x, lambda f, s: s * SIDE + f, core),
    )
    for part in parts:
        part.begin()
    own = [
        pltpu.make_async_copy(k_hbm, ko_ref.at[me], own_sem.at[7]),
        pltpu.make_async_copy(v_hbm, vo_ref.at[me], own_sem.at[8]),
    ]
    for copy in own:
        copy.start()
    for copy in loads:
        copy.wait()

    def all_parts(name, *args):
        return lambda: [getattr(part, name)(*args) for part in parts]

    stages = {
        1: all_parts("near"), 3: all_parts("pass_on", 0), 5: all_parts("far"),
    }
    sums = (sum00, sum11, sum10)
    ready = ssm_prepare(x_ref, step_ref, rate_ref, b_ref, c_ref, cum_ref, dl, bt_ref, ct_ref, sums)
    for h in range(HEADS):
        ssm_head(
            h, ready, x_ref, g_ref, skip_ref, cum_ref, bt_ref, ct_ref, sums,
            y_ref, dx_ref, xt_ref, eg_ref, send_ref, sums_ref,
        )
        if h in stages:
            stages[h]()
    pair = to_sibling(chip, core, send_ref, sib_ref, pair_sem)
    pair.start()
    for part in parts:
        part.pass_on(-1)
    ssm_end(b_ref, c_ref, sums, db_ref, dc_ref)
    pair.wait()
    combine(core, send_ref, sib_ref, comb_ref)
    start, wait = to_peers(chip, core, lambda to: comb_ref.at[to], got_ref.at[chip], s1, r1)
    start()
    got_ref[chip] = comb_ref[chip]
    for df in (1, 2):
        for part in parts:
            part.pass_on(df)
    for i in range(4):
        for part in parts:
            part.end(i)
    for copy in own:
        copy.wait()
    for part in parts:
        for copy in part.sib:
            copy.wait_recv()
    copies.finish()
    wait()


def front(k, v, x, g, b, c, step_t, rate_log, skip):
    local, wide = x.shape
    sds = jax.ShapeDtypeStruct
    full = sds((PEERS, local, HW), BF)
    dma = pltpu.SemaphoreType.DMA
    return pl.pallas_call(
        front_kernel,
        out_shape=(
            full,
            full,
            sds((CHIPS, PACKED, HW), BF),
            sds((2, CHIPS, PACKED, HW), BF),
            sds((local, wide), F32),
            sds((local, wide), F32),
            sds((local, wide), BF),
            sds((local, wide), BF),
            sds((local, HW), F32),
            sds((local, HW), F32),
            sds((2, local, HW), F32),
            sds((2 * HEADS, HW), F32),
        ),
        in_specs=[HB] * 9,
        out_specs=(VM,) * 12,
        scratch_shapes=[
            pltpu.VMEM((local, wide), BF),
            pltpu.VMEM((local, wide), BF),
            pltpu.VMEM((local, HW), BF),
            pltpu.VMEM((local, HW), BF),
            pltpu.VMEM((HEADS, local), F32),
            pltpu.SMEM((HEADS,), F32),
            pltpu.SMEM((HEADS,), F32),
            pltpu.VMEM((2, CHIPS, PACKED, HW), BF),
            pltpu.VMEM((CHIPS, PACKED, HW), BF),
            pltpu.VMEM((HW, local), F32),
            pltpu.VMEM((HW, local), BF),
            pltpu.VMEM((HW, local), BF),
            pltpu.VMEM((BT, BT), F32),
            pltpu.VMEM((BT, BT), F32),
            pltpu.VMEM((BT, BT), F32),
            dma((GATHER_COPIES,)),
            dma((GATHER_COPIES,)),
            dma((9,)),
            dma((CHIPS,)),
            dma((CHIPS,)),
            dma((2,)),
        ],
        compiler_params=pltpu.CompilerParams(
            collective_id=1, has_side_effects=True, vmem_limit_bytes=14 << 20
        ),
        cost_estimate=pl.CostEstimate(flops=1 << 30, bytes_accessed=16 << 20, transcendentals=1 << 19),
        name="front",
    )(k, v, x, g, b, c, step_t, rate_log, skip)


SCATTER_COPIES = 2 * 16


class ScatterPart:
    def __init__(self, copies, terms, sib, acc, near, far, fin, near2, far2, out, first, second, x_first, core, dev):
        self.c, self.terms, self.sib, self.acc = copies, terms, sib, acc
        self.near, self.far, self.fin, self.near2, self.far2, self.out = near, far, fin, near2, far2, out
        self.f, self.s, self.x_first, self.core, self.dev = first, second, x_first, core, dev

    def chunk(self, ref, ds, core=None):
        s = ring(self.s, ds)
        ref = ref if core is None else ref.at[core]
        return ref.at[:, s] if self.x_first else ref.at[s]

    def begin(self):
        self.sibs = {}
        for ds in (2, 1, -1, 0):
            self.sibs[ds] = self.c.start(
                self.chunk(self.terms, ds, 1 - self.core), self.chunk(self.sib, ds), self.dev(0, 0, True)
            )

    def own(self, ds, rows):
        mine = self.chunk(self.terms, ds, self.core)[:, rows, :].astype(F32)
        return mine + self.chunk(self.sib, ds)[:, rows, :].astype(F32)

    def put(self, ds, rows, extra=None):
        value = self.own(ds, rows)
        if extra is not None:
            value = value + extra.astype(F32)
        self.chunk(self.acc, ds)[:, rows, :] = value.astype(BF)

    def one(self):
        self.sibs[2].wait_recv()
        for rows in (LOW, UP):
            self.put(2, rows)
        here = self.chunk(self.acc, 2)
        self.far_up = self.c.start(here.at[:, LOW], self.far.at[0], self.dev(0, 1))
        self.far_down = self.c.start(here.at[:, UP], self.far.at[1], self.dev(0, -1))

    def two(self):
        self.sibs[1].wait_recv()
        self.put(1, UP)
        self.up_a = self.c.start(
            self.chunk(self.acc, 1).at[:, UP], self.near.at[0, :, UP], self.dev(0, 1)
        )
        self.sibs[-1].wait_recv()
        self.put(-1, LOW)
        self.down_a = self.c.start(
            self.chunk(self.acc, -1).at[:, LOW], self.near.at[1, :, LOW], self.dev(0, -1)
        )

    def three(self):
        self.far_up.wait_recv()
        self.put(1, LOW, self.far[0])
        self.up_b = self.c.start(
            self.chunk(self.acc, 1).at[:, LOW], self.near.at[0, :, LOW], self.dev(0, 1)
        )
        self.far_down.wait_recv()
        self.put(-1, UP, self.far[1])
        self.down_b = self.c.start(
            self.chunk(self.acc, -1).at[:, UP], self.near.at[1, :, UP], self.dev(0, -1)
        )

    def four(self):
        self.sibs[0].wait_recv()
        for copy in (self.up_a, self.down_a, self.up_b, self.down_b):
            copy.wait_recv()
        for rows in (LOW, UP):
            total = self.own(0, rows) + self.near[0, :, rows, :].astype(F32) + self.near[1, :, rows, :].astype(F32)
            self.fin[:, rows, :] = total.astype(BF)
        here = self.fin.at[ring(self.f, 2)]
        self.far_up = self.c.start(here.at[LOW], self.far2.at[0], self.dev(1, 0))
        self.far_down = self.c.start(here.at[UP], self.far2.at[1], self.dev(-1, 0))
        self.up_a = self.c.start(
            self.fin.at[ring(self.f, 1)].at[UP], self.near2.at[0, UP], self.dev(1, 0)
        )
        self.down_a = self.c.start(
            self.fin.at[ring(self.f, -1)].at[LOW], self.near2.at[1, LOW], self.dev(-1, 0)
        )

    def five(self):
        self.far_up.wait_recv()
        here = self.fin.at[ring(self.f, 1)]
        here[LOW, :] = (here[LOW, :].astype(F32) + self.far2[0].astype(F32)).astype(BF)
        self.up_b = self.c.start(here.at[LOW], self.near2.at[0, LOW], self.dev(1, 0))
        self.far_down.wait_recv()
        here = self.fin.at[ring(self.f, -1)]
        here[UP, :] = (here[UP, :].astype(F32) + self.far2[1].astype(F32)).astype(BF)
        self.down_b = self.c.start(here.at[UP], self.near2.at[1, UP], self.dev(-1, 0))

    def six(self):
        for copy in (self.up_a, self.down_a, self.up_b, self.down_b):
            copy.wait_recv()
        mine = self.fin.at[self.f][...].astype(F32)
        self.out[...] = (mine + self.near2[0].astype(F32) + self.near2[1].astype(F32)).astype(BF)


def scan_states(me, got_ref, back_ref, kept, decays, logs, sums_ref):
    log_sum = jnp.sum(got_ref[:, 2 * QUARTER : PACKED, :].astype(F32), axis=1)
    logs[...] = log_sum
    decays[...] = jnp.exp(log_sum)

    def forward(d, state):
        kept[d] = state
        back_ref[d, 0] = state.astype(BF)
        return decays[pl.ds(d, 1), :] * state + got_ref[d, 0:QUARTER, :].astype(F32)

    def backward(k, carry):
        grad, rate = carry
        d = CHIPS - 1 - k
        back_ref[d, 1] = grad.astype(BF)
        decay = decays[pl.ds(d, 1), :]
        rate = rate + (logs[pl.ds(d, 1), :] * decay) * (kept[d] * grad)
        return decay * grad + got_ref[d, QUARTER : 2 * QUARTER, :].astype(F32), rate

    zero = jnp.zeros((QUARTER, HW), F32)
    lax.fori_loop(0, CHIPS, forward, zero)
    _, rate = lax.fori_loop(0, CHIPS, backward, (zero, zero))
    rate = jnp.sum(rate, axis=0, keepdims=True)
    rows = lax.broadcasted_iota(jnp.int32, (2 * HEADS, HW), 0)
    sums_ref[...] += jnp.where(rows == me // 4, rate, 0.0)


def ssm_finish(
    core, st_ref, sib_ref, o_ref, y_ref, dx_ref, xt_ref, eg_ref, db_ref, dc_ref, cum_ref,
    b_ref, c_ref, x_ref, g_ref, out_ref, dxo_ref, dbo_ref, dco_ref, sums_ref,
):
    dc = dc_ref[...]
    db = db_ref[...]
    first = (core == 0).astype(F32)
    second = 1.0 - first
    for h in range(HEADS):
        owners = [((h * 4 + i) % 2, (h * 4 + i) // 2) for i in range(4)]

        def joined(pick):
            return jnp.concatenate([pick(*at) for at in owners], axis=0).astype(F32)

        chip_state = joined(lambda a, b: st_ref[a, b, 0])
        chip_grad = joined(lambda a, b: st_ref[a, b, 1])
        sib_state = joined(lambda a, b: sib_ref[a, b, 0:QUARTER, :])
        sib_grad = joined(lambda a, b: sib_ref[a, b, QUARTER : 2 * QUARTER, :])
        sib_logs = sib_ref[0, 2 * h, 2 * QUARTER : PACKED, :].astype(F32)
        sib_decay = jnp.exp(jnp.sum(sib_logs, axis=0, keepdims=True))
        s_in = (first * chip_state + second * (sib_decay * chip_state + sib_state)).astype(BF)
        g_out = (first * (sib_decay * chip_grad + sib_grad) + second * chip_grad).astype(BF)
        across = jnp.sum(
            first * (sib_grad * chip_state) + second * (chip_grad * sib_state), axis=0, keepdims=True
        )
        log_start, log_tail = cum_ref[0][:, h : h + 1], cum_ref[1][:, h : h + 1]
        y_in = jnp.exp(log_start) * nn(c_ref[...], s_in)
        dx_in = jnp.exp(log_tail) * nn(b_ref[...], g_out)
        out_ref[:, cols(h)] = (o_ref[:, cols(h)] + (y_ref[:, cols(h)] + y_in)).astype(BF)
        dxo_ref[:, cols(h)] = (dx_ref[:, cols(h)] + dx_in).astype(BF)
        dc = dc + nt(eg_ref[:, cols(h)], s_in)
        db = db + nt(xt_ref[:, cols(h)], g_out)
        gf, xf = g_ref[:, cols(h)].astype(F32), x_ref[:, cols(h)].astype(F32)
        terms = log_start * (gf * y_in) + log_tail * (xf * dx_in)
        whole = log_start[-1:, :]
        sums_ref[h : h + 1, :] += (
            jnp.sum(terms, axis=0, keepdims=True) + (whole * jnp.exp(whole)) * across
        )
    dco_ref[...] = dc.astype(BF)
    dbo_ref[...] = db.astype(BF)


def back_kernel(
    tk_ref, tv_ref, got_ref, sib_ref, o_ref, y_ref, dx_ref, xt_ref, eg_ref, db_ref, dc_ref, cum_ref, sums_in,
    b_ref, c_ref, x_ref, g_ref,
    dk_ref, dv_ref, out_ref, dxo_ref, dbo_ref, dco_ref, total_ref,
    sib_k, sib_v, acc_k, acc_v, near_k, near_v, far_k, far_v, fin_k, fin_v,
    near2_k, near2_v, far2_k, far2_v,
    back_ref, st_ref, kept, decays, logs, sums_ref, sib_sums, chip_sums, seq_sums, seq_total, dp_sums,
    send_sem, recv_sem, s1, r1, s2, r2, s3, r3, pair_sem, pair_sem2,
):
    me, x, y, core = place()
    layer = lax.axis_index("dp")
    chip = me // 2

    def local_scan():
        sums_ref[...] = sums_in[...]
        scan_states(me, got_ref, back_ref, kept, decays, logs, sums_ref)

    greet(chip, core, True, local_scan)
    copies = Copies(send_sem, recv_sem)

    def dev_k(df, ds, other=False):
        c = 1 - core if other else core
        return (ring(x, df) * SIDE + ring(y, ds)) * 2 + c

    def dev_v(df, ds, other=False):
        c = 1 - core if other else core
        return (ring(x, ds) * SIDE + ring(y, df)) * 2 + c

    parts = (
        ScatterPart(copies, tk_ref, sib_k, acc_k, near_k, far_k, fin_k, near2_k, far2_k, dk_ref, x, y, True, core, dev_k),
        ScatterPart(copies, tv_ref, sib_v, acc_v, near_v, far_v, fin_v, near2_v, far2_v, dv_ref, y, x, False, core, dev_v),
    )

    def stage(name):
        for part in parts:
            getattr(part, name)()

    stage("begin")
    start, wait_states = to_peers(
        chip, core, lambda to: back_ref.at[to], st_ref.at[core, chip], s1, r1
    )
    stage("one")
    start()
    st_ref[core, chip] = back_ref[chip]
    stage("two")
    wait_states()
    pair = to_sibling(chip, core, st_ref.at[core], st_ref.at[core], pair_sem)
    pair.start()
    stage("three")
    pair.wait()
    ssm_finish(
        core, st_ref, sib_ref, o_ref, y_ref, dx_ref, xt_ref, eg_ref, db_ref, dc_ref, cum_ref,
        b_ref, c_ref, x_ref, g_ref, out_ref, dxo_ref, dbo_ref, dco_ref, sums_ref,
    )
    pair = to_sibling(chip, core, sums_ref, sib_sums, pair_sem2)
    pair.start()
    stage("four")
    pair.wait()
    chip_sums[...] = sums_ref[...] + sib_sums[...]
    start, wait_sums = to_peers(chip, core, lambda to: chip_sums, seq_sums.at[chip], s2, r2)
    start()
    seq_sums[chip] = chip_sums[...]
    stage("five")
    wait_sums()
    seq_total[...] = jnp.sum(seq_sums[...], axis=0)

    def dp_copy(r):
        to = lax.rem(layer + r, LAYERS)
        return pltpu.make_async_remote_copy(
            src_ref=seq_total, dst_ref=dp_sums.at[layer], send_sem=s3.at[r], recv_sem=r3.at[r],
            device_id={"dp": to}, device_id_type=MESH,
        )

    @pl.loop(1, LAYERS)
    def _(r):
        dp_copy(r).start()

    dp_sums[layer] = seq_total[...]
    stage("six")

    @pl.loop(1, LAYERS)
    def _(r):
        dp_copy(r).wait()

    total = jnp.sum(jnp.sum(dp_sums[...], axis=0), axis=1, keepdims=True)
    total_ref[...] = jnp.broadcast_to(total, total_ref.shape)
    copies.finish()


def back(tk, tv, got, sib, o, y, dx, xt, eg, db, dc, cum, sums, b, c, x, g):
    local, wide = x.shape
    sds = jax.ShapeDtypeStruct
    small = sds((local, HW), BF)
    dma = pltpu.SemaphoreType.DMA
    square = pltpu.VMEM((SIDE, SIDE, local, HW), BF)
    near = pltpu.VMEM((2, SIDE, local, HW), BF)
    far = pltpu.VMEM((2, SIDE, BT, HW), BF)
    fin = pltpu.VMEM((SIDE, local, HW), BF)
    near2 = pltpu.VMEM((2, local, HW), BF)
    far2 = pltpu.VMEM((2, BT, HW), BF)
    tile = pltpu.VMEM((2 * HEADS, HW), F32)
    return pl.pallas_call(
        back_kernel,
        out_shape=(
            small, small, sds((local, wide), BF), sds((local, wide), BF), small, small,
            sds((2 * HEADS, HW), F32),
        ),
        in_specs=[VM] * 17,
        out_specs=(VM,) * 7,
        scratch_shapes=[
            square, square, square, square, near, near, far, far, fin, fin,
            near2, near2, far2, far2,
            pltpu.VMEM((CHIPS, 2, QUARTER, HW), BF),
            pltpu.VMEM((2, CHIPS, 2, QUARTER, HW), BF),
            pltpu.VMEM((CHIPS, QUARTER, HW), F32),
            pltpu.VMEM((CHIPS, HW), F32),
            pltpu.VMEM((CHIPS, HW), F32),
            tile, tile, tile,
            pltpu.VMEM((CHIPS, 2 * HEADS, HW), F32),
            tile,
            pltpu.VMEM((LAYERS, 2 * HEADS, HW), F32),
            dma((SCATTER_COPIES,)), dma((SCATTER_COPIES,)),
            dma((CHIPS,)), dma((CHIPS,)), dma((CHIPS,)), dma((CHIPS,)),
            dma((LAYERS,)), dma((LAYERS,)), dma((2,)), dma((2,)),
        ],
        compiler_params=pltpu.CompilerParams(
            collective_id=2, has_side_effects=True, vmem_limit_bytes=23 << 20
        ),
        cost_estimate=pl.CostEstimate(flops=1 << 29, bytes_accessed=16 << 20, transcendentals=1 << 12),
        name="back",
    )(tk, tv, got, sib, o, y, dx, xt, eg, db, dc, cum, sums, b, c, x, g)


def emit_kernel(tokens, *refs):
    count = (len(refs) - 4) // 2
    total_ref, rate_ref, skip_ref = refs[count], refs[2 * count + 1], refs[2 * count + 2]
    sem = refs[-1]
    moves = [
        pltpu.make_async_copy(refs[i], refs[count + 1 + i], sem.at[i]) for i in range(count)
    ]
    for move in moves:
        move.start()
    diagonal = lax.broadcasted_iota(jnp.int32, (HEADS, HW), 0) == lax.broadcasted_iota(
        jnp.int32, (HEADS, HW), 1
    )
    for ref, first, scale in ((rate_ref, 0, tokens), (skip_ref, HEADS, tokens * HW)):
        picked = jnp.where(diagonal, total_ref[first : first + HEADS, :], 0.0)
        row = jnp.sum(picked, axis=0, keepdims=True) / scale
        ref[...] = row[:, :HEADS]
    for move in moves:
        move.wait()


def emit(arrays, total, tokens):
    count = len(arrays)
    small = jax.ShapeDtypeStruct((1, HEADS), F32)
    return pl.pallas_call(
        functools.partial(emit_kernel, tokens),
        out_shape=tuple(pltpu.HBM(a.shape, a.dtype) for a in arrays)
        + (small, small),
        in_specs=[VM] * (count + 1),
        out_specs=(HB,) * count + (VM, VM),
        scratch_shapes=[pltpu.SemaphoreType.DMA((count,))],
        compiler_params=pltpu.CompilerParams(vmem_limit_bytes=4 << 20),
        cost_estimate=pl.CostEstimate(flops=0, bytes_accessed=3 << 20, transcendentals=0),
        name="emit",
    )(*arrays, total)


def body(query, key, value, ssm_input, in_b, in_c, step, rate_log, skip, block_mask, grad_out):
    q, k, v, x, b, c, g = (
        a[0] for a in (query, key, value, ssm_input, in_b, in_c, grad_out)
    )
    local = q.shape[0]
    fixed = [pltpu.with_memory_space_constraint(a, pltpu.HBM) for a in (k, v, x, g, b, c, step[0].T, rate_log, skip)]
    keys, values, got, sib, *local_terms = front(*fixed)
    keys, values = keys.reshape(-1, HW), values.reshape(-1, HW)
    attended, dq, terms_k, terms_v = attention(block_mask[0], q, g, keys, values)
    dk, dv, layer_out, dx, db, dc, total = back(
        terms_k, terms_v, got, sib, attended, *local_terms, b, c, x, g
    )
    tokens = lax.axis_size("dp") * lax.axis_size("seq") * local
    layer_out, dx, dk, dv, db, dc, rate, gain = emit(
        (layer_out, dx, dk, dv, db, dc), total, tokens
    )
    return (
        layer_out[None],
        dq[None],
        dk[None],
        dv[None],
        dx[None],
        db[None],
        dc[None],
        rate[0],
        gain[0],
    )


def solution(mesh):
    row = P("dp", "seq", None)
    in_specs = (row,) * 7 + (P(), P(), P("dp", None, None), row)
    out_specs = (row,) * 7 + (P(), P())
    return jax.shard_map(body, mesh=mesh, in_specs=in_specs, out_specs=out_specs, check_vma=False)
```

```python
import functools

import jax
import jax.numpy as jnp
from jax import lax
from jax.experimental import pallas as pl
from jax.experimental.pallas import tpu as pltpu
from jax.sharding import PartitionSpec as P

HW = 128
HEADS = 8
BT = 128
MOST = 24
WIDE = 8
NARROW = 4
FACTOR = HW ** (-0.5)
LOG2E = 1.4426950408889634
BF = jnp.bfloat16
F32 = jnp.float32
MESH = pl.DeviceIdType.MESH
HIGH = lax.Precision.HIGHEST

VM = pl.BlockSpec(memory_space=pltpu.VMEM)
HB = pl.BlockSpec(memory_space=pltpu.HBM)
SM = pl.BlockSpec(memory_space=pltpu.SMEM)


def nn(a, b):
    return lax.dot_general(a, b, (((1,), (0,)), ((), ())), preferred_element_type=F32)


def nt(a, b):
    return lax.dot_general(a, b, (((1,), (1,)), ((), ())), preferred_element_type=F32)


def tn(a, b):
    return lax.dot_general(a, b, (((0,), (0,)), ((), ())), preferred_element_type=F32)


def cols(h):
    return pl.ds(h * HW, HW)


def attention_kernel(
    mask_ref, q_ref, g_ref, k_ref, v_ref,
    o_ref, dq_ref, tk_ref, tv_ref,
    s_buf, acc_k, acc_v, qs, gs, g_t, o_t, dq_t, picked,
):
    total_blocks = mask_ref.shape[1]
    seq_at = lax.axis_index("seq")
    per_device = q_ref.shape[0] // BT
    acc_k[...] = jnp.zeros_like(acc_k)
    acc_v[...] = jnp.zeros_like(acc_v)

    @pl.loop(0, per_device)
    def _(block):
        row = seq_at * per_device + block

        def note(j, n):
            picked[n] = j
            return n + mask_ref[row, j]

        count = lax.fori_loop(0, total_blocks, note, jnp.int32(0), unroll=8)
        for i in range(WIDE - 1):
            picked[count + i] = picked[0]
        rest = lax.rem(count, WIDE)
        wide = count // WIDE + (rest > NARROW).astype(jnp.int32)
        narrow = jnp.logical_and(rest > 0, rest <= NARROW).astype(jnp.int32)
        rows = pl.ds(pl.multiple_of(block * BT, BT), BT)
        for h in range(HEADS):
            qs[cols(h), :] = q_ref[rows, cols(h)]
            g_head = g_ref[rows, cols(h)]
            gs[cols(h), :] = g_head
            g_t[:, cols(h)] = g_head.astype(F32).T

        def starts(at, size):
            return tuple(pl.multiple_of(picked[at + i] * BT, BT) for i in range(size))

        def group_of(ref, at, size):
            return jnp.concatenate([ref[pl.ds(first, BT), :] for first in starts(at, size)], axis=0)

        def over_groups(step, carry):
            carry = lax.fori_loop(0, wide, lambda p, c: step(p * WIDE, WIDE, c), carry)
            return lax.fori_loop(0, narrow, lambda p, c: step(wide * WIDE, NARROW, c), carry)

        def flat(value):
            return value.reshape(-1, value.shape[-1])

        def score_step(at, size, top):
            s = nt(group_of(k_ref, at, size), qs[...])
            parts = [s[:BT]]
            for i in range(1, size):
                bias = jnp.where(at + i < count, 0.0, -1e30).astype(F32)
                parts.append(s[i * BT : (i + 1) * BT] + bias)
            s = jnp.concatenate(parts, axis=0)
            s_buf[pl.ds(at, size)] = s.reshape(size, BT, -1)
            return jnp.maximum(top, jnp.max(s.reshape(-1, 8, s.shape[1]), axis=0))

        top = over_groups(score_step, jnp.full((8, HEADS * BT), -3e38, F32))
        top = jnp.max(top, axis=0, keepdims=True)
        o_t[...] = jnp.zeros_like(o_t)

        def weight_step(at, size, total):
            w = jnp.exp2((flat(s_buf[pl.ds(at, size)]) - top) * (FACTOR * LOG2E))
            s_buf[pl.ds(at, size)] = w.reshape(size, BT, -1)
            o_t[...] += tn(group_of(v_ref, at, size), w.astype(BF))
            return total + jnp.sum(w.reshape(-1, 8, w.shape[1]), axis=0)

        total = over_groups(weight_step, jnp.zeros((8, HEADS * BT), F32))
        inverse = 1.0 / jnp.sum(total, axis=0, keepdims=True)
        o_t[...] = o_t[...] * inverse
        delta = jnp.sum(o_t[...] * g_t[...], axis=0, keepdims=True)
        for h in range(HEADS):
            o_ref[rows, cols(h)] = o_t[:, cols(h)].T
        dq_t[...] = jnp.zeros_like(dq_t)

        def gradient_step(at, size, carry):
            probs = flat(s_buf[pl.ds(at, size)]) * inverse
            dprobs = nt(group_of(v_ref, at, size), gs[...])
            ds = (probs * (dprobs - delta)).astype(BF)
            dq_t[...] += tn(group_of(k_ref, at, size), ds)
            dk = nn(ds, qs[...])
            dv = nn(probs.astype(BF), gs[...])
            for i, first in enumerate(starts(at, size)):
                here = pl.ds(first, BT)
                acc_k[here, :] += dk[i * BT : (i + 1) * BT]
                acc_v[here, :] += dv[i * BT : (i + 1) * BT]
            return carry

        over_groups(gradient_step, 0)
        for h in range(HEADS):
            dq_ref[rows, cols(h)] = (dq_t[:, cols(h)] * FACTOR).T.astype(BF)

    @pl.loop(0, total_blocks, unroll=4)
    def _(j):
        here = pl.ds(pl.multiple_of(j * BT, BT), BT)
        chip = j // 4
        at = (
            lax.rem(j // 2, 2), chip // SIDE, lax.rem(chip, SIDE),
            pl.ds(pl.multiple_of(lax.rem(j, 2) * BT, BT), BT),
        )
        tk_ref[at] = (acc_k[here, :] * FACTOR).astype(BF)
        tv_ref[at] = acc_v[here, :].astype(BF)


def attention(mask, q, g, keys, values):
    local, wide = q.shape
    total = keys.shape[0]
    width = HEADS * BT
    return pl.pallas_call(
        attention_kernel,
        out_shape=(
            jax.ShapeDtypeStruct((local, wide), F32),
            jax.ShapeDtypeStruct((local, wide), BF),
            jax.ShapeDtypeStruct((2, SIDE, SIDE, local, HW), BF),
            jax.ShapeDtypeStruct((2, SIDE, SIDE, local, HW), BF),
        ),
        in_specs=[SM, VM, VM, VM, VM],
        out_specs=(VM, VM, VM, VM),
        scratch_shapes=[
            pltpu.VMEM((MOST, BT, width), F32),
            pltpu.VMEM((total, HW), F32),
            pltpu.VMEM((total, HW), F32),
            pltpu.VMEM((width, HW), BF),
            pltpu.VMEM((width, HW), BF),
            pltpu.VMEM((HW, width), F32),
            pltpu.VMEM((HW, width), F32),
            pltpu.VMEM((HW, width), F32),
            pltpu.SMEM((total // BT + 8,), jnp.int32),
        ],
        compiler_params=pltpu.CompilerParams(vmem_limit_bytes=38 << 20),
        cost_estimate=pl.CostEstimate(
            flops=12 * 24 * 1024 * 128 * 128 * 2, bytes_accessed=12 << 20, transcendentals=1 << 22
        ),
        name="attention",
    )(mask, q, g, keys, values)


SIDE = 4
CHIPS = SIDE * SIDE
PEERS = 2 * CHIPS
LAYERS = 8
QUARTER = 32
LOG_ROWS = 16
PACKED = 2 * QUARTER + LOG_ROWS


def place():
    me = lax.axis_index("seq")
    core = lax.rem(me, 2)
    chip = me // 2
    return me, chip // SIDE, lax.rem(chip, SIDE), core


def ring(a, step):
    return lax.rem(a + step + SIDE, SIDE)


def greet(chip, core, also_dp, between=None):
    barrier = pltpu.get_barrier_semaphore()

    @pl.loop(1, CHIPS)
    def _(r):
        to = lax.rem(chip + r, CHIPS) * 2 + core
        pl.semaphore_signal(barrier, inc=1, device_id={"seq": to}, device_id_type=MESH)

    pl.semaphore_signal(
        barrier, inc=1, device_id={"seq": chip * 2 + 1 - core}, device_id_type=MESH
    )
    waits = CHIPS
    if also_dp:
        layer = lax.axis_index("dp")

        @pl.loop(1, LAYERS)
        def _(r):
            to = lax.rem(layer + r, LAYERS)
            pl.semaphore_signal(barrier, inc=1, device_id={"dp": to}, device_id_type=MESH)

        waits += LAYERS - 1
    if between is not None:
        between()
    pl.semaphore_wait(barrier, waits)


def to_peers(chip, core, src, dst, send_sem, recv_sem):
    def copy(r):
        to = lax.rem(chip + r, CHIPS)
        return pltpu.make_async_remote_copy(
            src_ref=src(to), dst_ref=dst, send_sem=send_sem.at[r], recv_sem=recv_sem.at[r],
            device_id={"seq": to * 2 + core}, device_id_type=MESH,
        )

    def start():
        @pl.loop(1, CHIPS)
        def _(r):
            copy(r).start()

    def wait():
        @pl.loop(1, CHIPS)
        def _(r):
            copy(r).wait()

    return start, wait


def to_sibling(chip, core, src, dst, sems):
    return pltpu.make_async_remote_copy(
        src_ref=src, dst_ref=dst, send_sem=sems.at[0], recv_sem=sems.at[1],
        device_id={"seq": chip * 2 + 1 - core}, device_id_type=MESH,
    )


class Copies:
    def __init__(self, send_sem, recv_sem):
        self.send_sem, self.recv_sem, self.made = send_sem, recv_sem, []

    def start(self, src, dst, device):
        at = len(self.made)
        copy = pltpu.make_async_remote_copy(
            src_ref=src, dst_ref=dst, send_sem=self.send_sem.at[at], recv_sem=self.recv_sem.at[at],
            device_id={"seq": device}, device_id_type=MESH,
        )
        copy.start()
        self.made.append(copy)
        return copy

    def finish(self):
        for copy in self.made:
            copy.wait_send()


LOW, UP = pl.ds(0, BT), pl.ds(BT, BT)
GATHER_COPIES = 2 * (22 + 16)


class GatherPart:
    def __init__(self, copies, own, out, first, second, at, core):
        self.c, self.own, self.out = copies, own, out
        self.f, self.s, self.at, self.core = first, second, at, core

    def dev(self, df, ds, other=False):
        core = 1 - self.core if other else self.core
        return self.at(ring(self.f, df), ring(self.s, ds)) * 2 + core

    def block(self, df, ds):
        return self.out.at[self.dev(df, ds)]

    def sibling(self, df, ds, src=None):
        here = self.block(df, ds)
        return self.c.start(here if src is None else src, here, self.dev(0, 0, True))

    def begin(self):
        mine = self.block(0, 0)
        self.a_up = self.c.start(self.own, mine, self.dev(1, 0))
        self.a_down = self.c.start(self.own, mine, self.dev(-1, 0))
        self.col = {0: self.column(0, self.own)}
        self.sib = [self.sibling(0, 0, self.own)]

    def column(self, df, src=None):
        here = self.block(df, 0)
        src = here if src is None else src
        return self.c.start(src, here, self.dev(0, 1)), self.c.start(src, here, self.dev(0, -1))

    def near(self):
        self.a_up.wait_recv()
        here = self.block(-1, 0)
        self.b_up = self.c.start(here.at[LOW], here.at[LOW], self.dev(1, 0))
        self.col[-1] = self.column(-1)
        self.sib.append(self.sibling(-1, 0))
        self.a_down.wait_recv()
        here = self.block(1, 0)
        self.b_down = self.c.start(here.at[UP], here.at[UP], self.dev(-1, 0))
        self.col[1] = self.column(1)
        self.sib.append(self.sibling(1, 0))
        self.last = []

    def pass_on(self, df):
        up, down = self.col[df]
        up.wait_recv()
        here = self.block(df, -1)
        one = self.c.start(here.at[LOW], here.at[LOW], self.dev(0, 1))
        self.sib.append(self.sibling(df, -1))
        down.wait_recv()
        here = self.block(df, 1)
        two = self.c.start(here.at[UP], here.at[UP], self.dev(0, -1))
        self.sib.append(self.sibling(df, 1))
        self.last.append((df, one, two))

    def far(self):
        self.b_up.wait_recv()
        self.b_down.wait_recv()
        self.col[2] = self.column(2)
        self.sib.append(self.sibling(2, 0))

    def end(self, i):
        df, one, two = self.last[i]
        one.wait_recv()
        two.wait_recv()
        self.sib.append(self.sibling(df, 2))


def ssm_prepare(x_ref, step_ref, rate_ref, b_ref, c_ref, cum_ref, dl, bt_ref, ct_ref, sums):
    lanes = lax.broadcasted_iota(jnp.int32, (BT, BT), 1)
    subs = lax.broadcasted_iota(jnp.int32, (BT, BT), 0)
    upper = (subs <= lanes).astype(F32)
    dl[...] = jnp.zeros_like(dl)
    for h in range(HEADS):
        rate = jnp.exp(jnp.full((1, 1), rate_ref[h], F32))
        dl[h : h + 1, :] = -step_ref[h : h + 1, :] * rate
    run_t = []
    for i in range(2):
        run_t.append(
            lax.dot_general(
                dl[:, i * BT : (i + 1) * BT], upper, (((1,), (0,)), ((), ())),
                precision=HIGH, preferred_element_type=F32,
            )
        )
    run0, run1 = run_t[0].T, run_t[1].T
    end0, end1 = run0[BT - 1 : BT, :], run1[BT - 1 : BT, :]
    cum_ref[0] = jnp.concatenate([run0, run1 + end0], axis=0)
    cum_ref[1] = jnp.concatenate([end0 - run0 + end1, end1 - run1], axis=0)
    bt_ref[...] = b_ref[...].T
    ct_ref[...] = c_ref[...].T
    for total in sums:
        total[...] = jnp.zeros_like(total)
    b0, b1 = b_ref[0:BT, :], b_ref[BT : 2 * BT, :]
    c0, c1 = c_ref[0:BT, :], c_ref[BT : 2 * BT, :]
    return run0, run1, run_t[0], run_t[1], end0, end1, nt(c0, b0), nt(c1, b1), nt(c1, b0)


def split3(value):
    rows = lax.broadcasted_iota(jnp.int32, (LOG_ROWS, HW), 0)
    hi = value.astype(BF).astype(F32)
    mid = (value - hi).astype(BF).astype(F32)
    low = value - hi - mid
    out = jnp.where(rows == 0, hi, jnp.where(rows == 1, mid, jnp.where(rows == 2, low, 0.0)))
    return out.astype(BF)


def ssm_head(
    h, ready, x_ref, g_ref, skip_ref, cum_ref, bt_ref, ct_ref, sums,
    y_ref, dx_ref, xt_ref, eg_ref, send_ref, sums_ref,
):
    run0, run1, run0_t, run1_t, end0, end1, cb00, cb11, cb10 = ready
    sum00, sum11, sum10 = sums
    lanes = lax.broadcasted_iota(jnp.int32, (BT, BT), 1)
    subs = lax.broadcasted_iota(jnp.int32, (BT, BT), 0)
    lower = subs >= lanes
    x0, x1 = x_ref[0:BT, cols(h)], x_ref[BT : 2 * BT, cols(h)]
    g0, g1 = g_ref[0:BT, cols(h)], g_ref[BT : 2 * BT, cols(h)]
    gain = skip_ref[h]
    col0, col1 = run0[:, h : h + 1], run1[:, h : h + 1]
    row0, row1 = run0_t[h : h + 1, :], run1_t[h : h + 1, :]
    last0, last1 = end0[:, h : h + 1], end1[:, h : h + 1]

    def part(spread, cb, xs, gs, total, diagonal):
        if diagonal:
            decay = jnp.where(lower, jnp.exp(jnp.where(lower, spread, 0.0)), 0.0)
        else:
            decay = jnp.exp(spread)
        mixed = decay * cb
        outer = nt(gs, xs)
        total[...] += decay * outer
        terms = spread * (mixed * outer)
        mixed = mixed.astype(BF)
        return nn(mixed, xs), tn(mixed, gs), jnp.sum(terms, axis=0, keepdims=True)

    y00, dx00, r00 = part(col0 - row0, cb00, x0, g0, sum00, True)
    y11, dx11, r11 = part(col1 - row1, cb11, x1, g1, sum11, True)
    y10, dx10, r10 = part(col1 + (last0 - row0), cb10, x0, g1, sum10, False)
    xf0, xf1, gf0, gf1 = x0.astype(F32), x1.astype(F32), g0.astype(F32), g1.astype(F32)
    sums_ref[h : h + 1, :] = r00 + r11 + r10
    sums_ref[HEADS + h : HEADS + h + 1, :] = jnp.sum(xf0 * gf0 + xf1 * gf1, axis=0, keepdims=True)
    y_ref[0:BT, cols(h)] = y00 + gain * xf0
    y_ref[BT : 2 * BT, cols(h)] = y11 + y10 + gain * xf1
    dx_ref[0:BT, cols(h)] = dx00 + dx10 + gain * gf0
    dx_ref[BT : 2 * BT, cols(h)] = dx11 + gain * gf1
    start = jnp.exp(cum_ref[0][:, h : h + 1])
    tail = jnp.exp(cum_ref[1][:, h : h + 1])

    def state(turned, scaled, keep_ref):
        high = scaled.astype(BF)
        keep_ref[:, cols(h)] = high
        low = (scaled - high.astype(F32)).astype(BF)
        return (nn(turned, high) + nn(turned, low)).astype(BF)

    end_state = state(bt_ref[...], tail * jnp.concatenate([xf0, xf1], axis=0), xt_ref)
    start_grad = state(ct_ref[...], start * jnp.concatenate([gf0, gf1], axis=0), eg_ref)
    logs = split3(last0 + last1)
    for i in range(4):
        at = slice(i * QUARTER, (i + 1) * QUARTER)
        to = send_ref.at[(h * 4 + i) % 2, (h * 4 + i) // 2]
        to[0:QUARTER, :] = end_state[at]
        to[QUARTER : 2 * QUARTER, :] = start_grad[at]
        to[2 * QUARTER : PACKED, :] = logs


def ssm_end(b_ref, c_ref, sums, db_ref, dc_ref):
    s00, s11, s10 = (total[...].astype(BF) for total in sums)
    b0, b1 = b_ref[0:BT, :], b_ref[BT : 2 * BT, :]
    c0, c1 = c_ref[0:BT, :], c_ref[BT : 2 * BT, :]
    dc_ref[0:BT, :] = nn(s00, b0)
    dc_ref[BT : 2 * BT, :] = nn(s11, b1) + nn(s10, b0)
    db_ref[0:BT, :] = tn(s00, c0) + tn(s10, c1)
    db_ref[BT : 2 * BT, :] = tn(s11, c1)


def combine(core, send_ref, sib_ref, comb_ref):
    first = (core == 0).astype(F32)
    second = 1.0 - first
    for h in range(HEADS):
        at = pl.ds(2 * h, 2)
        mine, other = send_ref[core, at].astype(F32), sib_ref[core, at].astype(F32)
        log_mine = jnp.sum(mine[0, 2 * QUARTER :], axis=0, keepdims=True)
        log_other = jnp.sum(other[0, 2 * QUARTER :], axis=0, keepdims=True)
        by_mine, by_other = jnp.exp(log_mine), jnp.exp(log_other)
        ends = slice(0, QUARTER)
        comb_ref[at, ends, :] = (
            (first * by_other + second) * mine[:, ends] + (first + second * by_mine) * other[:, ends]
        ).astype(BF)
        grads = slice(QUARTER, 2 * QUARTER)
        comb_ref[at, grads, :] = (
            (first + second * by_other) * mine[:, grads] + (first * by_mine + second) * other[:, grads]
        ).astype(BF)
        logs = split3(log_mine + log_other)
        for i in range(2):
            comb_ref[2 * h + i, 2 * QUARTER : PACKED, :] = logs


def front_kernel(
    k_hbm, v_hbm, x_hbm, g_hbm, b_hbm, c_hbm, step_hbm, rate_hbm, skip_hbm,
    ko_ref, vo_ref, got_ref, sib_ref, y_ref, dx_ref, xt_ref, eg_ref, db_ref, dc_ref, cum_ref, sums_ref,
    x_ref, g_ref, b_ref, c_ref, step_ref, rate_ref, skip_ref, send_ref, comb_ref, dl, bt_ref, ct_ref, sum00, sum11, sum10,
    send_sem, recv_sem, own_sem, s1, r1, pair_sem,
):
    me, x, y, core = place()
    sources = (x_hbm, g_hbm, b_hbm, c_hbm, step_hbm, rate_hbm, skip_hbm)
    targets = (x_ref, g_ref, b_ref, c_ref, step_ref, rate_ref, skip_ref)
    loads = [
        pltpu.make_async_copy(src, dst, own_sem.at[i])
        for i, (src, dst) in enumerate(zip(sources, targets))
    ]
    for copy in loads:
        copy.start()
    chip = me // 2
    greet(chip, core, False)
    copies = Copies(send_sem, recv_sem)
    parts = (
        GatherPart(copies, k_hbm, ko_ref, x, y, lambda f, s: f * SIDE + s, core),
        GatherPart(copies, v_hbm, vo_ref, y, x, lambda f, s: s * SIDE + f, core),
    )
    for part in parts:
        part.begin()
    own = [
        pltpu.make_async_copy(k_hbm, ko_ref.at[me], own_sem.at[7]),
        pltpu.make_async_copy(v_hbm, vo_ref.at[me], own_sem.at[8]),
    ]
    for copy in own:
        copy.start()
    for copy in loads:
        copy.wait()

    def all_parts(name, *args):
        return lambda: [getattr(part, name)(*args) for part in parts]

    stages = {
        1: all_parts("near"), 3: all_parts("pass_on", 0), 5: all_parts("far"),
    }
    sums = (sum00, sum11, sum10)
    ready = ssm_prepare(x_ref, step_ref, rate_ref, b_ref, c_ref, cum_ref, dl, bt_ref, ct_ref, sums)
    for h in range(HEADS):
        ssm_head(
            h, ready, x_ref, g_ref, skip_ref, cum_ref, bt_ref, ct_ref, sums,
            y_ref, dx_ref, xt_ref, eg_ref, send_ref, sums_ref,
        )
        if h in stages:
            stages[h]()
    pair = to_sibling(chip, core, send_ref, sib_ref, pair_sem)
    pair.start()
    for part in parts:
        part.pass_on(-1)
    ssm_end(b_ref, c_ref, sums, db_ref, dc_ref)
    pair.wait()
    combine(core, send_ref, sib_ref, comb_ref)
    start, wait = to_peers(chip, core, lambda to: comb_ref.at[to], got_ref.at[chip], s1, r1)
    start()
    got_ref[chip] = comb_ref[chip]
    for df in (1, 2):
        for part in parts:
            part.pass_on(df)
    for i in range(4):
        for part in parts:
            part.end(i)
    for copy in own:
        copy.wait()
    for part in parts:
        for copy in part.sib:
            copy.wait_recv()
    copies.finish()
    wait()


def front(k, v, x, g, b, c, step_t, rate_log, skip):
    local, wide = x.shape
    sds = jax.ShapeDtypeStruct
    full = sds((PEERS, local, HW), BF)
    dma = pltpu.SemaphoreType.DMA
    return pl.pallas_call(
        front_kernel,
        out_shape=(
            full,
            full,
            sds((CHIPS, PACKED, HW), BF),
            sds((2, CHIPS, PACKED, HW), BF),
            sds((local, wide), F32),
            sds((local, wide), F32),
            sds((local, wide), BF),
            sds((local, wide), BF),
            sds((local, HW), F32),
            sds((local, HW), F32),
            sds((2, local, HW), F32),
            sds((2 * HEADS, HW), F32),
        ),
        in_specs=[HB] * 9,
        out_specs=(VM,) * 12,
        scratch_shapes=[
            pltpu.VMEM((local, wide), BF),
            pltpu.VMEM((local, wide), BF),
            pltpu.VMEM((local, HW), BF),
            pltpu.VMEM((local, HW), BF),
            pltpu.VMEM((HEADS, local), F32),
            pltpu.SMEM((HEADS,), F32),
            pltpu.SMEM((HEADS,), F32),
            pltpu.VMEM((2, CHIPS, PACKED, HW), BF),
            pltpu.VMEM((CHIPS, PACKED, HW), BF),
            pltpu.VMEM((HW, local), F32),
            pltpu.VMEM((HW, local), BF),
            pltpu.VMEM((HW, local), BF),
            pltpu.VMEM((BT, BT), F32),
            pltpu.VMEM((BT, BT), F32),
            pltpu.VMEM((BT, BT), F32),
            dma((GATHER_COPIES,)),
            dma((GATHER_COPIES,)),
            dma((9,)),
            dma((CHIPS,)),
            dma((CHIPS,)),
            dma((2,)),
        ],
        compiler_params=pltpu.CompilerParams(
            collective_id=1, has_side_effects=True, vmem_limit_bytes=14 << 20
        ),
        cost_estimate=pl.CostEstimate(flops=1 << 30, bytes_accessed=16 << 20, transcendentals=1 << 19),
        name="front",
    )(k, v, x, g, b, c, step_t, rate_log, skip)


SCATTER_COPIES = 2 * 16


class ScatterPart:
    def __init__(self, copies, terms, sib, acc, near, far, fin, near2, far2, out, first, second, x_first, core, dev):
        self.c, self.terms, self.sib, self.acc = copies, terms, sib, acc
        self.near, self.far, self.fin, self.near2, self.far2, self.out = near, far, fin, near2, far2, out
        self.f, self.s, self.x_first, self.core, self.dev = first, second, x_first, core, dev

    def chunk(self, ref, ds, core=None):
        s = ring(self.s, ds)
        ref = ref if core is None else ref.at[core]
        return ref.at[:, s] if self.x_first else ref.at[s]

    def begin(self):
        self.sibs = {}
        for ds in (2, 1, -1, 0):
            self.sibs[ds] = self.c.start(
                self.chunk(self.terms, ds, 1 - self.core), self.chunk(self.sib, ds), self.dev(0, 0, True)
            )

    def own(self, ds, rows):
        mine = self.chunk(self.terms, ds, self.core)[:, rows, :].astype(F32)
        return mine + self.chunk(self.sib, ds)[:, rows, :].astype(F32)

    def put(self, ds, rows, extra=None):
        value = self.own(ds, rows)
        if extra is not None:
            value = value + extra.astype(F32)
        self.chunk(self.acc, ds)[:, rows, :] = value.astype(BF)

    def one(self):
        self.sibs[2].wait_recv()
        for rows in (LOW, UP):
            self.put(2, rows)
        here = self.chunk(self.acc, 2)
        self.far_up = self.c.start(here.at[:, LOW], self.far.at[0], self.dev(0, 1))
        self.far_down = self.c.start(here.at[:, UP], self.far.at[1], self.dev(0, -1))

    def two(self):
        self.sibs[1].wait_recv()
        self.put(1, UP)
        self.up_a = self.c.start(
            self.chunk(self.acc, 1).at[:, UP], self.near.at[0, :, UP], self.dev(0, 1)
        )
        self.sibs[-1].wait_recv()
        self.put(-1, LOW)
        self.down_a = self.c.start(
            self.chunk(self.acc, -1).at[:, LOW], self.near.at[1, :, LOW], self.dev(0, -1)
        )

    def three(self):
        self.far_up.wait_recv()
        self.put(1, LOW, self.far[0])
        self.up_b = self.c.start(
            self.chunk(self.acc, 1).at[:, LOW], self.near.at[0, :, LOW], self.dev(0, 1)
        )
        self.far_down.wait_recv()
        self.put(-1, UP, self.far[1])
        self.down_b = self.c.start(
            self.chunk(self.acc, -1).at[:, UP], self.near.at[1, :, UP], self.dev(0, -1)
        )

    def four(self):
        self.sibs[0].wait_recv()
        for copy in (self.up_a, self.down_a, self.up_b, self.down_b):
            copy.wait_recv()
        for rows in (LOW, UP):
            total = self.own(0, rows) + self.near[0, :, rows, :].astype(F32) + self.near[1, :, rows, :].astype(F32)
            self.fin[:, rows, :] = total.astype(BF)
        here = self.fin.at[ring(self.f, 2)]
        self.far_up = self.c.start(here.at[LOW], self.far2.at[0], self.dev(1, 0))
        self.far_down = self.c.start(here.at[UP], self.far2.at[1], self.dev(-1, 0))
        self.up_a = self.c.start(
            self.fin.at[ring(self.f, 1)].at[UP], self.near2.at[0, UP], self.dev(1, 0)
        )
        self.down_a = self.c.start(
            self.fin.at[ring(self.f, -1)].at[LOW], self.near2.at[1, LOW], self.dev(-1, 0)
        )

    def five(self):
        self.far_up.wait_recv()
        here = self.fin.at[ring(self.f, 1)]
        here[LOW, :] = (here[LOW, :].astype(F32) + self.far2[0].astype(F32)).astype(BF)
        self.up_b = self.c.start(here.at[LOW], self.near2.at[0, LOW], self.dev(1, 0))
        self.far_down.wait_recv()
        here = self.fin.at[ring(self.f, -1)]
        here[UP, :] = (here[UP, :].astype(F32) + self.far2[1].astype(F32)).astype(BF)
        self.down_b = self.c.start(here.at[UP], self.near2.at[1, UP], self.dev(-1, 0))

    def six(self):
        for copy in (self.up_a, self.down_a, self.up_b, self.down_b):
            copy.wait_recv()
        mine = self.fin.at[self.f][...].astype(F32)
        self.out[...] = (mine + self.near2[0].astype(F32) + self.near2[1].astype(F32)).astype(BF)


def scan_states(me, got_ref, back_ref, kept, decays, logs, sums_ref):
    log_sum = jnp.sum(got_ref[:, 2 * QUARTER : PACKED, :].astype(F32), axis=1)
    logs[...] = log_sum
    decays[...] = jnp.exp(log_sum)

    def forward(d, state):
        kept[d] = state
        back_ref[d, 0] = state.astype(BF)
        return decays[pl.ds(d, 1), :] * state + got_ref[d, 0:QUARTER, :].astype(F32)

    def backward(k, carry):
        grad, rate = carry
        d = CHIPS - 1 - k
        back_ref[d, 1] = grad.astype(BF)
        decay = decays[pl.ds(d, 1), :]
        rate = rate + (logs[pl.ds(d, 1), :] * decay) * (kept[d] * grad)
        return decay * grad + got_ref[d, QUARTER : 2 * QUARTER, :].astype(F32), rate

    zero = jnp.zeros((QUARTER, HW), F32)
    lax.fori_loop(0, CHIPS, forward, zero)
    _, rate = lax.fori_loop(0, CHIPS, backward, (zero, zero))
    rate = jnp.sum(rate, axis=0, keepdims=True)
    rows = lax.broadcasted_iota(jnp.int32, (2 * HEADS, HW), 0)
    sums_ref[...] += jnp.where(rows == me // 4, rate, 0.0)


def ssm_finish(
    core, st_ref, sib_ref, o_ref, y_ref, dx_ref, xt_ref, eg_ref, db_ref, dc_ref, cum_ref,
    b_ref, c_ref, x_ref, g_ref, out_ref, dxo_ref, dbo_ref, dco_ref, sums_ref,
):
    dc = dc_ref[...]
    db = db_ref[...]
    first = (core == 0).astype(F32)
    second = 1.0 - first
    for h in range(HEADS):
        owners = [((h * 4 + i) % 2, (h * 4 + i) // 2) for i in range(4)]

        def joined(pick):
            return jnp.concatenate([pick(*at) for at in owners], axis=0).astype(F32)

        chip_state = joined(lambda a, b: st_ref[a, b, 0])
        chip_grad = joined(lambda a, b: st_ref[a, b, 1])
        sib_state = joined(lambda a, b: sib_ref[a, b, 0:QUARTER, :])
        sib_grad = joined(lambda a, b: sib_ref[a, b, QUARTER : 2 * QUARTER, :])
        sib_logs = sib_ref[0, 2 * h, 2 * QUARTER : PACKED, :].astype(F32)
        sib_decay = jnp.exp(jnp.sum(sib_logs, axis=0, keepdims=True))
        s_in = (first * chip_state + second * (sib_decay * chip_state + sib_state)).astype(BF)
        g_out = (first * (sib_decay * chip_grad + sib_grad) + second * chip_grad).astype(BF)
        across = jnp.sum(
            first * (sib_grad * chip_state) + second * (chip_grad * sib_state), axis=0, keepdims=True
        )
        log_start, log_tail = cum_ref[0][:, h : h + 1], cum_ref[1][:, h : h + 1]
        y_in = jnp.exp(log_start) * nn(c_ref[...], s_in)
        dx_in = jnp.exp(log_tail) * nn(b_ref[...], g_out)
        out_ref[:, cols(h)] = (o_ref[:, cols(h)] + (y_ref[:, cols(h)] + y_in)).astype(BF)
        dxo_ref[:, cols(h)] = (dx_ref[:, cols(h)] + dx_in).astype(BF)
        dc = dc + nt(eg_ref[:, cols(h)], s_in)
        db = db + nt(xt_ref[:, cols(h)], g_out)
        gf, xf = g_ref[:, cols(h)].astype(F32), x_ref[:, cols(h)].astype(F32)
        terms = log_start * (gf * y_in) + log_tail * (xf * dx_in)
        whole = log_start[-1:, :]
        sums_ref[h : h + 1, :] += (
            jnp.sum(terms, axis=0, keepdims=True) + (whole * jnp.exp(whole)) * across
        )
    dco_ref[...] = dc.astype(BF)
    dbo_ref[...] = db.astype(BF)


def back_kernel(
    tk_ref, tv_ref, got_ref, sib_ref, o_ref, y_ref, dx_ref, xt_ref, eg_ref, db_ref, dc_ref, cum_ref, sums_in,
    b_ref, c_ref, x_ref, g_ref,
    dk_ref, dv_ref, out_ref, dxo_ref, dbo_ref, dco_ref, total_ref,
    sib_k, sib_v, acc_k, acc_v, near_k, near_v, far_k, far_v, fin_k, fin_v,
    near2_k, near2_v, far2_k, far2_v,
    back_ref, st_ref, kept, decays, logs, sums_ref, sib_sums, chip_sums, seq_sums, seq_total, dp_sums,
    send_sem, recv_sem, s1, r1, s2, r2, s3, r3, pair_sem, pair_sem2,
):
    me, x, y, core = place()
    layer = lax.axis_index("dp")
    chip = me // 2

    def local_scan():
        sums_ref[...] = sums_in[...]
        scan_states(me, got_ref, back_ref, kept, decays, logs, sums_ref)

    greet(chip, core, True, local_scan)
    copies = Copies(send_sem, recv_sem)

    def dev_k(df, ds, other=False):
        c = 1 - core if other else core
        return (ring(x, df) * SIDE + ring(y, ds)) * 2 + c

    def dev_v(df, ds, other=False):
        c = 1 - core if other else core
        return (ring(x, ds) * SIDE + ring(y, df)) * 2 + c

    parts = (
        ScatterPart(copies, tk_ref, sib_k, acc_k, near_k, far_k, fin_k, near2_k, far2_k, dk_ref, x, y, True, core, dev_k),
        ScatterPart(copies, tv_ref, sib_v, acc_v, near_v, far_v, fin_v, near2_v, far2_v, dv_ref, y, x, False, core, dev_v),
    )

    def stage(name):
        for part in parts:
            getattr(part, name)()

    stage("begin")
    start, wait_states = to_peers(
        chip, core, lambda to: back_ref.at[to], st_ref.at[core, chip], s1, r1
    )
    stage("one")
    start()
    st_ref[core, chip] = back_ref[chip]
    stage("two")
    stage("three")
    wait_states()
    pair = to_sibling(chip, core, st_ref.at[core], st_ref.at[core], pair_sem)
    pair.start()
    pair.wait()
    ssm_finish(
        core, st_ref, sib_ref, o_ref, y_ref, dx_ref, xt_ref, eg_ref, db_ref, dc_ref, cum_ref,
        b_ref, c_ref, x_ref, g_ref, out_ref, dxo_ref, dbo_ref, dco_ref, sums_ref,
    )
    pair = to_sibling(chip, core, sums_ref, sib_sums, pair_sem2)
    pair.start()
    stage("four")
    pair.wait()
    chip_sums[...] = sums_ref[...] + sib_sums[...]
    start, wait_sums = to_peers(chip, core, lambda to: chip_sums, seq_sums.at[chip], s2, r2)
    start()
    seq_sums[chip] = chip_sums[...]
    stage("five")
    wait_sums()
    seq_total[...] = jnp.sum(seq_sums[...], axis=0)

    def dp_copy(r):
        to = lax.rem(layer + r, LAYERS)
        return pltpu.make_async_remote_copy(
            src_ref=seq_total, dst_ref=dp_sums.at[layer], send_sem=s3.at[r], recv_sem=r3.at[r],
            device_id={"dp": to}, device_id_type=MESH,
        )

    @pl.loop(1, LAYERS)
    def _(r):
        dp_copy(r).start()

    dp_sums[layer] = seq_total[...]
    stage("six")

    @pl.loop(1, LAYERS)
    def _(r):
        dp_copy(r).wait()

    total = jnp.sum(jnp.sum(dp_sums[...], axis=0), axis=1, keepdims=True)
    total_ref[...] = jnp.broadcast_to(total, total_ref.shape)
    copies.finish()


def back(tk, tv, got, sib, o, y, dx, xt, eg, db, dc, cum, sums, b, c, x, g):
    local, wide = x.shape
    sds = jax.ShapeDtypeStruct
    small = sds((local, HW), BF)
    dma = pltpu.SemaphoreType.DMA
    square = pltpu.VMEM((SIDE, SIDE, local, HW), BF)
    near = pltpu.VMEM((2, SIDE, local, HW), BF)
    far = pltpu.VMEM((2, SIDE, BT, HW), BF)
    fin = pltpu.VMEM((SIDE, local, HW), BF)
    near2 = pltpu.VMEM((2, local, HW), BF)
    far2 = pltpu.VMEM((2, BT, HW), BF)
    tile = pltpu.VMEM((2 * HEADS, HW), F32)
    return pl.pallas_call(
        back_kernel,
        out_shape=(
            small, small, sds((local, wide), BF), sds((local, wide), BF), small, small,
            sds((2 * HEADS, HW), F32),
        ),
        in_specs=[VM] * 17,
        out_specs=(VM,) * 7,
        scratch_shapes=[
            square, square, square, square, near, near, far, far, fin, fin,
            near2, near2, far2, far2,
            pltpu.VMEM((CHIPS, 2, QUARTER, HW), BF),
            pltpu.VMEM((2, CHIPS, 2, QUARTER, HW), BF),
            pltpu.VMEM((CHIPS, QUARTER, HW), F32),
            pltpu.VMEM((CHIPS, HW), F32),
            pltpu.VMEM((CHIPS, HW), F32),
            tile, tile, tile,
            pltpu.VMEM((CHIPS, 2 * HEADS, HW), F32),
            tile,
            pltpu.VMEM((LAYERS, 2 * HEADS, HW), F32),
            dma((SCATTER_COPIES,)), dma((SCATTER_COPIES,)),
            dma((CHIPS,)), dma((CHIPS,)), dma((CHIPS,)), dma((CHIPS,)),
            dma((LAYERS,)), dma((LAYERS,)), dma((2,)), dma((2,)),
        ],
        compiler_params=pltpu.CompilerParams(
            collective_id=2, has_side_effects=True, vmem_limit_bytes=23 << 20
        ),
        cost_estimate=pl.CostEstimate(flops=1 << 29, bytes_accessed=16 << 20, transcendentals=1 << 12),
        name="back",
    )(tk, tv, got, sib, o, y, dx, xt, eg, db, dc, cum, sums, b, c, x, g)


def emit_kernel(tokens, *refs):
    count = (len(refs) - 4) // 2
    total_ref, rate_ref, skip_ref = refs[count], refs[2 * count + 1], refs[2 * count + 2]
    sem = refs[-1]
    moves = [
        pltpu.make_async_copy(refs[i], refs[count + 1 + i], sem.at[i]) for i in range(count)
    ]
    for move in moves:
        move.start()
    diagonal = lax.broadcasted_iota(jnp.int32, (HEADS, HW), 0) == lax.broadcasted_iota(
        jnp.int32, (HEADS, HW), 1
    )
    for ref, first, scale in ((rate_ref, 0, tokens), (skip_ref, HEADS, tokens * HW)):
        picked = jnp.where(diagonal, total_ref[first : first + HEADS, :], 0.0)
        row = jnp.sum(picked, axis=0, keepdims=True) / scale
        ref[...] = row[:, :HEADS]
    for move in moves:
        move.wait()


def emit(arrays, total, tokens):
    count = len(arrays)
    small = jax.ShapeDtypeStruct((1, HEADS), F32)
    return pl.pallas_call(
        functools.partial(emit_kernel, tokens),
        out_shape=tuple(pltpu.HBM(a.shape, a.dtype) for a in arrays)
        + (small, small),
        in_specs=[VM] * (count + 1),
        out_specs=(HB,) * count + (VM, VM),
        scratch_shapes=[pltpu.SemaphoreType.DMA((count,))],
        compiler_params=pltpu.CompilerParams(vmem_limit_bytes=4 << 20),
        cost_estimate=pl.CostEstimate(flops=0, bytes_accessed=3 << 20, transcendentals=0),
        name="emit",
    )(*arrays, total)


def body(query, key, value, ssm_input, in_b, in_c, step, rate_log, skip, block_mask, grad_out):
    q, k, v, x, b, c, g = (
        a[0] for a in (query, key, value, ssm_input, in_b, in_c, grad_out)
    )
    local = q.shape[0]
    fixed = [pltpu.with_memory_space_constraint(a, pltpu.HBM) for a in (k, v, x, g, b, c, step[0].T, rate_log, skip)]
    keys, values, got, sib, *local_terms = front(*fixed)
    keys, values = keys.reshape(-1, HW), values.reshape(-1, HW)
    attended, dq, terms_k, terms_v = attention(block_mask[0], q, g, keys, values)
    dk, dv, layer_out, dx, db, dc, total = back(
        terms_k, terms_v, got, sib, attended, *local_terms, b, c, x, g
    )
    tokens = lax.axis_size("dp") * lax.axis_size("seq") * local
    layer_out, dx, dk, dv, db, dc, rate, gain = emit(
        (layer_out, dx, dk, dv, db, dc), total, tokens
    )
    return (
        layer_out[None],
        dq[None],
        dk[None],
        dv[None],
        dx[None],
        db[None],
        dc[None],
        rate[0],
        gain[0],
    )


def solution(mesh):
    row = P("dp", "seq", None)
    in_specs = (row,) * 7 + (P(), P(), P("dp", None, None), row)
    out_specs = (row,) * 7 + (P(), P())
    return jax.shard_map(body, mesh=mesh, in_specs=in_specs, out_specs=out_specs, check_vma=False)
```
